256 devices in a mesh: lat: 32 (over x_lo, z, core), ch: 8 (over y, x_hi).
Axes of the slice: x: 4 (x_hi: 2, x_lo: 2; x = x_hi * 2 + x_lo), y: 4, z: 8, core: 2. Of those that a mesh axis runs over, the one named last changes fastest.
Arguments:
- spectrum: bfloat16 [512, 64, 2, 2, 256], P('lat', 'ch'), may hold values from -0.01953125 to 0.01953125
- legendre: bfloat16 [640, 256, 512], P('lat'), as said below
- block_slots: int32 [32], replicated, may hold values from 0 to 31, each once
- kernel_values: bfloat16 [3, 640, 6, 9], P(None, 'lat'), may hold values from -2 to 2
- near_rows: int32 [640, 6], P('lat'), may hold values from 0 to 639, as said below
- mix_weights: bfloat16 [3, 64, 64], replicated, may hold values from -0.4375 to 0.4375
Outputs:
- convolved: bfloat16 [64, 640, 1440], P('ch', 'lat')
The draws below stay inside these ranges and needn't reach their ends.
Inputs may be any that keep to these rules, and one draw needn't show every extreme that they name: legendre[r, k, m] is zero where m + 2 * k + p >= 512, with p = 0 for r < 320 and p = 1 otherwise. near_rows[r, q] lies within 2 rows of r; slot 0 holds max(r - 2, 0) and slot 1 holds min(r + 2, 639). `block_slots`: each order block appears once.
All inputs are finite; a program needn't handle non-finite values.
Results may differ from the reference program's by a relative error of at most 0.005.
Values may be sent and summed in bfloat16 or wider, within the bound.
No kernel may reach another device: no remote copies, remote signals or barrier semaphores. Data moves between devices by JAX's collectives and lax.ppermute only.
A program may use at most 320 MiB of HBM per device.

```python
import math
import jax
import jax.numpy as jnp
from jax import lax

NLAT = 640
NLON = 1440
LMAX = 512
C = 64
ORDER_BLOCK = 16
KER = 3
SLOTS = 6
REACH = 2
LON_REACH = 4
TAPS = 9
HALF_DEG = 256
BLOCKS = 32


def draw_legendre(key, part):
    row_ids = jnp.arange(NLAT, dtype=jnp.int32)[:, None, None]
    step_ids = jnp.arange(HALF_DEG, dtype=jnp.int32)[None, :, None]
    orders = jnp.arange(LMAX, dtype=jnp.int32)[None, None, :]
    parity = (row_ids >= NLAT // 2).astype(jnp.int32)
    keep_mask = orders + 2 * step_ids + parity < LMAX
    values = jax.random.normal(key, (NLAT, HALF_DEG, LMAX), jnp.float32)
    return jnp.where(keep_mask, values, 0.0).astype(jnp.bfloat16)


def draw_near_rows(key, part):
    base_rows = jnp.arange(NLAT, dtype=jnp.int32)[:, None]
    offsets = jax.random.randint(key, (NLAT, SLOTS), -REACH, REACH + 1, dtype=jnp.int32)
    offsets = offsets.at[:, 0].set(-REACH).at[:, 1].set(REACH)
    return jnp.clip(base_rows + offsets, 0, NLAT - 1).astype(jnp.int32)


def shard_levels(own_key, dims, pieces, least, high):
    level, own = 1.0, jax.random.fold_in(own_key, 6)
    for position, shards_of in pieces:
        heights = jnp.exp(jax.random.uniform(jax.random.fold_in(own, position), (shards_of,), jnp.float32, least / len(pieces), high / len(pieces)))
        level = level * jnp.repeat(heights, dims[position] // shards_of).reshape([-1 if axis == position else 1 for axis in range(len(dims))])
    return level


def gaussian(key, dims, deviation, reach, cuts=(), held_as=jnp.bfloat16):
    array = deviation * jax.random.normal(key, dims, jnp.float32)
    if cuts:
        array = array * shard_levels(key, dims, cuts, -0.22, 0.18)
    return jnp.clip(array, -reach, reach).astype(held_as)


def setup_inputs(seed: int = 0) -> dict:
    streams_of = jax.random.split(jax.random.key(seed), 7)
    spectrum = gaussian(streams_of[0], (LMAX, C, 2, 2, HALF_DEG), 0.0014, 0.01953125, ((0, 32), (1, 8)))
    legendre = draw_legendre(jax.random.fold_in(streams_of[6], 71), 0)
    block_slots = jax.random.permutation(streams_of[2], BLOCKS).astype(jnp.int32)
    kernel_values = gaussian(streams_of[3], (KER, NLAT, SLOTS, TAPS), 0.136, 2.0, ((1, 32),))
    near_rows = draw_near_rows(jax.random.fold_in(streams_of[6], 71), 0)
    mix_weights = gaussian(streams_of[5], (KER, C, C), (KER * C) ** -0.5, 0.4375)
    return {"spectrum": spectrum, "legendre": legendre, "block_slots": block_slots, "kernel_values": kernel_values, "near_rows": near_rows, "mix_weights": mix_weights}


def fourier_table():
    orders = jnp.arange(LMAX, dtype=jnp.int32)
    places = jnp.arange(NLON, dtype=jnp.int32)
    phases = (orders[:, None] * places[None, :]) % NLON
    angles = phases.astype(jnp.float32) * (2.0 * math.pi / NLON)
    weight = jnp.where(orders == 0, 1.0, 2.0).astype(jnp.float32)[:, None]
    return jnp.concatenate([weight * jnp.cos(angles), -weight * jnp.sin(angles)], axis=0)


def reference(spectrum, legendre, block_slots, kernel_values, near_rows, mix_weights):
    slot_rows = jnp.arange(LMAX, dtype=jnp.int32)
    order_rows = block_slots[slot_rows // ORDER_BLOCK] * ORDER_BLOCK + slot_rows % ORDER_BLOCK
    by_order = jnp.zeros_like(spectrum).at[order_rows].set(spectrum)
    half_rows = NLAT // 2
    table_f = legendre.astype(jnp.float32)
    coeff_rows = by_order.astype(jnp.float32)
    north_part = jnp.einsum("rkm,mcxk->rcxm", table_f[:half_rows], coeff_rows[:, :, 0], precision=lax.Precision.HIGHEST)
    south_part = jnp.einsum("rkm,mcxk->rcxm", table_f[half_rows:], coeff_rows[:, :, 1], precision=lax.Precision.HIGHEST)
    own_part = jnp.concatenate([north_part, south_part], axis=0)
    mirror_sign = jnp.where(jnp.arange(NLAT) < half_rows, -1.0, 1.0).astype(jnp.float32)[:, None, None, None]
    spectral = own_part + mirror_sign * own_part[::-1]
    grid_field = jnp.dot(spectral.reshape(NLAT * C, 2 * LMAX), fourier_table(), precision=lax.Precision.HIGHEST, preferred_element_type=jnp.float32)
    grid_field = grid_field.reshape(NLAT, C, NLON).astype(jnp.bfloat16)
    kernel = kernel_values.astype(jnp.float32)
    spread = jnp.zeros((KER, NLAT, C, NLON), jnp.float32)
    for slot_index in range(SLOTS):
        picked = jnp.take(grid_field, near_rows[:, slot_index], axis=0).astype(jnp.float32)
        for offset in range(TAPS):
            rolled = jnp.roll(picked, LON_REACH - offset, axis=2)
            spread = spread + kernel[:, :, slot_index, offset][:, :, None, None] * rolled[None]
    weights = mix_weights.astype(jnp.float32)
    convolved = jnp.einsum("kcd,krcx->drx", weights, spread, precision=lax.Precision.HIGHEST)
    return convolved.astype(jnp.bfloat16)
```

```python
import math

import jax
import jax.numpy as jnp
import ml_dtypes
import numpy as np
from jax import lax
from jax.experimental import pallas as pl
from jax.experimental.pallas import tpu as pltpu
from jax.sharding import PartitionSpec as P

NLAT = 640
NLON = 1440
LMAX = 512
C = 64
ORDER_BLOCK = 16
KER = 3
SLOTS = 6
REACH = 2
LON_REACH = 4
TAPS = 9
STEPS = 256
BLOCKS = 32
LATS = 32
CHS = 8
ROWS = NLAT // LATS
OWN = C // CHS
SUB = ORDER_BLOCK // CHS
HALO_ROWS = ROWS + 2 * REACH
SPREAD = 2 * REACH + 1
PICKS = LATS * SUB
LANES = 128
BF = jnp.bfloat16
F32 = jnp.float32
NT = (((1,), (1,)), ((), ()))
VMEM = pltpu.VMEM


def longitude_table():
    orders = (
        ORDER_BLOCK * np.arange(BLOCKS)[None, :, None]
        + SUB * np.arange(CHS)[:, None, None]
        + np.arange(SUB)[None, None, :]
    ).reshape(CHS, 1, PICKS, 1)
    phases = (orders * np.arange(NLON)) % NLON
    angles = phases * (2.0 * math.pi / NLON)
    weight = np.where(orders == 0, 1.0, 2.0)
    table = np.concatenate([weight * np.cos(angles), -weight * np.sin(angles)], axis=1)
    return table.reshape(CHS * LANES, NLON).astype(ml_dtypes.bfloat16)


PICK_ROWS = 4


def pick_kernel(hot_ref, leg_ref, out_ref, buf, wide, sems):
    copies = []
    for g in range(ROWS // PICK_ROWS):
        rows = pl.ds(g * PICK_ROWS, PICK_ROWS)
        copies.append(pltpu.make_async_copy(leg_ref.at[rows], buf.at[rows], sems.at[g]))
        copies[-1].start()
    for r in range(ROWS):
        if r % PICK_ROWS == 0:
            copies[r // PICK_ROWS].wait()
        picked = lax.dot_general(hot_ref[...], buf[r], NT, preferred_element_type=F32)
        for h in range(STEPS // LANES):
            wide[h, pl.ds(r, PICKS, stride=ROWS), :] = picked[:, h * LANES : (h + 1) * LANES]
    for h in range(STEPS // LANES):
        flat = wide[h].astype(BF)
        out_ref[:, :, h * LANES : (h + 1) * LANES] = flat.reshape(LATS, SUB * ROWS, LANES)


def pick(hot, legendre):
    return pl.pallas_call(
        pick_kernel,
        out_shape=jax.ShapeDtypeStruct((LATS, SUB * ROWS, STEPS), BF),
        in_specs=[pl.BlockSpec(memory_space=VMEM), pl.BlockSpec(memory_space=pl.ANY)],
        out_specs=pl.BlockSpec(memory_space=VMEM),
        scratch_shapes=[
            pltpu.VMEM((ROWS, STEPS, LMAX), BF),
            pltpu.VMEM((STEPS // LANES, PICKS * ROWS, LANES), F32),
            pltpu.SemaphoreType.DMA((ROWS // PICK_ROWS,)),
        ],
        compiler_params=pltpu.CompilerParams(vmem_limit_bytes=40 << 20),
        cost_estimate=pl.CostEstimate(flops=2 * 64 * 512 * 5120, bytes_accessed=6 << 20, transcendentals=0),
        name="pick",
    )(hot, legendre)


def order_kernel(leg_ref, spec_ref, out_ref, raw, leg, specs, full):
    half = NLAT // 2
    for i in range(LATS):
        for h in range(STEPS // LANES):
            lanes = slice(h * LANES, (h + 1) * LANES)
            raw[h, pl.ds(i * SUB * ROWS, SUB * ROWS), :] = leg_ref[i, :, lanes].astype(F32)
    for h in range(STEPS // LANES):
        lanes = slice(h * LANES, (h + 1) * LANES)
        specs[h] = spec_ref[:, :, lanes].reshape(CHS * C, LANES).astype(F32)
    for i in range(LATS):
        for t in range(SUB):
            for h in range(STEPS // LANES):
                leg[t, h, pl.ds(i * ROWS, ROWS), :] = raw[h, pl.ds((i * SUB + t) * ROWS, ROWS), :]
    rows = lax.broadcasted_iota(jnp.int32, (LANES, LANES), 0)
    cols = lax.broadcasted_iota(jnp.int32, (LANES, LANES), 1)
    turn = jnp.where(rows + cols == LANES - 1, 1.0, 0.0).astype(BF)
    stride = 4
    full[...] = jnp.zeros_like(full)
    for t in range(SUB):
        table = jnp.concatenate([leg[t, h] for h in range(STEPS // LANES)], axis=1).astype(BF)
        count = NLAT // LANES
        turned = jnp.concatenate(
            [
                jnp.dot(
                    turn,
                    table[(count - 1 - n) * LANES : (count - n) * LANES],
                    preferred_element_type=F32,
                ).astype(BF)
                for n in range(count)
            ],
            axis=0,
        )
        coeffs = []
        for p in range(2):
            pieces = []
            for x in range(2):
                for j in range(CHS):
                    start = j * C + t * 4 * OWN + p * 2 + x
                    pieces.append(
                        jnp.concatenate(
                            [
                                specs[h, pl.ds(start, OWN, stride=stride), :]
                                for h in range(STEPS // LANES)
                            ],
                            axis=1,
                        )
                    )
            coeffs.append(jnp.concatenate(pieces, axis=0).astype(BF))

        def dot(a, b):
            return lax.dot_general(a, b, NT, preferred_element_type=F32)

        full[t, pl.ds(8, half), :] = dot(table[:half], coeffs[0]) - dot(turned[:half], coeffs[1])
        full[t, pl.ds(8 + half, half), :] = dot(table[half:], coeffs[1]) + dot(turned[half:], coeffs[0])
    for i in range(LATS):
        start = 8 - REACH + i * ROWS
        block = [full[t, pl.ds(start, HALO_ROWS), :] for t in range(SUB)]
        out_ref[i] = jnp.concatenate(block, axis=0).astype(BF)


def order_stage(leg, spec):
    return pl.pallas_call(
        order_kernel,
        out_shape=jax.ShapeDtypeStruct((LATS, SUB * HALO_ROWS, LANES), BF),
        in_specs=[pl.BlockSpec(memory_space=VMEM)] * 2,
        out_specs=pl.BlockSpec(memory_space=VMEM),
        scratch_shapes=[
            pltpu.VMEM((STEPS // LANES, LATS * SUB * ROWS, LANES), F32),
            pltpu.VMEM((SUB, STEPS // LANES, NLAT, LANES), F32),
            pltpu.VMEM((STEPS // LANES, CHS * C, LANES), F32),
            pltpu.VMEM((SUB, NLAT + 16, LANES), F32),
        ],
        compiler_params=pltpu.CompilerParams(vmem_limit_bytes=40 << 20),
        cost_estimate=pl.CostEstimate(flops=700 << 20, bytes_accessed=2 << 20, transcendentals=0),
        name="order_stage",
    )(leg, spec)


def row_kernel(slots_ref, rows_ref, coef_ref, mix_ref, out_ref, field, plain, crossed, wide):
    for i in range(LATS):
        block = slots_ref[i]
        start = pl.multiple_of(block * (SUB * HALO_ROWS), 8)
        field[pl.ds(start, SUB * HALO_ROWS), :] = rows_ref[i].astype(F32)
    low = lax.broadcasted_iota(jnp.int32, (C, LANES), 1) < PICKS
    for r in range(HALO_ROWS):
        one = field[pl.ds(r, PICKS, stride=HALO_ROWS), :]
        both = jnp.concatenate([one, one], axis=0).T
        plain[r] = jnp.where(low, both[:C], both[C:])
        crossed[r] = jnp.where(low, both[C:], both[:C])
    for r in range(ROWS):
        tops, rests = [], []
        for b in range(KER):
            total = None
            for d in range(SPREAD):
                row = (r * KER + b) * SPREAD + d
                term = coef_ref[0, row : row + 1, :] * plain[r + d] + coef_ref[1, row : row + 1, :] * crossed[r + d]
                total = term if total is None else total + term
            top = total.astype(BF)
            tops.append(top)
            rests.append((total - top.astype(F32)).astype(BF))
        both = jnp.concatenate(tops + rests, axis=0)
        mixed = jnp.dot(mix_ref[...], both, preferred_element_type=F32)
        wide[pl.ds(r, C, stride=ROWS), :] = mixed
    out_ref[...] = wide[...].astype(BF).reshape(CHS, OWN * ROWS, LANES)


def row_stage(block_slots, rows, coefs, mix):
    return pl.pallas_call(
        row_kernel,
        out_shape=jax.ShapeDtypeStruct((CHS, OWN * ROWS, LANES), BF),
        in_specs=[pl.BlockSpec(memory_space=pltpu.SMEM)] + [pl.BlockSpec(memory_space=VMEM)] * 3,
        out_specs=pl.BlockSpec(memory_space=VMEM),
        scratch_shapes=[
            pltpu.VMEM((BLOCKS * SUB * HALO_ROWS, LANES), F32),
            pltpu.VMEM((HALO_ROWS, C, LANES), F32),
            pltpu.VMEM((HALO_ROWS, C, LANES), F32),
            pltpu.VMEM((C * ROWS, LANES), F32),
        ],
        compiler_params=pltpu.CompilerParams(vmem_limit_bytes=40 << 20),
        cost_estimate=pl.CostEstimate(flops=200 << 20, bytes_accessed=2 << 20, transcendentals=0),
        name="row_stage",
    )(block_slots, rows, coefs, mix)


def longitude_kernel(rows_ref, table_ref, out_ref, wide):
    lhs = jnp.concatenate([rows_ref[j] for j in range(CHS)], axis=1)
    wide[...] = jnp.dot(lhs, table_ref[...], preferred_element_type=F32)
    for o in range(OWN):
        out_ref[o] = wide[pl.ds(o * ROWS, ROWS), :].astype(BF)


def longitude_stage(rows, table):
    return pl.pallas_call(
        longitude_kernel,
        out_shape=jax.ShapeDtypeStruct((OWN, ROWS, NLON), BF),
        in_specs=[pl.BlockSpec(memory_space=VMEM)] * 2,
        out_specs=pl.BlockSpec(memory_space=VMEM),
        scratch_shapes=[pltpu.VMEM((OWN * ROWS, NLON), F32)],
        compiler_params=pltpu.CompilerParams(vmem_limit_bytes=40 << 20),
        cost_estimate=pl.CostEstimate(flops=480 << 20, bytes_accessed=4 << 20, transcendentals=0),
        name="longitude_stage",
    )(rows, table)


def stencil_coefs(kernel_values, near_rows, lat_index, ch_index):
    own_rows = lat_index * ROWS + jnp.arange(ROWS, dtype=jnp.int32)
    step = near_rows - own_rows[:, None] + REACH
    hit = (step[:, :, None] == jnp.arange(SPREAD, dtype=jnp.int32)).astype(F32)
    taps = jnp.sum(
        hit[None, :, :, :, None] * kernel_values.astype(F32)[:, :, :, None, :], axis=2
    )
    taps = jnp.transpose(taps, (1, 0, 2, 3)).reshape(ROWS * KER * SPREAD, TAPS)
    lane = jnp.arange(LANES, dtype=jnp.int32)
    orders = (lane % PICKS) // SUB * ORDER_BLOCK + lane % SUB + SUB * ch_index
    phases = (orders[None, :] * (jnp.arange(TAPS, dtype=jnp.int32) - LON_REACH)[:, None]) % NLON
    angles = phases.astype(F32) * (2.0 * math.pi / NLON)
    side = jnp.where(lane < PICKS, -1.0, 1.0).astype(F32)
    waves = jnp.stack([jnp.cos(angles), side * jnp.sin(angles)])
    return jnp.einsum("ns,xsl->xnl", taps, waves, precision=lax.Precision.HIGHEST)


def per_device(spectrum, legendre, block_slots, kernel_values, near_rows, mix_weights):
    lat_index = lax.axis_index("lat")
    ch_index = lax.axis_index("ch")
    wanted = (
        block_slots[:, None] * ORDER_BLOCK + SUB * ch_index + jnp.arange(SUB, dtype=jnp.int32)
    ).reshape(PICKS, 1)
    hot = (wanted == jnp.arange(LMAX, dtype=jnp.int32)).astype(BF)
    picked = pick(hot, legendre)
    leg = lax.all_to_all(picked, "lat", 0, 0, tiled=True)
    spec = lax.all_to_all(spectrum.reshape(CHS, C, STEPS), "ch", 0, 0, tiled=True)
    by_order = order_stage(leg, spec)
    by_row = lax.all_to_all(by_order, "lat", 0, 0, tiled=True)
    coefs = stencil_coefs(kernel_values, near_rows, lat_index, ch_index)
    mix = jnp.transpose(mix_weights, (2, 0, 1)).reshape(C, KER * C)
    mixed = row_stage(block_slots, by_row, coefs, jnp.concatenate([mix, mix], axis=1))
    own = lax.all_to_all(mixed, "ch", 0, 0, tiled=True)
    return longitude_stage(own, jnp.asarray(longitude_table()))


def solution(mesh):
    return jax.shard_map(
        per_device,
        mesh=mesh,
        in_specs=(
            P("lat", "ch", None, None, None),
            P("lat", None, None),
            P(),
            P(None, "lat", None, None),
            P("lat", None),
            P(),
        ),
        out_specs=P("ch", "lat", None),
        check_vma=False,
    )
```

```python
import math

import jax
import jax.numpy as jnp
import ml_dtypes
import numpy as np
from jax import lax
from jax.experimental import pallas as pl
from jax.experimental.pallas import tpu as pltpu
from jax.sharding import PartitionSpec as P

NLAT = 640
NLON = 1440
LMAX = 512
C = 64
ORDER_BLOCK = 16
KER = 3
SLOTS = 6
REACH = 2
LON_REACH = 4
TAPS = 9
STEPS = 256
BLOCKS = 32
LATS = 32
CHS = 8
ROWS = NLAT // LATS
OWN = C // CHS
SUB = ORDER_BLOCK // CHS
HALO_ROWS = ROWS + 2 * REACH
SPREAD = 2 * REACH + 1
PICKS = LATS * SUB
LANES = 128
BF = jnp.bfloat16
F32 = jnp.float32
NT = (((1,), (1,)), ((), ()))
TN = (((0,), (0,)), ((), ()))
VMEM = pltpu.VMEM
GRANT = 60 << 20
PAIR = 2
TURNS = CHS // PAIR
LAT_CHUNK = 8


HALF_LON = NLON // 2
WAVE_ROWS = 16


def order_table():
    orders = (
        ORDER_BLOCK * np.arange(BLOCKS)[None, :, None]
        + SUB * np.arange(CHS)[:, None, None]
        + np.arange(SUB)[None, None, :]
    )
    return orders.reshape(CHS, 1, PICKS, 1)


def longitude_table():
    orders = order_table()
    phases = (orders * np.arange(HALF_LON)) % NLON
    angles = phases * (2.0 * math.pi / NLON)
    weight = np.where(orders == 0, 1.0, 2.0)
    table = np.concatenate([weight * np.cos(angles), -weight * np.sin(angles)], axis=1)
    return table.reshape(CHS * LANES, HALF_LON).astype(ml_dtypes.bfloat16)


def wave_table():
    shifts = np.arange(TAPS)[:, None] - LON_REACH
    orders = order_table().reshape(CHS, 1, PICKS)
    angles = ((orders * shifts) % NLON) * (2.0 * math.pi / NLON)
    waves = np.zeros((CHS, WAVE_ROWS, 2 * LANES), np.float32)
    cosine, sine = np.cos(angles), np.sin(angles)
    waves[:, :TAPS] = np.concatenate([cosine, cosine, -sine, sine], axis=2)
    return waves


PICK_ROWS = 2
PICK_AHEAD = 4


def pick_kernel(slots_ref, leg_ref, out_ref, buf, wide, flat, sems, out_sem):
    copies = []
    for g in range(ROWS // PICK_ROWS):
        rows = pl.ds(g * PICK_ROWS, PICK_ROWS)
        copies.append(pltpu.make_async_copy(leg_ref.at[rows], buf.at[rows], sems.at[g]))
    for copy in copies[:PICK_AHEAD]:
        copy.start()
    lines = lax.broadcasted_iota(jnp.int32, (PICKS, LMAX), 0)
    orders = lax.broadcasted_iota(jnp.int32, (PICKS, LMAX), 1)
    blocks = jnp.zeros((PICKS, LMAX), jnp.int32)
    for i in range(LATS):
        blocks = jnp.where(lines // SUB == i, slots_ref[i], blocks)
    wanted = blocks * ORDER_BLOCK + lines % SUB + SUB * lax.axis_index("ch")
    hot = jnp.where(orders == wanted, 1.0, 0.0).astype(BF)
    for r in range(ROWS):
        if r % PICK_ROWS == 0:
            copies[r // PICK_ROWS].wait()
            for copy in copies[r // PICK_ROWS + PICK_AHEAD :][:1]:
                copy.start()
        picked = lax.dot_general(hot, buf[r], NT, preferred_element_type=F32)
        for h in range(STEPS // LANES):
            wide[h, pl.ds(r, PICKS, stride=ROWS), :] = picked[:, h * LANES : (h + 1) * LANES]
    for h in range(STEPS // LANES):
        half = wide[h].astype(BF)
        flat[:, :, h * LANES : (h + 1) * LANES] = half.reshape(LATS, SUB * ROWS, LANES)
    done = pltpu.make_async_copy(flat, out_ref, out_sem)
    done.start()
    done.wait()


def pick(block_slots, legendre):
    return pl.pallas_call(
        pick_kernel,
        out_shape=jax.ShapeDtypeStruct((LATS, SUB * ROWS, STEPS), BF),
        in_specs=[pl.BlockSpec(memory_space=pltpu.SMEM), pl.BlockSpec(memory_space=pltpu.HBM)],
        out_specs=pl.BlockSpec(memory_space=pltpu.HBM),
        scratch_shapes=[
            pltpu.VMEM((ROWS, STEPS, LMAX), BF),
            pltpu.VMEM((STEPS // LANES, PICKS * ROWS, LANES), F32),
            pltpu.VMEM((LATS, SUB * ROWS, STEPS), BF),
            pltpu.SemaphoreType.DMA((ROWS // PICK_ROWS,)),
            pltpu.SemaphoreType.DMA,
        ],
        compiler_params=pltpu.CompilerParams(vmem_limit_bytes=GRANT),
        cost_estimate=pl.CostEstimate(flops=2 * 64 * 512 * 5120, bytes_accessed=6 << 20, transcendentals=0),
        name="pick",
    )(block_slots, legendre)


def order_kernel(leg_ref, *refs):
    pieces_in, (out_ref, got, raw, leg, specs, full, send, sems) = refs[:TURNS], refs[TURNS:]
    half = NLAT // 2
    ch_index = lax.axis_index("ch")
    side = lax.rem(ch_index, PAIR)
    arrivals, departures = [], []
    for g in range(LATS // LAT_CHUNK):
        part = pl.ds(g * LAT_CHUNK, LAT_CHUNK)
        arrivals.append(pltpu.make_async_copy(leg_ref.at[part], got.at[part], sems.at[0, g]))
        arrivals[-1].start()
        departures.append(pltpu.make_async_copy(send.at[part], out_ref.at[part], sems.at[1, g]))
    for d in range(TURNS):
        turn = lax.rem(lax.div(ch_index, PAIR) + (TURNS - d), TURNS)
        for q in range(PAIR):
            source = turn * PAIR + (side if q == 0 else 1 - side)
            for h in range(STEPS // LANES):
                lanes = slice(h * LANES, (h + 1) * LANES)
                start = pl.multiple_of(source * C, C)
                specs[h, pl.ds(start, C), :] = pieces_in[d][q, :, lanes].astype(F32)
    for i in range(LATS):
        if i % LAT_CHUNK == 0:
            arrivals[i // LAT_CHUNK].wait()
        for h in range(STEPS // LANES):
            lanes = slice(h * LANES, (h + 1) * LANES)
            raw[h, pl.ds(i * SUB * ROWS, SUB * ROWS), :] = got[i, :, lanes].astype(F32)
    for i in range(LATS):
        for t in range(SUB):
            for h in range(STEPS // LANES):
                leg[t, h, pl.ds(i * ROWS, ROWS), :] = raw[h, pl.ds((i * SUB + t) * ROWS, ROWS), :]
    rows = lax.broadcasted_iota(jnp.int32, (LANES, LANES), 0)
    cols = lax.broadcasted_iota(jnp.int32, (LANES, LANES), 1)
    turn = jnp.where(rows + cols == LANES - 1, 1.0, 0.0).astype(BF)
    stride = 4
    full[...] = jnp.zeros_like(full)
    for t in range(SUB):
        table = jnp.concatenate([leg[t, h] for h in range(STEPS // LANES)], axis=1).astype(BF)
        count = NLAT // LANES
        turned = jnp.concatenate(
            [
                jnp.dot(
                    turn,
                    table[(count - 1 - n) * LANES : (count - n) * LANES],
                    preferred_element_type=F32,
                ).astype(BF)
                for n in range(count)
            ],
            axis=0,
        )
        coeffs = []
        for p in range(2):
            pieces = []
            for x in range(2):
                for j in range(CHS):
                    start = j * C + t * 4 * OWN + p * 2 + x
                    pieces.append(
                        jnp.concatenate(
                            [
                                specs[h, pl.ds(start, OWN, stride=stride), :]
                                for h in range(STEPS // LANES)
                            ],
                            axis=1,
                        )
                    )
            coeffs.append(jnp.concatenate(pieces, axis=0).astype(BF))

        def dot(a, b):
            return lax.dot_general(a, b, NT, preferred_element_type=F32)

        full[t, pl.ds(8, half), :] = dot(table[:half], coeffs[0]) - dot(turned[:half], coeffs[1])
        full[t, pl.ds(8 + half, half), :] = dot(table[half:], coeffs[1]) + dot(turned[half:], coeffs[0])
    for i in range(LATS):
        start = 8 - REACH + i * ROWS
        block = [full[t, pl.ds(start, HALO_ROWS), :] for t in range(SUB)]
        send[i] = jnp.concatenate(block, axis=0).astype(BF)
        if i % LAT_CHUNK == LAT_CHUNK - 1:
            departures[i // LAT_CHUNK].start()
    for copy in departures:
        copy.wait()


def order_stage(leg, pieces):
    return pl.pallas_call(
        order_kernel,
        out_shape=jax.ShapeDtypeStruct((LATS, SUB * HALO_ROWS, LANES), BF),
        in_specs=[pl.BlockSpec(memory_space=pltpu.HBM)] + [pl.BlockSpec(memory_space=VMEM)] * TURNS,
        out_specs=pl.BlockSpec(memory_space=pltpu.HBM),
        scratch_shapes=[
            pltpu.VMEM((LATS, SUB * ROWS, STEPS), BF),
            pltpu.VMEM((STEPS // LANES, LATS * SUB * ROWS, LANES), F32),
            pltpu.VMEM((SUB, STEPS // LANES, NLAT, LANES), F32),
            pltpu.VMEM((STEPS // LANES, CHS * C, LANES), F32),
            pltpu.VMEM((SUB, NLAT + 16, LANES), F32),
            pltpu.VMEM((LATS, SUB * HALO_ROWS, LANES), BF),
            pltpu.SemaphoreType.DMA((2, LATS // LAT_CHUNK)),
        ],
        compiler_params=pltpu.CompilerParams(vmem_limit_bytes=GRANT),
        cost_estimate=pl.CostEstimate(flops=700 << 20, bytes_accessed=2 << 20, transcendentals=0),
        name="order_stage",
    )(leg, *pieces)


def coef_kernel(values_ref, near_ref, mix_ref, waves_ref, coef_ref, mixed_ref, taps):
    first = lax.axis_index("lat") * ROWS
    step = near_ref[...] - lax.broadcasted_iota(jnp.int32, (SLOTS, ROWS), 1) - (first - REACH)
    taps[...] = jnp.zeros_like(taps)
    for d in range(SPREAD):
        hit = jnp.where(step == d, 1.0, 0.0)
        for b in range(KER):
            for s in range(TAPS):
                value = values_ref[b, s].astype(F32)
                taps[b * SPREAD + d, s : s + 1, :] = jnp.sum(hit * value, axis=0, keepdims=True)
    waves = waves_ref[lax.axis_index("ch")]
    for n in range(KER * SPREAD):
        coef_ref[n] = lax.dot_general(
            taps[n], waves, TN, precision=lax.Precision.HIGHEST, preferred_element_type=F32
        )
    turned = jnp.concatenate([mix_ref[b].astype(F32).T for b in range(KER)], axis=1)
    mixed_ref[...] = jnp.concatenate([turned, turned], axis=1).astype(BF)


def coef_stage(kernel_values, near_rows, mix_weights):
    return pl.pallas_call(
        coef_kernel,
        out_shape=(
            jax.ShapeDtypeStruct((KER * SPREAD, ROWS, 2 * LANES), F32),
            jax.ShapeDtypeStruct((C, 2 * KER * C), BF),
        ),
        in_specs=[pl.BlockSpec(memory_space=VMEM)] * 4,
        out_specs=[pl.BlockSpec(memory_space=VMEM)] * 2,
        scratch_shapes=[pltpu.VMEM((KER * SPREAD, WAVE_ROWS, ROWS), F32)],
        compiler_params=pltpu.CompilerParams(vmem_limit_bytes=16 << 20),
        cost_estimate=pl.CostEstimate(flops=16 << 20, bytes_accessed=1 << 20, transcendentals=0),
        name="coef_stage",
    )(
        jnp.transpose(kernel_values, (0, 3, 2, 1)),
        jnp.transpose(near_rows, (1, 0)),
        mix_weights,
        jnp.asarray(wave_table()),
    )


def row_kernel(slots_ref, rows_ref, coef_ref, mix_ref, out_ref, field, plain, crossed):
    for i in range(LATS):
        block = slots_ref[i]
        start = pl.multiple_of(block * (SUB * HALO_ROWS), 8)
        field[pl.ds(start, SUB * HALO_ROWS), :] = rows_ref[i].astype(F32)
    low = lax.broadcasted_iota(jnp.int32, (C, LANES), 1) < PICKS
    for r in range(HALO_ROWS):
        one = field[pl.ds(r, PICKS, stride=HALO_ROWS), :]
        both = jnp.concatenate([one, one], axis=0).T
        plain[r] = jnp.where(low, both[:C], both[C:])
        crossed[r] = jnp.where(low, both[C:], both[:C])
    for r in range(ROWS):
        tops, rests = [], []
        for b in range(KER):
            total = None
            for d in range(SPREAD):
                n = b * SPREAD + d
                term = coef_ref[n, r : r + 1, :LANES] * plain[r + d]
                term = term + coef_ref[n, r : r + 1, LANES:] * crossed[r + d]
                total = term if total is None else total + term
            top = total.astype(BF)
            tops.append(top)
            rests.append((total - top.astype(F32)).astype(BF))
        both = jnp.concatenate(tops + rests, axis=0)
        mixed = jnp.dot(mix_ref[...], both, preferred_element_type=F32)
        out_ref[:, r * OWN : (r + 1) * OWN, :] = mixed.astype(BF).reshape(CHS, OWN, LANES)


def row_stage(block_slots, rows, coefs, mix):
    return pl.pallas_call(
        row_kernel,
        out_shape=jax.ShapeDtypeStruct((CHS, OWN * ROWS, LANES), BF),
        in_specs=[
            pl.BlockSpec(memory_space=pltpu.SMEM),
            pl.BlockSpec(memory_space=VMEM),
            pl.BlockSpec(memory_space=VMEM),
            pl.BlockSpec(memory_space=VMEM),
        ],
        out_specs=pl.BlockSpec(memory_space=VMEM),
        scratch_shapes=[
            pltpu.VMEM((BLOCKS * SUB * HALO_ROWS, LANES), F32),
            pltpu.VMEM((HALO_ROWS, C, LANES), F32),
            pltpu.VMEM((HALO_ROWS, C, LANES), F32),
        ],
        compiler_params=pltpu.CompilerParams(vmem_limit_bytes=16 << 20),
        cost_estimate=pl.CostEstimate(flops=200 << 20, bytes_accessed=2 << 20, transcendentals=0),
        name="row_stage",
    )(block_slots, rows, coefs, mix)


def longitude_kernel(rows_ref, table_ref, out_ref):
    even = jnp.concatenate([rows_ref[j] for j in range(CHS)], axis=1)
    lane = lax.broadcasted_iota(jnp.int32, even.shape, 1)
    flipped = jnp.where(lane % SUB == 0, even.astype(F32), -even.astype(F32)).astype(BF)
    both = jnp.concatenate([even, flipped], axis=0)
    field = jnp.dot(both, table_ref[...], preferred_element_type=F32)
    count = OWN * ROWS
    whole = jnp.concatenate([field[:count], field[count:]], axis=1)
    out_ref[...] = whole.astype(BF).reshape(ROWS, OWN, NLON)


def longitude_stage(rows, table):
    return pl.pallas_call(
        longitude_kernel,
        out_shape=jax.ShapeDtypeStruct((ROWS, OWN, NLON), BF),
        in_specs=[pl.BlockSpec(memory_space=VMEM)] * 2,
        out_specs=pl.BlockSpec(memory_space=VMEM),
        compiler_params=pltpu.CompilerParams(vmem_limit_bytes=40 << 20),
        cost_estimate=pl.CostEstimate(flops=480 << 20, bytes_accessed=4 << 20, transcendentals=0),
        name="longitude_stage",
    )(rows, table)


def per_device(spectrum, legendre, block_slots, kernel_values, near_rows, mix_weights):
    ch_index = lax.axis_index("ch")
    picked = pick(block_slots, legendre)
    picked, spectrum = lax.optimization_barrier((picked, spectrum))
    leg = lax.all_to_all(picked, "lat", 0, 0, tiled=True)
    blocks = spectrum.reshape(TURNS, PAIR, C, STEPS)
    turn, side = ch_index // PAIR, ch_index % PAIR
    kept = lax.dynamic_index_in_dim(blocks, side, 1, keepdims=False)
    given = lax.dynamic_index_in_dim(blocks, 1 - side, 1, keepdims=False)
    taken = lax.ppermute(given, "ch", [(j, j ^ 1) for j in range(CHS)])
    both = jnp.stack([kept, taken], axis=1)
    pieces = []
    for d in range(TURNS):
        piece = lax.dynamic_index_in_dim(both, (turn + d) % TURNS, 0, keepdims=False)
        shift = [(j, (j + PAIR * d) % CHS) for j in range(CHS)]
        pieces.append(lax.ppermute(piece, "ch", shift) if d else piece)
    by_order = order_stage(leg, pieces)
    by_order, kernel_values, near_rows, mix_weights = lax.optimization_barrier(
        (by_order, kernel_values, near_rows, mix_weights)
    )
    by_row = lax.all_to_all(by_order, "lat", 0, 0, tiled=True)
    coefs, mix = coef_stage(kernel_values, near_rows, mix_weights)
    mixed = row_stage(block_slots, by_row, coefs, mix)
    own = lax.all_to_all(mixed, "ch", 0, 0, tiled=True)
    field = longitude_stage(own, jnp.asarray(longitude_table()))
    return jnp.transpose(field, (1, 0, 2))


def solution(mesh):
    return jax.shard_map(
        per_device,
        mesh=mesh,
        in_specs=(
            P("lat", "ch", None, None, None),
            P("lat", None, None),
            P(),
            P(None, "lat", None, None),
            P("lat", None),
            P(),
        ),
        out_specs=P("ch", "lat", None),
        check_vma=False,
    )
```

```python
import math

import jax
import jax.numpy as jnp
import ml_dtypes
import numpy as np
from jax import lax
from jax.experimental import pallas as pl
from jax.experimental.pallas import tpu as pltpu
from jax.sharding import PartitionSpec as P

NLAT = 640
NLON = 1440
LMAX = 512
C = 64
ORDER_BLOCK = 16
KER = 3
SLOTS = 6
REACH = 2
LON_REACH = 4
TAPS = 9
STEPS = 256
BLOCKS = 32
LATS = 32
CHS = 8
ROWS = NLAT // LATS
OWN = C // CHS
SUB = ORDER_BLOCK // CHS
HALO_ROWS = ROWS + 2 * REACH
SPREAD = 2 * REACH + 1
PICKS = LATS * SUB
LANES = 128
BF = jnp.bfloat16
F32 = jnp.float32
NT = (((1,), (1,)), ((), ()))
TN = (((0,), (0,)), ((), ()))
VMEM = pltpu.VMEM
GRANT = 60 << 20
PAIR = 2
TURNS = CHS // PAIR
LAT_CHUNK = 8


HALF_LON = NLON // 2
WAVE_ROWS = 16


def order_table():
    orders = (
        ORDER_BLOCK * np.arange(BLOCKS)[None, None, :]
        + SUB * np.arange(CHS)[:, None, None]
        + np.arange(SUB)[None, :, None]
    )
    return orders.reshape(CHS, 1, PICKS, 1)


def longitude_table():
    orders = order_table()
    phases = (orders * np.arange(HALF_LON)) % NLON
    angles = phases * (2.0 * math.pi / NLON)
    weight = np.where(orders == 0, 1.0, 2.0)
    table = np.concatenate([weight * np.cos(angles), -weight * np.sin(angles)], axis=1)
    return table.reshape(CHS * LANES, HALF_LON).astype(ml_dtypes.bfloat16)


def wave_table():
    shifts = np.arange(TAPS)[:, None] - LON_REACH
    orders = order_table().reshape(CHS, 1, PICKS)
    angles = ((orders * shifts) % NLON) * (2.0 * math.pi / NLON)
    waves = np.zeros((CHS, WAVE_ROWS, 2 * LANES), np.float32)
    cosine, sine = np.cos(angles), np.sin(angles)
    waves[:, :TAPS] = np.concatenate([cosine, cosine, -sine, sine], axis=2)
    return waves


PICK_ROWS = 4
PICK_AHEAD = 3
GROUPS = ROWS // PICK_ROWS
PICK_LINES = PICK_ROWS * SUB
EDGE = 12


def pick_kernel(slots_ref, leg_ref, out_ref, buf, wide, flat, sems):
    arrivals, departures = [], []
    for g in range(GROUPS):
        rows = pl.ds(g * PICK_ROWS, PICK_ROWS)
        lines = pl.ds(g * PICK_LINES, PICK_LINES)
        arrivals.append(pltpu.make_async_copy(leg_ref.at[rows], buf.at[rows], sems.at[0, g]))
        departures.append(pltpu.make_async_copy(flat.at[g], out_ref.at[:, lines, :], sems.at[1, g]))
    for copy in arrivals[:PICK_AHEAD]:
        copy.start()
    line = lax.broadcasted_iota(jnp.int32, (PICKS, LMAX), 0)
    order = lax.broadcasted_iota(jnp.int32, (PICKS, LMAX), 1)
    blocks = jnp.zeros((PICKS, LMAX), jnp.int32)
    for i in range(LATS):
        blocks = jnp.where(line % LATS == i, slots_ref[i], blocks)
    wanted = blocks * ORDER_BLOCK + line // LATS + SUB * lax.axis_index("ch")
    hot = jnp.where(order == wanted, 1.0, 0.0).astype(BF)
    for g in range(GROUPS):
        arrivals[g].wait()
        for copy in arrivals[g + PICK_AHEAD :][:1]:
            copy.start()
        for r in range(PICK_ROWS):
            picked = lax.dot_general(
                hot, buf[g * PICK_ROWS + r], NT, preferred_element_type=F32
            )
            for t in range(SUB):
                for h in range(STEPS // LANES):
                    wide[g, h, pl.ds(r * SUB + t, LATS, stride=PICK_LINES), :] = picked[
                        t * LATS : (t + 1) * LATS, h * LANES : (h + 1) * LANES
                    ]
        for h in range(STEPS // LANES):
            flat[g, :, :, h * LANES : (h + 1) * LANES] = (
                wide[g, h].reshape(LATS, PICK_LINES, LANES).astype(BF)
            )
        departures[g].start()
    for copy in departures:
        copy.wait()


def pick(block_slots, legendre):
    return pl.pallas_call(
        pick_kernel,
        out_shape=jax.ShapeDtypeStruct((LATS, ROWS * SUB, STEPS), BF),
        in_specs=[pl.BlockSpec(memory_space=pltpu.SMEM), pl.BlockSpec(memory_space=pltpu.HBM)],
        out_specs=pl.BlockSpec(memory_space=pltpu.HBM),
        scratch_shapes=[
            pltpu.VMEM((ROWS, STEPS, LMAX), BF),
            pltpu.VMEM((GROUPS, STEPS // LANES, LATS * PICK_LINES, LANES), F32),
            pltpu.VMEM((GROUPS, LATS, PICK_LINES, STEPS), BF),
            pltpu.SemaphoreType.DMA((2, GROUPS)),
        ],
        compiler_params=pltpu.CompilerParams(vmem_limit_bytes=GRANT),
        cost_estimate=pl.CostEstimate(flops=2 * 64 * 512 * 5120, bytes_accessed=6 << 20, transcendentals=0),
        name="pick",
    )(block_slots, legendre)


def order_kernel(leg_ref, *refs):
    pieces_in, (out_ref, raw, specs, full, send, sems) = refs[:TURNS], refs[TURNS:]
    half = NLAT // 2
    ch_index = lax.axis_index("ch")
    side = lax.rem(ch_index, PAIR)
    departures = []
    for g in range(LATS // LAT_CHUNK):
        part = pl.ds(g * LAT_CHUNK, LAT_CHUNK)
        departures.append(pltpu.make_async_copy(send.at[part], out_ref.at[part], sems.at[g]))
    for d in range(TURNS):
        turn = lax.rem(lax.div(ch_index, PAIR) + (TURNS - d), TURNS)
        for q in range(PAIR):
            source = turn * PAIR + (side if q == 0 else 1 - side)
            for h in range(STEPS // LANES):
                lanes = slice(h * LANES, (h + 1) * LANES)
                start = pl.multiple_of(source * C, C)
                specs[h, pl.ds(start, C), :] = pieces_in[d][q, :, lanes].astype(F32)
    for h in range(STEPS // LANES):
        lanes = slice(h * LANES, (h + 1) * LANES)
        raw[h] = leg_ref[:, :, lanes].astype(F32).reshape(LATS * ROWS * SUB, LANES)
    rows = lax.broadcasted_iota(jnp.int32, (LANES, LANES), 0)
    cols = lax.broadcasted_iota(jnp.int32, (LANES, LANES), 1)
    turn = jnp.where(rows + cols == LANES - 1, 1.0, 0.0).astype(BF)
    stride = 4
    full[:16, :] = jnp.zeros((16, LANES), F32)
    full[SUB * NLAT :, :] = jnp.zeros((2 * EDGE, LANES), F32)
    for t in range(SUB):
        table = jnp.concatenate(
            [raw[h, pl.ds(t, NLAT, stride=SUB), :] for h in range(STEPS // LANES)], axis=1
        ).astype(BF)
        count = NLAT // LANES
        turned = jnp.concatenate(
            [
                jnp.dot(
                    turn,
                    table[(count - 1 - n) * LANES : (count - n) * LANES],
                    preferred_element_type=F32,
                ).astype(BF)
                for n in range(count)
            ],
            axis=0,
        )
        coeffs = []
        for p in range(2):
            pieces = []
            for x in range(2):
                for j in range(CHS):
                    start = j * C + t * 4 * OWN + p * 2 + x
                    pieces.append(
                        jnp.concatenate(
                            [
                                specs[h, pl.ds(start, OWN, stride=stride), :]
                                for h in range(STEPS // LANES)
                            ],
                            axis=1,
                        )
                    )
            coeffs.append(jnp.concatenate(pieces, axis=0).astype(BF))

        def dot(a, b):
            return lax.dot_general(a, b, NT, preferred_element_type=F32)

        north = dot(table[:half], coeffs[0]) - dot(turned[:half], coeffs[1])
        south = dot(table[half:], coeffs[1]) + dot(turned[half:], coeffs[0])
        full[pl.ds(EDGE + t, half, stride=SUB), :] = north
        full[pl.ds(EDGE + t + SUB * half, half, stride=SUB), :] = south
    for i in range(LATS):
        start = EDGE - REACH * SUB + i * ROWS * SUB
        send[i] = full[start : start + HALO_ROWS * SUB, :].astype(BF)
        if i % LAT_CHUNK == LAT_CHUNK - 1:
            departures[i // LAT_CHUNK].start()
    for copy in departures:
        copy.wait()


def order_stage(leg, pieces):
    return pl.pallas_call(
        order_kernel,
        out_shape=jax.ShapeDtypeStruct((LATS, HALO_ROWS * SUB, LANES), BF),
        in_specs=[pl.BlockSpec(memory_space=VMEM)] * (1 + TURNS),
        out_specs=pl.BlockSpec(memory_space=pltpu.HBM),
        scratch_shapes=[
            pltpu.VMEM((STEPS // LANES, LATS * SUB * ROWS, LANES), F32),
            pltpu.VMEM((STEPS // LANES, CHS * C, LANES), F32),
            pltpu.VMEM((SUB * NLAT + 2 * EDGE, LANES), F32),
            pltpu.VMEM((LATS, SUB * HALO_ROWS, LANES), BF),
            pltpu.SemaphoreType.DMA((LATS // LAT_CHUNK,)),
        ],
        compiler_params=pltpu.CompilerParams(vmem_limit_bytes=GRANT),
        cost_estimate=pl.CostEstimate(flops=700 << 20, bytes_accessed=2 << 20, transcendentals=0),
        name="order_stage",
    )(leg, *pieces)


def coef_kernel(values_ref, near_ref, mix_ref, waves_ref, coef_ref, mixed_ref, taps):
    first = lax.axis_index("lat") * ROWS
    step = near_ref[...] - lax.broadcasted_iota(jnp.int32, (SLOTS, ROWS), 1) - (first - REACH)
    taps[...] = jnp.zeros_like(taps)
    for d in range(SPREAD):
        hit = jnp.where(step == d, 1.0, 0.0)
        for b in range(KER):
            for s in range(TAPS):
                value = values_ref[b, s].astype(F32)
                taps[b * SPREAD + d, s : s + 1, :] = jnp.sum(hit * value, axis=0, keepdims=True)
    waves = waves_ref[lax.axis_index("ch")]
    for n in range(KER * SPREAD):
        coef_ref[n] = lax.dot_general(
            taps[n], waves, TN, precision=lax.Precision.HIGHEST, preferred_element_type=F32
        )
    turned = jnp.concatenate([mix_ref[b].astype(F32).T for b in range(KER)], axis=1)
    mixed_ref[...] = jnp.concatenate([turned, turned], axis=1).astype(BF)


def coef_stage(kernel_values, near_rows, mix_weights):
    return pl.pallas_call(
        coef_kernel,
        out_shape=(
            jax.ShapeDtypeStruct((KER * SPREAD, ROWS, 2 * LANES), F32),
            jax.ShapeDtypeStruct((C, 2 * KER * C), BF),
        ),
        in_specs=[pl.BlockSpec(memory_space=VMEM)] * 4,
        out_specs=[pl.BlockSpec(memory_space=VMEM)] * 2,
        scratch_shapes=[pltpu.VMEM((KER * SPREAD, WAVE_ROWS, ROWS), F32)],
        compiler_params=pltpu.CompilerParams(vmem_limit_bytes=16 << 20),
        cost_estimate=pl.CostEstimate(flops=16 << 20, bytes_accessed=1 << 20, transcendentals=0),
        name="coef_stage",
    )(
        jnp.transpose(kernel_values, (0, 3, 2, 1)),
        jnp.transpose(near_rows, (1, 0)),
        mix_weights,
        jnp.asarray(wave_table()),
    )


def row_kernel(slots_ref, rows_ref, coef_ref, mix_ref, out_ref, field, plain, crossed):
    for i in range(LATS):
        block = slots_ref[i]
        start = pl.multiple_of(block * (SUB * HALO_ROWS), 8)
        field[pl.ds(start, SUB * HALO_ROWS), :] = rows_ref[i].astype(F32)
    low = lax.broadcasted_iota(jnp.int32, (C, LANES), 1) < PICKS
    for r in range(HALO_ROWS):
        one = jnp.concatenate(
            [
                field[pl.ds(r * SUB + t, BLOCKS, stride=SUB * HALO_ROWS), :]
                for t in range(SUB)
            ],
            axis=0,
        )
        both = jnp.concatenate([one, one], axis=0).T
        plain[r] = jnp.where(low, both[:C], both[C:])
        crossed[r] = jnp.where(low, both[C:], both[:C])
    for r in range(ROWS):
        tops, rests = [], []
        for b in range(KER):
            total = None
            for d in range(SPREAD):
                n = b * SPREAD + d
                term = coef_ref[n, r : r + 1, :LANES] * plain[r + d]
                term = term + coef_ref[n, r : r + 1, LANES:] * crossed[r + d]
                total = term if total is None else total + term
            top = total.astype(BF)
            tops.append(top)
            rests.append((total - top.astype(F32)).astype(BF))
        both = jnp.concatenate(tops + rests, axis=0)
        mixed = jnp.dot(mix_ref[...], both, preferred_element_type=F32)
        out_ref[:, r * OWN : (r + 1) * OWN, :] = mixed.astype(BF).reshape(CHS, OWN, LANES)


def row_stage(block_slots, rows, coefs, mix):
    return pl.pallas_call(
        row_kernel,
        out_shape=jax.ShapeDtypeStruct((CHS, OWN * ROWS, LANES), BF),
        in_specs=[
            pl.BlockSpec(memory_space=pltpu.SMEM),
            pl.BlockSpec(memory_space=VMEM),
            pl.BlockSpec(memory_space=VMEM),
            pl.BlockSpec(memory_space=VMEM),
        ],
        out_specs=pl.BlockSpec(memory_space=VMEM),
        scratch_shapes=[
            pltpu.VMEM((BLOCKS * SUB * HALO_ROWS, LANES), F32),
            pltpu.VMEM((HALO_ROWS, C, LANES), F32),
            pltpu.VMEM((HALO_ROWS, C, LANES), F32),
        ],
        compiler_params=pltpu.CompilerParams(vmem_limit_bytes=16 << 20),
        cost_estimate=pl.CostEstimate(flops=200 << 20, bytes_accessed=2 << 20, transcendentals=0),
        name="row_stage",
    )(block_slots, rows, coefs, mix)


def longitude_kernel(rows_ref, table_ref, out_ref):
    even = jnp.concatenate([rows_ref[j] for j in range(CHS)], axis=1)
    lane = lax.broadcasted_iota(jnp.int32, even.shape, 1)
    flipped = jnp.where(lane % PICKS < BLOCKS, even.astype(F32), -even.astype(F32)).astype(BF)
    both = jnp.concatenate([even, flipped], axis=0)
    field = jnp.dot(both, table_ref[...], preferred_element_type=F32)
    count = OWN * ROWS
    whole = jnp.concatenate([field[:count], field[count:]], axis=1)
    out_ref[...] = whole.astype(BF).reshape(ROWS, OWN, NLON)


def longitude_stage(rows, table):
    return pl.pallas_call(
        longitude_kernel,
        out_shape=jax.ShapeDtypeStruct((ROWS, OWN, NLON), BF),
        in_specs=[pl.BlockSpec(memory_space=VMEM)] * 2,
        out_specs=pl.BlockSpec(memory_space=VMEM),
        compiler_params=pltpu.CompilerParams(vmem_limit_bytes=40 << 20),
        cost_estimate=pl.CostEstimate(flops=480 << 20, bytes_accessed=4 << 20, transcendentals=0),
        name="longitude_stage",
    )(rows, table)


def per_device(spectrum, legendre, block_slots, kernel_values, near_rows, mix_weights):
    ch_index = lax.axis_index("ch")
    picked = pick(block_slots, legendre)
    picked, spectrum = lax.optimization_barrier((picked, spectrum))
    leg = lax.all_to_all(picked, "lat", 0, 0, tiled=True)
    blocks = spectrum.reshape(TURNS, PAIR, C, STEPS)
    turn, side = ch_index // PAIR, ch_index % PAIR
    kept = lax.dynamic_index_in_dim(blocks, side, 1, keepdims=False)
    given = lax.dynamic_index_in_dim(blocks, 1 - side, 1, keepdims=False)
    taken = lax.ppermute(given, "ch", [(j, j ^ 1) for j in range(CHS)])
    both = jnp.stack([kept, taken], axis=1)
    pieces = []
    for d in range(TURNS):
        piece = lax.dynamic_index_in_dim(both, (turn + d) % TURNS, 0, keepdims=False)
        shift = [(j, (j + PAIR * d) % CHS) for j in range(CHS)]
        pieces.append(lax.ppermute(piece, "ch", shift) if d else piece)
    by_order = order_stage(leg, pieces)
    by_order, kernel_values, near_rows, mix_weights = lax.optimization_barrier(
        (by_order, kernel_values, near_rows, mix_weights)
    )
    by_row = lax.all_to_all(by_order, "lat", 0, 0, tiled=True)
    coefs, mix = coef_stage(kernel_values, near_rows, mix_weights)
    mixed = row_stage(block_slots, by_row, coefs, mix)
    own = lax.all_to_all(mixed, "ch", 0, 0, tiled=True)
    field = longitude_stage(own, jnp.asarray(longitude_table()))
    return jnp.transpose(field, (1, 0, 2))


def solution(mesh):
    return jax.shard_map(
        per_device,
        mesh=mesh,
        in_specs=(
            P("lat", "ch", None, None, None),
            P("lat", None, None),
            P(),
            P(None, "lat", None, None),
            P("lat", None),
            P(),
        ),
        out_specs=P("ch", "lat", None),
        check_vma=False,
    )
```

```python
import math

import jax
import jax.numpy as jnp
import ml_dtypes
import numpy as np
from jax import lax
from jax.experimental import pallas as pl
from jax.experimental.pallas import tpu as pltpu
from jax.sharding import PartitionSpec as P

NLAT = 640
NLON = 1440
LMAX = 512
C = 64
ORDER_BLOCK = 16
KER = 3
SLOTS = 6
REACH = 2
LON_REACH = 4
TAPS = 9
STEPS = 256
BLOCKS = 32
LATS = 32
CHS = 8
ROWS = NLAT // LATS
OWN = C // CHS
SUB = ORDER_BLOCK // CHS
HALO_ROWS = ROWS + 2 * REACH
SPREAD = 2 * REACH + 1
PICKS = LATS * SUB
LANES = 128
BF = jnp.bfloat16
F32 = jnp.float32
NT = (((1,), (1,)), ((), ()))
TN = (((0,), (0,)), ((), ()))
VMEM = pltpu.VMEM
GRANT = 62 << 20
PAIR = 2
TURNS = CHS // PAIR
LAT_CHUNK = 8


HALF_LON = NLON // 2
WAVE_ROWS = 16


def order_table():
    orders = (
        ORDER_BLOCK * np.arange(BLOCKS)[None, None, :]
        + SUB * np.arange(CHS)[:, None, None]
        + np.arange(SUB)[None, :, None]
    )
    return orders.reshape(CHS, 1, PICKS, 1)


def longitude_table():
    orders = order_table()
    phases = (orders * np.arange(HALF_LON)) % NLON
    angles = phases * (2.0 * math.pi / NLON)
    weight = np.where(orders == 0, 1.0, 2.0)
    table = np.concatenate([weight * np.cos(angles), -weight * np.sin(angles)], axis=1)
    return table.reshape(CHS * LANES, HALF_LON).astype(ml_dtypes.bfloat16)


def wave_table():
    shifts = np.arange(TAPS)[:, None] - LON_REACH
    orders = order_table().reshape(CHS, 1, PICKS)
    angles = ((orders * shifts) % NLON) * (2.0 * math.pi / NLON)
    waves = np.zeros((CHS, WAVE_ROWS, 2 * LANES), np.float32)
    cosine, sine = np.cos(angles), np.sin(angles)
    waves[:, :TAPS] = np.concatenate([cosine, cosine, -sine, sine], axis=2)
    return waves


PICK_ROWS = 4
PICK_AHEAD = 4
GROUPS = ROWS // PICK_ROWS
PICK_LINES = PICK_ROWS * SUB
EDGE = 12
ORDER_LIMITS = (LMAX, LMAX - 2 * LANES)


def pick_kernel(slots_ref, leg_ref, out_ref, buf, wide, flat, sems):
    arrivals, departures = [], []
    for g in range(GROUPS):
        rows = pl.ds(g * PICK_ROWS, PICK_ROWS)
        lines = pl.ds(g * PICK_LINES, PICK_LINES)
        pair = []
        for h in range(STEPS // LANES):
            part = (rows, pl.ds(h * LANES, LANES), pl.ds(0, ORDER_LIMITS[h]))
            pair.append(pltpu.make_async_copy(leg_ref.at[part], buf.at[part], sems.at[h, g]))
        arrivals.append(pair)
        departures.append(pltpu.make_async_copy(flat.at[g], out_ref.at[:, lines, :], sems.at[2, g]))
    for pair in arrivals[:PICK_AHEAD]:
        for copy in pair:
            copy.start()
    line = lax.broadcasted_iota(jnp.int32, (PICKS, LANES), 0)
    lane = lax.broadcasted_iota(jnp.int32, (PICKS, LANES), 1)
    blocks = jnp.zeros((PICKS, LANES), jnp.int32)
    for i in range(LATS):
        blocks = jnp.where(line % LATS == i, slots_ref[i], blocks)
    wanted = blocks * ORDER_BLOCK + line // LATS + SUB * lax.axis_index("ch")
    hot = jnp.concatenate(
        [
            jnp.where(lane + n * LANES == wanted, 1.0, 0.0).astype(BF)
            for n in range(LMAX // LANES)
        ],
        axis=1,
    )
    for g in range(GROUPS):
        for copy in arrivals[g]:
            copy.wait()
        for pair in arrivals[g + PICK_AHEAD :][:1]:
            for copy in pair:
                copy.start()
        for r in range(PICK_ROWS):
            for h in range(STEPS // LANES):
                limit = ORDER_LIMITS[h]
                block = buf[g * PICK_ROWS + r, h * LANES : (h + 1) * LANES, :limit]
                picked = lax.dot_general(hot[:, :limit], block, NT, preferred_element_type=F32)
                for t in range(SUB):
                    wide[g, h, pl.ds(r * SUB + t, LATS, stride=PICK_LINES), :] = picked[
                        t * LATS : (t + 1) * LATS
                    ]
        for h in range(STEPS // LANES):
            flat[g, :, :, h * LANES : (h + 1) * LANES] = (
                wide[g, h].reshape(LATS, PICK_LINES, LANES).astype(BF)
            )
        departures[g].start()
    for copy in departures:
        copy.wait()


def pick(block_slots, legendre):
    return pl.pallas_call(
        pick_kernel,
        out_shape=jax.ShapeDtypeStruct((LATS, ROWS * SUB, STEPS), BF),
        in_specs=[pl.BlockSpec(memory_space=pltpu.SMEM), pl.BlockSpec(memory_space=pltpu.HBM)],
        out_specs=pl.BlockSpec(memory_space=pltpu.HBM),
        scratch_shapes=[
            pltpu.VMEM((ROWS, STEPS, LMAX), BF),
            pltpu.VMEM((GROUPS, STEPS // LANES, LATS * PICK_LINES, LANES), F32),
            pltpu.VMEM((GROUPS, LATS, PICK_LINES, STEPS), BF),
            pltpu.SemaphoreType.DMA((3, GROUPS)),
        ],
        compiler_params=pltpu.CompilerParams(vmem_limit_bytes=GRANT),
        cost_estimate=pl.CostEstimate(flops=2 * 64 * 512 * 5120, bytes_accessed=6 << 20, transcendentals=0),
        name="pick",
    )(block_slots, legendre)


def order_kernel(leg_ref, *refs):
    pieces_in, (out_ref, got, raw, specs, full, send, sems) = refs[:TURNS], refs[TURNS:]
    half = NLAT // 2
    ch_index = lax.axis_index("ch")
    side = lax.rem(ch_index, PAIR)
    arrivals, departures = [], []
    for g in range(LATS // LAT_CHUNK):
        part = pl.ds(g * LAT_CHUNK, LAT_CHUNK)
        arrivals.append(pltpu.make_async_copy(leg_ref.at[part], got.at[part], sems.at[0, g]))
        arrivals[-1].start()
        departures.append(pltpu.make_async_copy(send.at[part], out_ref.at[part], sems.at[1, g]))
    for d in range(TURNS):
        turn = lax.rem(lax.div(ch_index, PAIR) + (TURNS - d), TURNS)
        for q in range(PAIR):
            source = turn * PAIR + (side if q == 0 else 1 - side)
            for h in range(STEPS // LANES):
                lanes = slice(h * LANES, (h + 1) * LANES)
                start = pl.multiple_of(source * C, C)
                specs[h, pl.ds(start, C), :] = pieces_in[d][q, :, lanes].astype(F32)
    lines = LAT_CHUNK * ROWS * SUB
    for g in range(LATS // LAT_CHUNK):
        arrivals[g].wait()
        part = got[g * LAT_CHUNK : (g + 1) * LAT_CHUNK]
        for h in range(STEPS // LANES):
            lanes = slice(h * LANES, (h + 1) * LANES)
            raw[h, pl.ds(g * lines, lines), :] = part[:, :, lanes].astype(F32).reshape(lines, LANES)
    rows = lax.broadcasted_iota(jnp.int32, (LANES, LANES), 0)
    cols = lax.broadcasted_iota(jnp.int32, (LANES, LANES), 1)
    turn = jnp.where(rows + cols == LANES - 1, 1.0, 0.0).astype(BF)
    stride = 4
    full[:16, :] = jnp.zeros((16, LANES), F32)
    full[SUB * NLAT :, :] = jnp.zeros((2 * EDGE, LANES), F32)
    for t in range(SUB):
        table = jnp.concatenate(
            [raw[h, pl.ds(t, NLAT, stride=SUB), :] for h in range(STEPS // LANES)], axis=1
        ).astype(BF)
        count = NLAT // LANES
        turned = jnp.concatenate(
            [
                jnp.dot(
                    turn,
                    table[(count - 1 - n) * LANES : (count - n) * LANES],
                    preferred_element_type=F32,
                ).astype(BF)
                for n in range(count)
            ],
            axis=0,
        )
        coeffs = []
        for p in range(2):
            pieces = []
            for x in range(2):
                for j in range(CHS):
                    start = j * C + t * 4 * OWN + p * 2 + x
                    pieces.append(
                        jnp.concatenate(
                            [
                                specs[h, pl.ds(start, OWN, stride=stride), :]
                                for h in range(STEPS // LANES)
                            ],
                            axis=1,
                        )
                    )
            coeffs.append(jnp.concatenate(pieces, axis=0).astype(BF))

        def dot(a, b):
            return lax.dot_general(a, b, NT, preferred_element_type=F32)

        north = dot(table[:half], coeffs[0]) - dot(turned[:half], coeffs[1])
        south = dot(table[half:], coeffs[1]) + dot(turned[half:], coeffs[0])
        full[pl.ds(EDGE + t, half, stride=SUB), :] = north
        full[pl.ds(EDGE + t + SUB * half, half, stride=SUB), :] = south
    for i in range(LATS):
        start = EDGE - REACH * SUB + i * ROWS * SUB
        send[i] = full[start : start + HALO_ROWS * SUB, :].astype(BF)
        if i % LAT_CHUNK == LAT_CHUNK - 1:
            departures[i // LAT_CHUNK].start()
    for copy in departures:
        copy.wait()


def order_stage(leg, pieces):
    return pl.pallas_call(
        order_kernel,
        out_shape=jax.ShapeDtypeStruct((LATS, HALO_ROWS * SUB, LANES), BF),
        in_specs=[pl.BlockSpec(memory_space=pltpu.HBM)] + [pl.BlockSpec(memory_space=VMEM)] * TURNS,
        out_specs=pl.BlockSpec(memory_space=pltpu.HBM),
        scratch_shapes=[
            pltpu.VMEM((LATS, SUB * ROWS, STEPS), BF),
            pltpu.VMEM((STEPS // LANES, LATS * SUB * ROWS, LANES), F32),
            pltpu.VMEM((STEPS // LANES, CHS * C, LANES), F32),
            pltpu.VMEM((SUB * NLAT + 2 * EDGE, LANES), F32),
            pltpu.VMEM((LATS, SUB * HALO_ROWS, LANES), BF),
            pltpu.SemaphoreType.DMA((2, LATS // LAT_CHUNK)),
        ],
        compiler_params=pltpu.CompilerParams(vmem_limit_bytes=GRANT),
        cost_estimate=pl.CostEstimate(flops=700 << 20, bytes_accessed=2 << 20, transcendentals=0),
        name="order_stage",
    )(leg, *pieces)


def coef_kernel(values_ref, near_ref, mix_ref, waves_ref, coef_ref, mixed_ref, taps):
    first = lax.axis_index("lat") * ROWS
    step = near_ref[...] - lax.broadcasted_iota(jnp.int32, (SLOTS, ROWS), 1) - (first - REACH)
    taps[...] = jnp.zeros_like(taps)
    for d in range(SPREAD):
        hit = jnp.where(step == d, 1.0, 0.0)
        for b in range(KER):
            for s in range(TAPS):
                value = values_ref[b, s].astype(F32)
                taps[b * SPREAD + d, s : s + 1, :] = jnp.sum(hit * value, axis=0, keepdims=True)
    waves = waves_ref[lax.axis_index("ch")]
    for n in range(KER * SPREAD):
        coef_ref[n] = lax.dot_general(
            taps[n], waves, TN, precision=lax.Precision.HIGHEST, preferred_element_type=F32
        )
    turned = jnp.concatenate([mix_ref[b].astype(F32).T for b in range(KER)], axis=1)
    mixed_ref[...] = jnp.concatenate([turned, turned], axis=1).astype(BF)


def coef_stage(kernel_values, near_rows, mix_weights):
    return pl.pallas_call(
        coef_kernel,
        out_shape=(
            jax.ShapeDtypeStruct((KER * SPREAD, ROWS, 2 * LANES), F32),
            jax.ShapeDtypeStruct((C, 2 * KER * C), BF),
        ),
        in_specs=[pl.BlockSpec(memory_space=VMEM)] * 4,
        out_specs=[pl.BlockSpec(memory_space=VMEM)] * 2,
        scratch_shapes=[pltpu.VMEM((KER * SPREAD, WAVE_ROWS, ROWS), F32)],
        compiler_params=pltpu.CompilerParams(vmem_limit_bytes=16 << 20),
        cost_estimate=pl.CostEstimate(flops=16 << 20, bytes_accessed=1 << 20, transcendentals=0),
        name="coef_stage",
    )(
        jnp.transpose(kernel_values, (0, 3, 2, 1)),
        jnp.transpose(near_rows, (1, 0)),
        mix_weights,
        jnp.asarray(wave_table()),
    )


def row_kernel(slots_ref, rows_ref, coef_ref, mix_ref, out_ref, field, plain, crossed):
    for i in range(LATS):
        block = slots_ref[i]
        start = pl.multiple_of(block * (SUB * HALO_ROWS), 8)
        field[pl.ds(start, SUB * HALO_ROWS), :] = rows_ref[i].astype(F32)
    low = lax.broadcasted_iota(jnp.int32, (C, LANES), 1) < PICKS
    for r in range(HALO_ROWS):
        one = jnp.concatenate(
            [
                field[pl.ds(r * SUB + t, BLOCKS, stride=SUB * HALO_ROWS), :]
                for t in range(SUB)
            ],
            axis=0,
        )
        both = jnp.concatenate([one, one], axis=0).T
        plain[r] = jnp.where(low, both[:C], both[C:])
        crossed[r] = jnp.where(low, both[C:], both[:C])
    for r in range(ROWS):
        tops, rests = [], []
        for b in range(KER):
            total = None
            for d in range(SPREAD):
                n = b * SPREAD + d
                term = coef_ref[n, r : r + 1, :LANES] * plain[r + d]
                term = term + coef_ref[n, r : r + 1, LANES:] * crossed[r + d]
                total = term if total is None else total + term
            top = total.astype(BF)
            tops.append(top)
            rests.append((total - top.astype(F32)).astype(BF))
        both = jnp.concatenate(tops + rests, axis=0)
        mixed = jnp.dot(mix_ref[...], both, preferred_element_type=F32)
        out_ref[:, r * OWN : (r + 1) * OWN, :] = mixed.astype(BF).reshape(CHS, OWN, LANES)


def row_stage(block_slots, rows, coefs, mix):
    return pl.pallas_call(
        row_kernel,
        out_shape=jax.ShapeDtypeStruct((CHS, OWN * ROWS, LANES), BF),
        in_specs=[
            pl.BlockSpec(memory_space=pltpu.SMEM),
            pl.BlockSpec(memory_space=VMEM),
            pl.BlockSpec(memory_space=VMEM),
            pl.BlockSpec(memory_space=VMEM),
        ],
        out_specs=pl.BlockSpec(memory_space=VMEM),
        scratch_shapes=[
            pltpu.VMEM((BLOCKS * SUB * HALO_ROWS, LANES), F32),
            pltpu.VMEM((HALO_ROWS, C, LANES), F32),
            pltpu.VMEM((HALO_ROWS, C, LANES), F32),
        ],
        compiler_params=pltpu.CompilerParams(vmem_limit_bytes=16 << 20),
        cost_estimate=pl.CostEstimate(flops=200 << 20, bytes_accessed=2 << 20, transcendentals=0),
        name="row_stage",
    )(block_slots, rows, coefs, mix)


LON_PARTS = 4


def longitude_kernel(rows_ref, table_ref, out_ref, field, whole, sems):
    even = jnp.concatenate([rows_ref[j] for j in range(CHS)], axis=1)
    lane = lax.broadcasted_iota(jnp.int32, even.shape, 1)
    flipped = jnp.where(lane % PICKS < BLOCKS, even.astype(F32), -even.astype(F32)).astype(BF)
    both = jnp.concatenate([even, flipped], axis=0)
    field[...] = jnp.dot(both, table_ref[...], preferred_element_type=F32)
    count, rows = OWN * ROWS, ROWS // LON_PARTS
    lines = rows * OWN
    departures = []
    for g in range(LON_PARTS):
        first = field[g * lines : (g + 1) * lines]
        second = field[count + g * lines : count + (g + 1) * lines]
        part = pl.ds(g * rows, rows)
        whole[part] = jnp.concatenate([first, second], axis=1).astype(BF).reshape(rows, OWN, NLON)
        departures.append(pltpu.make_async_copy(whole.at[part], out_ref.at[part], sems.at[g]))
        departures[-1].start()
    for copy in departures:
        copy.wait()


def longitude_stage(rows, table):
    return pl.pallas_call(
        longitude_kernel,
        out_shape=jax.ShapeDtypeStruct((ROWS, OWN, NLON), BF),
        in_specs=[pl.BlockSpec(memory_space=VMEM)] * 2,
        out_specs=pl.BlockSpec(memory_space=pltpu.HBM),
        scratch_shapes=[
            pltpu.VMEM((2 * OWN * ROWS, HALF_LON), F32),
            pltpu.VMEM((ROWS, OWN, NLON), BF),
            pltpu.SemaphoreType.DMA((LON_PARTS,)),
        ],
        compiler_params=pltpu.CompilerParams(vmem_limit_bytes=40 << 20),
        cost_estimate=pl.CostEstimate(flops=480 << 20, bytes_accessed=4 << 20, transcendentals=0),
        name="longitude_stage",
    )(rows, table)


def per_device(spectrum, legendre, block_slots, kernel_values, near_rows, mix_weights):
    ch_index = lax.axis_index("ch")
    picked = pick(block_slots, legendre)
    picked, spectrum = lax.optimization_barrier((picked, spectrum))
    leg = lax.all_to_all(picked, "lat", 0, 0, tiled=True)
    blocks = spectrum.reshape(TURNS, PAIR, C, STEPS)
    turn, side = ch_index // PAIR, ch_index % PAIR
    kept = lax.dynamic_index_in_dim(blocks, side, 1, keepdims=False)
    given = lax.dynamic_index_in_dim(blocks, 1 - side, 1, keepdims=False)
    taken = lax.ppermute(given, "ch", [(j, j ^ 1) for j in range(CHS)])
    both = jnp.stack([kept, taken], axis=1)
    pieces = []
    for d in range(TURNS):
        piece = lax.dynamic_index_in_dim(both, (turn + d) % TURNS, 0, keepdims=False)
        shift = [(j, (j + PAIR * d) % CHS) for j in range(CHS)]
        pieces.append(lax.ppermute(piece, "ch", shift) if d else piece)
    by_order = order_stage(leg, pieces)
    by_order, kernel_values, near_rows, mix_weights = lax.optimization_barrier(
        (by_order, kernel_values, near_rows, mix_weights)
    )
    by_row = lax.all_to_all(by_order, "lat", 0, 0, tiled=True)
    coefs, mix = coef_stage(kernel_values, near_rows, mix_weights)
    mixed = row_stage(block_slots, by_row, coefs, mix)
    own = lax.all_to_all(mixed, "ch", 0, 0, tiled=True)
    field = longitude_stage(own, jnp.asarray(longitude_table()))
    return jnp.transpose(field, (1, 0, 2))


def solution(mesh):
    return jax.shard_map(
        per_device,
        mesh=mesh,
        in_specs=(
            P("lat", "ch", None, None, None),
            P("lat", None, None),
            P(),
            P(None, "lat", None, None),
            P("lat", None),
            P(),
        ),
        out_specs=P("ch", "lat", None),
        check_vma=False,
    )
```

```python
import math

import jax
import jax.numpy as jnp
import ml_dtypes
import numpy as np
from jax import lax
from jax.experimental import pallas as pl
from jax.experimental.pallas import tpu as pltpu
from jax.sharding import PartitionSpec as P

NLAT = 640
NLON = 1440
LMAX = 512
C = 64
ORDER_BLOCK = 16
KER = 3
SLOTS = 6
REACH = 2
LON_REACH = 4
TAPS = 9
STEPS = 256
BLOCKS = 32
LATS = 32
CHS = 8
ROWS = NLAT // LATS
OWN = C // CHS
SUB = ORDER_BLOCK // CHS
HALO_ROWS = ROWS + 2 * REACH
SPREAD = 2 * REACH + 1
PICKS = LATS * SUB
LANES = 128
BF = jnp.bfloat16
F32 = jnp.float32
NT = (((1,), (1,)), ((), ()))
TN = (((0,), (0,)), ((), ()))
VMEM = pltpu.VMEM
GRANT = 62 << 20
PAIR = 2
TURNS = CHS // PAIR


HALF_LON = NLON // 2
WAVE_ROWS = 16


def order_table():
    orders = (
        ORDER_BLOCK * np.arange(BLOCKS)[None, None, :]
        + SUB * np.arange(CHS)[:, None, None]
        + np.arange(SUB)[None, :, None]
    )
    return orders.reshape(CHS, 1, PICKS, 1)


def longitude_table():
    orders = order_table()
    phases = (orders * np.arange(HALF_LON)) % NLON
    angles = phases * (2.0 * math.pi / NLON)
    weight = np.where(orders == 0, 1.0, 2.0)
    table = np.concatenate([weight * np.cos(angles), -weight * np.sin(angles)], axis=1)
    return table.reshape(CHS * LANES, HALF_LON).astype(ml_dtypes.bfloat16)


def wave_table():
    shifts = np.arange(TAPS)[:, None] - LON_REACH
    orders = order_table().reshape(CHS, 1, PICKS)
    angles = ((orders * shifts) % NLON) * (2.0 * math.pi / NLON)
    waves = np.zeros((CHS, WAVE_ROWS, 2 * LANES), np.float32)
    cosine, sine = np.cos(angles), np.sin(angles)
    waves[:, :TAPS] = np.concatenate([cosine, cosine, -sine, sine], axis=2)
    return waves


PICK_ROWS = 4
PICK_AHEAD = 4
GROUPS = ROWS // PICK_ROWS
PICK_LINES = PICK_ROWS * SUB
EDGE = 12
ORDER_LIMITS = (LMAX, LMAX - 2 * LANES)


def pick_kernel(slots_ref, leg_ref, out_ref, buf, wide, flat, sems):
    arrivals, departures = [], []
    for g in range(GROUPS):
        rows = pl.ds(g * PICK_ROWS, PICK_ROWS)
        lines = pl.ds(g * PICK_LINES, PICK_LINES)
        pair = []
        for h in range(STEPS // LANES):
            part = (rows, pl.ds(h * LANES, LANES), pl.ds(0, ORDER_LIMITS[h]))
            pair.append(pltpu.make_async_copy(leg_ref.at[part], buf.at[part], sems.at[h, g]))
        arrivals.append(pair)
        departures.append(pltpu.make_async_copy(flat.at[g], out_ref.at[:, lines, :], sems.at[2, g]))
    for pair in arrivals[:PICK_AHEAD]:
        for copy in pair:
            copy.start()
    line = lax.broadcasted_iota(jnp.int32, (PICKS, LANES), 0)
    lane = lax.broadcasted_iota(jnp.int32, (PICKS, LANES), 1)
    blocks = jnp.zeros((PICKS, LANES), jnp.int32)
    for i in range(LATS):
        blocks = jnp.where(line % LATS == i, slots_ref[i], blocks)
    wanted = blocks * ORDER_BLOCK + line // LATS + SUB * lax.axis_index("ch")
    hot = jnp.concatenate(
        [
            jnp.where(lane + n * LANES == wanted, 1.0, 0.0).astype(BF)
            for n in range(LMAX // LANES)
        ],
        axis=1,
    )
    for g in range(GROUPS):
        for copy in arrivals[g]:
            copy.wait()
        for pair in arrivals[g + PICK_AHEAD :][:1]:
            for copy in pair:
                copy.start()
        for r in range(PICK_ROWS):
            for h in range(STEPS // LANES):
                limit = ORDER_LIMITS[h]
                block = buf[g * PICK_ROWS + r, h * LANES : (h + 1) * LANES, :limit]
                picked = lax.dot_general(hot[:, :limit], block, NT, preferred_element_type=F32)
                for t in range(SUB):
                    wide[g, h, pl.ds(r * SUB + t, LATS, stride=PICK_LINES), :] = picked[
                        t * LATS : (t + 1) * LATS
                    ]
        for h in range(STEPS // LANES):
            flat[g, :, :, h * LANES : (h + 1) * LANES] = (
                wide[g, h].reshape(LATS, PICK_LINES, LANES).astype(BF)
            )
        departures[g].start()
    for copy in departures:
        copy.wait()


def pick(block_slots, legendre):
    return pl.pallas_call(
        pick_kernel,
        out_shape=jax.ShapeDtypeStruct((LATS, ROWS * SUB, STEPS), BF),
        in_specs=[pl.BlockSpec(memory_space=pltpu.SMEM), pl.BlockSpec(memory_space=pltpu.HBM)],
        out_specs=pl.BlockSpec(memory_space=pltpu.HBM),
        scratch_shapes=[
            pltpu.VMEM((ROWS, STEPS, LMAX), BF),
            pltpu.VMEM((GROUPS, STEPS // LANES, LATS * PICK_LINES, LANES), F32),
            pltpu.VMEM((GROUPS, LATS, PICK_LINES, STEPS), BF),
            pltpu.SemaphoreType.DMA((3, GROUPS)),
        ],
        compiler_params=pltpu.CompilerParams(vmem_limit_bytes=GRANT),
        cost_estimate=pl.CostEstimate(flops=2 * 64 * 512 * 5120, bytes_accessed=6 << 20, transcendentals=0),
        name="pick",
    )(block_slots, legendre)


def order_kernel(leg_ref, *refs):
    pieces_in, (out_ref, raw, specs, full) = refs[:TURNS], refs[TURNS:]
    half = NLAT // 2
    ch_index = lax.axis_index("ch")
    side = lax.rem(ch_index, PAIR)
    for d in range(TURNS):
        turn = lax.rem(lax.div(ch_index, PAIR) + (TURNS - d), TURNS)
        for q in range(PAIR):
            source = turn * PAIR + (side if q == 0 else 1 - side)
            for h in range(STEPS // LANES):
                lanes = slice(h * LANES, (h + 1) * LANES)
                start = pl.multiple_of(source * C, C)
                specs[h, pl.ds(start, C), :] = pieces_in[d][q, :, lanes].astype(F32)
    for h in range(STEPS // LANES):
        lanes = slice(h * LANES, (h + 1) * LANES)
        raw[h] = leg_ref[:, :, lanes].astype(F32).reshape(LATS * ROWS * SUB, LANES)
    rows = lax.broadcasted_iota(jnp.int32, (LANES, LANES), 0)
    cols = lax.broadcasted_iota(jnp.int32, (LANES, LANES), 1)
    turn = jnp.where(rows + cols == LANES - 1, 1.0, 0.0).astype(BF)
    stride = 4
    full[:16, :] = jnp.zeros((16, LANES), F32)
    full[SUB * NLAT :, :] = jnp.zeros((2 * EDGE, LANES), F32)
    for t in range(SUB):
        table = jnp.concatenate(
            [raw[h, pl.ds(t, NLAT, stride=SUB), :] for h in range(STEPS // LANES)], axis=1
        ).astype(BF)
        count = NLAT // LANES
        turned = jnp.concatenate(
            [
                jnp.dot(
                    turn,
                    table[(count - 1 - n) * LANES : (count - n) * LANES],
                    preferred_element_type=F32,
                ).astype(BF)
                for n in range(count)
            ],
            axis=0,
        )
        coeffs = []
        for p in range(2):
            pieces = []
            for x in range(2):
                for j in range(CHS):
                    start = j * C + t * 4 * OWN + p * 2 + x
                    pieces.append(
                        jnp.concatenate(
                            [
                                specs[h, pl.ds(start, OWN, stride=stride), :]
                                for h in range(STEPS // LANES)
                            ],
                            axis=1,
                        )
                    )
            coeffs.append(jnp.concatenate(pieces, axis=0).astype(BF))

        def dot(a, b):
            return lax.dot_general(a, b, NT, preferred_element_type=F32)

        north = dot(table[:half], coeffs[0]) - dot(turned[:half], coeffs[1])
        south = dot(table[half:], coeffs[1]) + dot(turned[half:], coeffs[0])
        full[pl.ds(EDGE + t, half, stride=SUB), :] = north
        full[pl.ds(EDGE + t + SUB * half, half, stride=SUB), :] = south
    for i in range(LATS):
        start = EDGE - REACH * SUB + i * ROWS * SUB
        out_ref[i] = full[start : start + HALO_ROWS * SUB, :].astype(BF)


def order_stage(leg, pieces):
    return pl.pallas_call(
        order_kernel,
        out_shape=jax.ShapeDtypeStruct((LATS, HALO_ROWS * SUB, LANES), BF),
        in_specs=[pl.BlockSpec(memory_space=VMEM)] * (1 + TURNS),
        out_specs=pl.BlockSpec(memory_space=VMEM),
        scratch_shapes=[
            pltpu.VMEM((STEPS // LANES, LATS * SUB * ROWS, LANES), F32),
            pltpu.VMEM((STEPS // LANES, CHS * C, LANES), F32),
            pltpu.VMEM((SUB * NLAT + 2 * EDGE, LANES), F32),
        ],
        compiler_params=pltpu.CompilerParams(vmem_limit_bytes=24 << 20),
        cost_estimate=pl.CostEstimate(flops=700 << 20, bytes_accessed=2 << 20, transcendentals=0),
        name="order_stage",
    )(leg, *pieces)


def coef_kernel(values_ref, near_ref, mix_ref, waves_ref, coef_ref, mixed_ref, taps):
    first = lax.axis_index("lat") * ROWS
    step = near_ref[...] - lax.broadcasted_iota(jnp.int32, (SLOTS, ROWS), 1) - (first - REACH)
    taps[...] = jnp.zeros_like(taps)
    for d in range(SPREAD):
        hit = jnp.where(step == d, 1.0, 0.0)
        for b in range(KER):
            for s in range(TAPS):
                value = values_ref[b, s].astype(F32)
                taps[b * SPREAD + d, s : s + 1, :] = jnp.sum(hit * value, axis=0, keepdims=True)
    waves = waves_ref[lax.axis_index("ch")]
    for n in range(KER * SPREAD):
        coef_ref[n] = lax.dot_general(
            taps[n], waves, TN, precision=lax.Precision.HIGHEST, preferred_element_type=F32
        )
    turned = jnp.concatenate([mix_ref[b].astype(F32).T for b in range(KER)], axis=1)
    mixed_ref[...] = jnp.concatenate([turned, turned], axis=1).astype(BF)


def coef_stage(kernel_values, near_rows, mix_weights):
    return pl.pallas_call(
        coef_kernel,
        out_shape=(
            jax.ShapeDtypeStruct((KER * SPREAD, ROWS, 2 * LANES), F32),
            jax.ShapeDtypeStruct((C, 2 * KER * C), BF),
        ),
        in_specs=[pl.BlockSpec(memory_space=VMEM)] * 4,
        out_specs=[pl.BlockSpec(memory_space=VMEM)] * 2,
        scratch_shapes=[pltpu.VMEM((KER * SPREAD, WAVE_ROWS, ROWS), F32)],
        compiler_params=pltpu.CompilerParams(vmem_limit_bytes=16 << 20),
        cost_estimate=pl.CostEstimate(flops=16 << 20, bytes_accessed=1 << 20, transcendentals=0),
        name="coef_stage",
    )(
        jnp.transpose(kernel_values, (0, 3, 2, 1)),
        jnp.transpose(near_rows, (1, 0)),
        mix_weights,
        jnp.asarray(wave_table()),
    )


def row_kernel(slots_ref, rows_ref, coef_ref, mix_ref, out_ref, field, plain, crossed):
    for i in range(LATS):
        block = slots_ref[i]
        start = pl.multiple_of(block * (SUB * HALO_ROWS), 8)
        field[pl.ds(start, SUB * HALO_ROWS), :] = rows_ref[i].astype(F32)
    low = lax.broadcasted_iota(jnp.int32, (C, LANES), 1) < PICKS
    for r in range(HALO_ROWS):
        one = jnp.concatenate(
            [
                field[pl.ds(r * SUB + t, BLOCKS, stride=SUB * HALO_ROWS), :]
                for t in range(SUB)
            ],
            axis=0,
        )
        both = jnp.concatenate([one, one], axis=0).T
        plain[r] = jnp.where(low, both[:C], both[C:])
        crossed[r] = jnp.where(low, both[C:], both[:C])
    for r in range(ROWS):
        tops, rests = [], []
        for b in range(KER):
            total = None
            for d in range(SPREAD):
                n = b * SPREAD + d
                term = coef_ref[n, r : r + 1, :LANES] * plain[r + d]
                term = term + coef_ref[n, r : r + 1, LANES:] * crossed[r + d]
                total = term if total is None else total + term
            top = total.astype(BF)
            tops.append(top)
            rests.append((total - top.astype(F32)).astype(BF))
        both = jnp.concatenate(tops + rests, axis=0)
        mixed = jnp.dot(mix_ref[...], both, preferred_element_type=F32)
        out_ref[:, r * OWN : (r + 1) * OWN, :] = mixed.astype(BF).reshape(CHS, OWN, LANES)


def row_stage(block_slots, rows, coefs, mix):
    return pl.pallas_call(
        row_kernel,
        out_shape=jax.ShapeDtypeStruct((CHS, OWN * ROWS, LANES), BF),
        in_specs=[
            pl.BlockSpec(memory_space=pltpu.SMEM),
            pl.BlockSpec(memory_space=VMEM),
            pl.BlockSpec(memory_space=VMEM),
            pl.BlockSpec(memory_space=VMEM),
        ],
        out_specs=pl.BlockSpec(memory_space=VMEM),
        scratch_shapes=[
            pltpu.VMEM((BLOCKS * SUB * HALO_ROWS, LANES), F32),
            pltpu.VMEM((HALO_ROWS, C, LANES), F32),
            pltpu.VMEM((HALO_ROWS, C, LANES), F32),
        ],
        compiler_params=pltpu.CompilerParams(vmem_limit_bytes=16 << 20),
        cost_estimate=pl.CostEstimate(flops=200 << 20, bytes_accessed=2 << 20, transcendentals=0),
        name="row_stage",
    )(block_slots, rows, coefs, mix)


LON_PARTS = 4


def longitude_kernel(rows_ref, table_ref, out_ref, field, whole, sems):
    even = jnp.concatenate([rows_ref[j] for j in range(CHS)], axis=1)
    lane = lax.broadcasted_iota(jnp.int32, even.shape, 1)
    flipped = jnp.where(lane % PICKS < BLOCKS, even.astype(F32), -even.astype(F32)).astype(BF)
    both = jnp.concatenate([even, flipped], axis=0)
    field[...] = jnp.dot(both, table_ref[...], preferred_element_type=F32)
    count, rows = OWN * ROWS, ROWS // LON_PARTS
    lines = rows * OWN
    departures = []
    for g in range(LON_PARTS):
        first = field[g * lines : (g + 1) * lines]
        second = field[count + g * lines : count + (g + 1) * lines]
        part = pl.ds(g * rows, rows)
        whole[part] = jnp.concatenate([first, second], axis=1).astype(BF).reshape(rows, OWN, NLON)
        departures.append(pltpu.make_async_copy(whole.at[part], out_ref.at[part], sems.at[g]))
        departures[-1].start()
    for copy in departures:
        copy.wait()


def longitude_stage(rows, table):
    return pl.pallas_call(
        longitude_kernel,
        out_shape=jax.ShapeDtypeStruct((ROWS, OWN, NLON), BF),
        in_specs=[pl.BlockSpec(memory_space=VMEM)] * 2,
        out_specs=pl.BlockSpec(memory_space=pltpu.HBM),
        scratch_shapes=[
            pltpu.VMEM((2 * OWN * ROWS, HALF_LON), F32),
            pltpu.VMEM((ROWS, OWN, NLON), BF),
            pltpu.SemaphoreType.DMA((LON_PARTS,)),
        ],
        compiler_params=pltpu.CompilerParams(vmem_limit_bytes=40 << 20),
        cost_estimate=pl.CostEstimate(flops=480 << 20, bytes_accessed=4 << 20, transcendentals=0),
        name="longitude_stage",
    )(rows, table)


def per_device(spectrum, legendre, block_slots, kernel_values, near_rows, mix_weights):
    ch_index = lax.axis_index("ch")
    picked = pick(block_slots, legendre)
    picked, spectrum = lax.optimization_barrier((picked, spectrum))
    leg = lax.all_to_all(picked, "lat", 0, 0, tiled=True)
    blocks = spectrum.reshape(TURNS, PAIR, C, STEPS)
    turn, side = ch_index // PAIR, ch_index % PAIR
    kept = lax.dynamic_index_in_dim(blocks, side, 1, keepdims=False)
    given = lax.dynamic_index_in_dim(blocks, 1 - side, 1, keepdims=False)
    taken = lax.ppermute(given, "ch", [(j, j ^ 1) for j in range(CHS)])
    both = jnp.stack([kept, taken], axis=1)
    pieces = []
    for d in range(TURNS):
        piece = lax.dynamic_index_in_dim(both, (turn + d) % TURNS, 0, keepdims=False)
        shift = [(j, (j + PAIR * d) % CHS) for j in range(CHS)]
        pieces.append(lax.ppermute(piece, "ch", shift) if d else piece)
    by_order = order_stage(leg, pieces)
    by_order, kernel_values, near_rows, mix_weights = lax.optimization_barrier(
        (by_order, kernel_values, near_rows, mix_weights)
    )
    by_row = lax.all_to_all(by_order, "lat", 0, 0, tiled=True)
    coefs, mix = coef_stage(kernel_values, near_rows, mix_weights)
    mixed = row_stage(block_slots, by_row, coefs, mix)
    own = lax.all_to_all(mixed, "ch", 0, 0, tiled=True)
    field = longitude_stage(own, jnp.asarray(longitude_table()))
    return jnp.transpose(field, (1, 0, 2))


def solution(mesh):
    return jax.shard_map(
        per_device,
        mesh=mesh,
        in_specs=(
            P("lat", "ch", None, None, None),
            P("lat", None, None),
            P(),
            P(None, "lat", None, None),
            P("lat", None),
            P(),
        ),
        out_specs=P("ch", "lat", None),
        check_vma=False,
    )
```

```python
import math

import jax
import jax.numpy as jnp
import ml_dtypes
import numpy as np
from jax import lax
from jax.experimental import pallas as pl
from jax.experimental.pallas import tpu as pltpu
from jax.sharding import PartitionSpec as P

NLAT = 640
NLON = 1440
LMAX = 512
C = 64
ORDER_BLOCK = 16
KER = 3
SLOTS = 6
REACH = 2
LON_REACH = 4
TAPS = 9
STEPS = 256
BLOCKS = 32
LATS = 32
CHS = 8
ROWS = NLAT // LATS
OWN = C // CHS
SUB = ORDER_BLOCK // CHS
HALO_ROWS = ROWS + 2 * REACH
SPREAD = 2 * REACH + 1
PICKS = LATS * SUB
LANES = 128
BF = jnp.bfloat16
F32 = jnp.float32
NT = (((1,), (1,)), ((), ()))
TN = (((0,), (0,)), ((), ()))
VMEM = pltpu.VMEM
GRANT = 62 << 20
PAIR = 2
TURNS = CHS // PAIR


HALF_LON = NLON // 2
WAVE_ROWS = 16


def order_table():
    orders = (
        ORDER_BLOCK * np.arange(BLOCKS)[None, None, :]
        + SUB * np.arange(CHS)[:, None, None]
        + np.arange(SUB)[None, :, None]
    )
    return orders.reshape(CHS, 1, PICKS, 1)


def longitude_table():
    orders = order_table()
    phases = (orders * np.arange(HALF_LON)) % NLON
    angles = phases * (2.0 * math.pi / NLON)
    weight = np.where(orders == 0, 1.0, 2.0)
    table = np.concatenate([weight * np.cos(angles), -weight * np.sin(angles)], axis=1)
    return table.reshape(CHS * LANES, HALF_LON).astype(ml_dtypes.bfloat16)


def wave_table():
    shifts = np.arange(TAPS)[:, None] - LON_REACH
    orders = order_table().reshape(CHS, 1, PICKS)
    angles = ((orders * shifts) % NLON) * (2.0 * math.pi / NLON)
    waves = np.zeros((CHS, WAVE_ROWS, 2 * LANES), np.float32)
    cosine, sine = np.cos(angles), np.sin(angles)
    waves[:, :TAPS] = np.concatenate([cosine, cosine, -sine, sine], axis=2)
    return waves


PICK_GROUPS = (4, 4, 8, 4)
EDGE = 12
ORDER_LIMITS = (LMAX, LMAX - 2 * LANES)


def pick_kernel(slots_ref, leg_ref, out_ref, buf, wide, flat, sems):
    arrivals, departures, firsts = [], [], []
    for g, count in enumerate(PICK_GROUPS):
        first = sum(PICK_GROUPS[:g])
        firsts.append(first)
        pair = []
        for h in range(STEPS // LANES):
            part = (pl.ds(first, count), pl.ds(h * LANES, LANES), pl.ds(0, ORDER_LIMITS[h]))
            pair.append(pltpu.make_async_copy(leg_ref.at[part], buf.at[part], sems.at[h, g]))
            pair[-1].start()
        arrivals.append(pair)
        lines = pl.ds(first * SUB, count * SUB)
        departures.append(
            pltpu.make_async_copy(flat.at[:, lines, :], out_ref.at[:, lines, :], sems.at[2, g])
        )
    line = lax.broadcasted_iota(jnp.int32, (PICKS, LANES), 0)
    lane = lax.broadcasted_iota(jnp.int32, (PICKS, LANES), 1)
    blocks = jnp.zeros((PICKS, LANES), jnp.int32)
    for i in range(LATS):
        blocks = jnp.where(line % LATS == i, slots_ref[i], blocks)
    wanted = blocks * ORDER_BLOCK + line // LATS + SUB * lax.axis_index("ch")
    hot = jnp.concatenate(
        [
            jnp.where(lane + n * LANES == wanted, 1.0, 0.0).astype(BF)
            for n in range(LMAX // LANES)
        ],
        axis=1,
    )
    for g, count in enumerate(PICK_GROUPS):
        for copy in arrivals[g]:
            copy.wait()
        first, size = firsts[g], count * SUB
        base = first * SUB * LATS
        for h in range(STEPS // LANES):
            limit = ORDER_LIMITS[h]
            lanes = slice(h * LANES, (h + 1) * LANES)
            for r in range(count):
                block = buf[first + r, lanes, :limit]
                picked = lax.dot_general(hot[:, :limit], block, NT, preferred_element_type=F32)
                for t in range(SUB):
                    wide[h, pl.ds(base + r * SUB + t, LATS, stride=size), :] = picked[
                        t * LATS : (t + 1) * LATS
                    ]
            flat[:, first * SUB : first * SUB + size, lanes] = (
                wide[h, base : base + LATS * size].reshape(LATS, size, LANES).astype(BF)
            )
        departures[g].start()
    for copy in departures:
        copy.wait()


def pick(block_slots, legendre):
    return pl.pallas_call(
        pick_kernel,
        out_shape=jax.ShapeDtypeStruct((LATS, ROWS * SUB, STEPS), BF),
        in_specs=[pl.BlockSpec(memory_space=pltpu.SMEM), pl.BlockSpec(memory_space=pltpu.HBM)],
        out_specs=pl.BlockSpec(memory_space=pltpu.HBM),
        scratch_shapes=[
            pltpu.VMEM((ROWS, STEPS, LMAX), BF),
            pltpu.VMEM((STEPS // LANES, LATS * ROWS * SUB, LANES), F32),
            pltpu.VMEM((LATS, ROWS * SUB, STEPS), BF),
            pltpu.SemaphoreType.DMA((3, len(PICK_GROUPS))),
        ],
        compiler_params=pltpu.CompilerParams(vmem_limit_bytes=GRANT),
        cost_estimate=pl.CostEstimate(flops=2 * 64 * 512 * 5120, bytes_accessed=6 << 20, transcendentals=0),
        name="pick",
    )(block_slots, legendre)


def order_kernel(leg_ref, *refs):
    pieces_in, (out_ref, raw, specs, full) = refs[:TURNS], refs[TURNS:]
    half = NLAT // 2
    ch_index = lax.axis_index("ch")
    side = lax.rem(ch_index, PAIR)
    for d in range(TURNS):
        turn = lax.rem(lax.div(ch_index, PAIR) + (TURNS - d), TURNS)
        for q in range(PAIR):
            source = turn * PAIR + (side if q == 0 else 1 - side)
            for h in range(STEPS // LANES):
                lanes = slice(h * LANES, (h + 1) * LANES)
                start = pl.multiple_of(source * C, C)
                specs[h, pl.ds(start, C), :] = pieces_in[d][q, :, lanes].astype(F32)
    for h in range(STEPS // LANES):
        lanes = slice(h * LANES, (h + 1) * LANES)
        raw[h] = leg_ref[:, :, lanes].astype(F32).reshape(LATS * ROWS * SUB, LANES)
    rows = lax.broadcasted_iota(jnp.int32, (LANES, LANES), 0)
    cols = lax.broadcasted_iota(jnp.int32, (LANES, LANES), 1)
    turn = jnp.where(rows + cols == LANES - 1, 1.0, 0.0).astype(BF)
    stride = 4
    full[:16, :] = jnp.zeros((16, LANES), F32)
    full[SUB * NLAT :, :] = jnp.zeros((2 * EDGE, LANES), F32)
    for t in range(SUB):
        table = jnp.concatenate(
            [raw[h, pl.ds(t, NLAT, stride=SUB), :] for h in range(STEPS // LANES)], axis=1
        ).astype(BF)
        count = NLAT // LANES
        turned = jnp.concatenate(
            [
                jnp.dot(
                    turn,
                    table[(count - 1 - n) * LANES : (count - n) * LANES],
                    preferred_element_type=F32,
                ).astype(BF)
                for n in range(count)
            ],
            axis=0,
        )
        coeffs = []
        for p in range(2):
            pieces = []
            for x in range(2):
                for j in range(CHS):
                    start = j * C + t * 4 * OWN + p * 2 + x
                    pieces.append(
                        jnp.concatenate(
                            [
                                specs[h, pl.ds(start, OWN, stride=stride), :]
                                for h in range(STEPS // LANES)
                            ],
                            axis=1,
                        )
                    )
            coeffs.append(jnp.concatenate(pieces, axis=0).astype(BF))

        def dot(a, b):
            return lax.dot_general(a, b, NT, preferred_element_type=F32)

        north = dot(table[:half], coeffs[0]) - dot(turned[:half], coeffs[1])
        south = dot(table[half:], coeffs[1]) + dot(turned[half:], coeffs[0])
        full[pl.ds(EDGE + t, half, stride=SUB), :] = north
        full[pl.ds(EDGE + t + SUB * half, half, stride=SUB), :] = south
    for i in range(LATS):
        start = EDGE - REACH * SUB + i * ROWS * SUB
        out_ref[i] = full[start : start + HALO_ROWS * SUB, :].astype(BF)


def order_stage(leg, pieces):
    return pl.pallas_call(
        order_kernel,
        out_shape=jax.ShapeDtypeStruct((LATS, HALO_ROWS * SUB, LANES), BF),
        in_specs=[pl.BlockSpec(memory_space=VMEM)] * (1 + TURNS),
        out_specs=pl.BlockSpec(memory_space=VMEM),
        scratch_shapes=[
            pltpu.VMEM((STEPS // LANES, LATS * SUB * ROWS, LANES), F32),
            pltpu.VMEM((STEPS // LANES, CHS * C, LANES), F32),
            pltpu.VMEM((SUB * NLAT + 2 * EDGE, LANES), F32),
        ],
        compiler_params=pltpu.CompilerParams(vmem_limit_bytes=24 << 20),
        cost_estimate=pl.CostEstimate(flops=700 << 20, bytes_accessed=2 << 20, transcendentals=0),
        name="order_stage",
    )(leg, *pieces)


def coef_kernel(values_ref, near_ref, mix_ref, waves_ref, coef_ref, mixed_ref, taps):
    first = lax.axis_index("lat") * ROWS
    step = near_ref[...] - lax.broadcasted_iota(jnp.int32, (SLOTS, ROWS), 1) - (first - REACH)
    taps[...] = jnp.zeros_like(taps)
    for d in range(SPREAD):
        hit = jnp.where(step == d, 1.0, 0.0)
        for b in range(KER):
            for s in range(TAPS):
                value = values_ref[b, s].astype(F32)
                taps[b * SPREAD + d, s : s + 1, :] = jnp.sum(hit * value, axis=0, keepdims=True)
    waves = waves_ref[lax.axis_index("ch")]
    for n in range(KER * SPREAD):
        coef_ref[n] = lax.dot_general(
            taps[n], waves, TN, precision=lax.Precision.HIGHEST, preferred_element_type=F32
        )
    turned = jnp.concatenate([mix_ref[b].astype(F32).T for b in range(KER)], axis=0)
    mixed_ref[...] = jnp.concatenate([turned, turned], axis=1).astype(BF)


def coef_stage(kernel_values, near_rows, mix_weights):
    return pl.pallas_call(
        coef_kernel,
        out_shape=(
            jax.ShapeDtypeStruct((KER * SPREAD, ROWS, 2 * LANES), F32),
            jax.ShapeDtypeStruct((KER * C, 2 * C), BF),
        ),
        in_specs=[pl.BlockSpec(memory_space=VMEM)] * 4,
        out_specs=[pl.BlockSpec(memory_space=VMEM)] * 2,
        scratch_shapes=[pltpu.VMEM((KER * SPREAD, WAVE_ROWS, ROWS), F32)],
        compiler_params=pltpu.CompilerParams(vmem_limit_bytes=16 << 20),
        cost_estimate=pl.CostEstimate(flops=16 << 20, bytes_accessed=1 << 20, transcendentals=0),
        name="coef_stage",
    )(
        jnp.transpose(kernel_values, (0, 3, 2, 1)),
        jnp.transpose(near_rows, (1, 0)),
        mix_weights,
        jnp.asarray(wave_table()),
    )


def row_kernel(slots_ref, rows_ref, coef_ref, mix_ref, out_ref, field, mixed):
    for i in range(LATS):
        block = slots_ref[i]
        start = pl.multiple_of(block * (SUB * HALO_ROWS), 8)
        field[pl.ds(start, SUB * HALO_ROWS), :] = rows_ref[i].astype(F32)
    low = lax.broadcasted_iota(jnp.int32, (PICKS, LANES), 1) < C
    weights = mix_ref[...]
    for r in range(HALO_ROWS):
        one = jnp.concatenate(
            [
                field[pl.ds(r * SUB + t, BLOCKS, stride=SUB * HALO_ROWS), :]
                for t in range(SUB)
            ],
            axis=0,
        )
        real = jnp.where(low, one, 0.0)
        imag = jnp.where(low, 0.0, one)
        both = jnp.concatenate([real, imag, imag, real], axis=0).astype(BF)
        mixed[r] = lax.dot_general(weights, both, NT, preferred_element_type=F32)
    for r in range(ROWS):
        total = None
        for b in range(KER):
            for d in range(SPREAD):
                n = b * SPREAD + d
                part = mixed[r + d, b * C : (b + 1) * C, :]
                term = coef_ref[n, r : r + 1, :LANES] * part[:, :LANES]
                term = term + coef_ref[n, r : r + 1, LANES:] * part[:, LANES:]
                total = term if total is None else total + term
        out_ref[:, r * OWN : (r + 1) * OWN, :] = total.astype(BF).reshape(CHS, OWN, LANES)


def row_stage(block_slots, rows, coefs, mix):
    return pl.pallas_call(
        row_kernel,
        out_shape=jax.ShapeDtypeStruct((CHS, OWN * ROWS, LANES), BF),
        in_specs=[
            pl.BlockSpec(memory_space=pltpu.SMEM),
            pl.BlockSpec(memory_space=VMEM),
            pl.BlockSpec(memory_space=VMEM),
            pl.BlockSpec(memory_space=VMEM),
        ],
        out_specs=pl.BlockSpec(memory_space=VMEM),
        scratch_shapes=[
            pltpu.VMEM((BLOCKS * SUB * HALO_ROWS, LANES), F32),
            pltpu.VMEM((HALO_ROWS, KER * C, 2 * LANES), F32),
        ],
        compiler_params=pltpu.CompilerParams(vmem_limit_bytes=16 << 20),
        cost_estimate=pl.CostEstimate(flops=200 << 20, bytes_accessed=2 << 20, transcendentals=0),
        name="row_stage",
    )(block_slots, rows, coefs, mix)


LON_PARTS = 2


def longitude_kernel(rows_ref, table_ref, out_ref, whole, sems):
    rows = ROWS // LON_PARTS
    lines = rows * OWN
    departures = []
    for g in range(LON_PARTS):
        even = jnp.concatenate(
            [rows_ref[j, g * lines : (g + 1) * lines] for j in range(CHS)], axis=1
        )
        lane = lax.broadcasted_iota(jnp.int32, even.shape, 1)
        flipped = jnp.where(lane % PICKS < BLOCKS, even.astype(F32), -even.astype(F32)).astype(BF)
        both = jnp.concatenate([even, flipped], axis=0)
        field = jnp.dot(both, table_ref[...], preferred_element_type=F32)
        part = pl.ds(g * rows, rows)
        halves = jnp.concatenate([field[:lines], field[lines:]], axis=1)
        whole[part] = halves.astype(BF).reshape(rows, OWN, NLON)
        departures.append(pltpu.make_async_copy(whole.at[part], out_ref.at[part], sems.at[g]))
        departures[-1].start()
    for copy in departures:
        copy.wait()


def longitude_stage(rows, table):
    return pl.pallas_call(
        longitude_kernel,
        out_shape=jax.ShapeDtypeStruct((ROWS, OWN, NLON), BF),
        in_specs=[pl.BlockSpec(memory_space=VMEM)] * 2,
        out_specs=pl.BlockSpec(memory_space=pltpu.HBM),
        scratch_shapes=[
            pltpu.VMEM((ROWS, OWN, NLON), BF),
            pltpu.SemaphoreType.DMA((LON_PARTS,)),
        ],
        compiler_params=pltpu.CompilerParams(vmem_limit_bytes=40 << 20),
        cost_estimate=pl.CostEstimate(flops=480 << 20, bytes_accessed=4 << 20, transcendentals=0),
        name="longitude_stage",
    )(rows, table)


def per_device(spectrum, legendre, block_slots, kernel_values, near_rows, mix_weights):
    ch_index = lax.axis_index("ch")
    picked = pick(block_slots, legendre)
    picked, spectrum = lax.optimization_barrier((picked, spectrum))
    leg = lax.all_to_all(picked, "lat", 0, 0, tiled=True)
    blocks = spectrum.reshape(TURNS, PAIR, C, STEPS)
    turn, side = ch_index // PAIR, ch_index % PAIR
    kept = lax.dynamic_index_in_dim(blocks, side, 1, keepdims=False)
    given = lax.dynamic_index_in_dim(blocks, 1 - side, 1, keepdims=False)
    taken = lax.ppermute(given, "ch", [(j, j ^ 1) for j in range(CHS)])
    both = jnp.stack([kept, taken], axis=1)
    pieces = []
    for d in range(TURNS):
        piece = lax.dynamic_index_in_dim(both, (turn + d) % TURNS, 0, keepdims=False)
        shift = [(j, (j + PAIR * d) % CHS) for j in range(CHS)]
        pieces.append(lax.ppermute(piece, "ch", shift) if d else piece)
    by_order = order_stage(leg, pieces)
    by_order, kernel_values, near_rows, mix_weights = lax.optimization_barrier(
        (by_order, kernel_values, near_rows, mix_weights)
    )
    by_row = lax.all_to_all(by_order, "lat", 0, 0, tiled=True)
    coefs, mix = coef_stage(kernel_values, near_rows, mix_weights)
    mixed = row_stage(block_slots, by_row, coefs, mix)
    own = lax.all_to_all(mixed, "ch", 0, 0, tiled=True)
    field = longitude_stage(own, jnp.asarray(longitude_table()))
    return jnp.transpose(field, (1, 0, 2))


def solution(mesh):
    return jax.shard_map(
        per_device,
        mesh=mesh,
        in_specs=(
            P("lat", "ch", None, None, None),
            P("lat", None, None),
            P(),
            P(None, "lat", None, None),
            P("lat", None),
            P(),
        ),
        out_specs=P("ch", "lat", None),
        check_vma=False,
    )
```

```python
import math

import jax
import jax.numpy as jnp
import ml_dtypes
import numpy as np
from jax import lax
from jax.experimental import pallas as pl
from jax.experimental.pallas import tpu as pltpu
from jax.sharding import PartitionSpec as P

NLAT = 640
NLON = 1440
LMAX = 512
C = 64
ORDER_BLOCK = 16
KER = 3
SLOTS = 6
REACH = 2
LON_REACH = 4
TAPS = 9
STEPS = 256
BLOCKS = 32
LATS = 32
CHS = 8
ROWS = NLAT // LATS
OWN = C // CHS
SUB = ORDER_BLOCK // CHS
HALO_ROWS = ROWS + 2 * REACH
SPREAD = 2 * REACH + 1
PICKS = LATS * SUB
LANES = 128
BF = jnp.bfloat16
F32 = jnp.float32
NT = (((1,), (1,)), ((), ()))
TN = (((0,), (0,)), ((), ()))
VMEM = pltpu.VMEM
GRANT = 62 << 20
MARGIN = 48
PAIR = 2
TURNS = CHS // PAIR


HALF_LON = NLON // 2
WAVE_ROWS = 16


def order_table():
    orders = (
        ORDER_BLOCK * np.arange(BLOCKS)[None, None, :]
        + SUB * np.arange(CHS)[:, None, None]
        + np.arange(SUB)[None, :, None]
    )
    return orders.reshape(CHS, 1, PICKS, 1)


def longitude_table():
    orders = order_table()
    phases = (orders * np.arange(HALF_LON)) % NLON
    angles = phases * (2.0 * math.pi / NLON)
    weight = np.where(orders == 0, 1.0, 2.0)
    table = np.concatenate([weight * np.cos(angles), -weight * np.sin(angles)], axis=1)
    return table.reshape(CHS * LANES, HALF_LON).astype(ml_dtypes.bfloat16)


def wave_table():
    shifts = np.arange(TAPS)[:, None] - LON_REACH
    orders = order_table().reshape(CHS, 1, PICKS)
    angles = ((orders * shifts) % NLON) * (2.0 * math.pi / NLON)
    waves = np.zeros((CHS, WAVE_ROWS, 2 * LANES), np.float32)
    cosine, sine = np.cos(angles), np.sin(angles)
    waves[:, :TAPS] = np.concatenate([cosine, cosine, -sine, sine], axis=2)
    return waves


PICK_GROUPS = (4, 4, 8, 4)
EDGE = 12
ORDER_LIMITS = (LMAX, LMAX - 2 * LANES)


def pick_kernel(slots_ref, leg_ref, out_ref, buf, wide, flat, sems):
    arrivals, departures, firsts = [], [], []
    for g, count in enumerate(PICK_GROUPS):
        first = sum(PICK_GROUPS[:g])
        firsts.append(first)
        pair = []
        for h in range(STEPS // LANES):
            part = (pl.ds(first, count), pl.ds(h * LANES, LANES), pl.ds(0, ORDER_LIMITS[h]))
            pair.append(pltpu.make_async_copy(leg_ref.at[part], buf.at[part], sems.at[h, g]))
            pair[-1].start()
        arrivals.append(pair)
        lines = pl.ds(first * SUB, count * SUB)
        departures.append(
            pltpu.make_async_copy(flat.at[:, lines, :], out_ref.at[:, lines, :], sems.at[2, g])
        )
    line = lax.broadcasted_iota(jnp.int32, (PICKS, LANES), 0)
    lane = lax.broadcasted_iota(jnp.int32, (PICKS, LANES), 1)
    blocks = jnp.zeros((PICKS, LANES), jnp.int32)
    for i in range(LATS):
        blocks = jnp.where(line % LATS == i, slots_ref[i], blocks)
    wanted = blocks * ORDER_BLOCK + line // LATS + SUB * lax.axis_index("ch")
    hot = jnp.concatenate(
        [
            jnp.where(lane + n * LANES == wanted, 1.0, 0.0).astype(BF)
            for n in range(LMAX // LANES)
        ],
        axis=1,
    )
    for g, count in enumerate(PICK_GROUPS):
        for copy in arrivals[g]:
            copy.wait()
        first, size = firsts[g], count * SUB
        base = first * SUB * LATS
        limit = ORDER_LIMITS[1]
        for r in range(count):
            lead = lax.dot_general(
                hot[:, :limit], buf[first + r, :, :limit], NT, preferred_element_type=F32
            )
            rest = lax.dot_general(
                hot[:, limit:], buf[first + r, :LANES, limit:], NT, preferred_element_type=F32
            )
            for h, picked in enumerate((lead[:, :LANES] + rest, lead[:, LANES:])):
                for t in range(SUB):
                    wide[h, pl.ds(base + r * SUB + t, LATS, stride=size), :] = picked[
                        t * LATS : (t + 1) * LATS
                    ]
        for h in range(STEPS // LANES):
            lanes = slice(h * LANES, (h + 1) * LANES)
            flat[:, first * SUB : first * SUB + size, lanes] = (
                wide[h, base : base + LATS * size].reshape(LATS, size, LANES).astype(BF)
            )
        departures[g].start()
    for copy in departures:
        copy.wait()


def pick(block_slots, legendre):
    return pl.pallas_call(
        pick_kernel,
        out_shape=jax.ShapeDtypeStruct((LATS, ROWS * SUB, STEPS), BF),
        in_specs=[pl.BlockSpec(memory_space=pltpu.SMEM), pl.BlockSpec(memory_space=pltpu.HBM)],
        out_specs=pl.BlockSpec(memory_space=pltpu.HBM),
        scratch_shapes=[
            pltpu.VMEM((ROWS, STEPS, LMAX), BF),
            pltpu.VMEM((STEPS // LANES, LATS * ROWS * SUB + MARGIN, LANES), F32),
            pltpu.VMEM((LATS, ROWS * SUB, STEPS), BF),
            pltpu.SemaphoreType.DMA((3, len(PICK_GROUPS))),
        ],
        compiler_params=pltpu.CompilerParams(vmem_limit_bytes=GRANT),
        cost_estimate=pl.CostEstimate(flops=2 * 64 * 512 * 5120, bytes_accessed=6 << 20, transcendentals=0),
        name="pick",
    )(block_slots, legendre)


def order_kernel(leg_ref, *refs):
    pieces_in, (out_ref, raw, specs, full) = refs[:TURNS], refs[TURNS:]
    half = NLAT // 2
    ch_index = lax.axis_index("ch")
    side = lax.rem(ch_index, PAIR)
    for d in range(TURNS):
        turn = lax.rem(lax.div(ch_index, PAIR) + (TURNS - d), TURNS)
        for q in range(PAIR):
            source = turn * PAIR + (side if q == 0 else 1 - side)
            for h in range(STEPS // LANES):
                lanes = slice(h * LANES, (h + 1) * LANES)
                start = pl.multiple_of(source * C, C)
                specs[h, pl.ds(start, C), :] = pieces_in[d][q, :, lanes].astype(F32)
    for h in range(STEPS // LANES):
        lanes = slice(h * LANES, (h + 1) * LANES)
        lines = leg_ref[:, :, lanes].astype(F32).reshape(LATS * ROWS * SUB, LANES)
        raw[h, : LATS * ROWS * SUB, :] = lines
    rows = lax.broadcasted_iota(jnp.int32, (LANES, LANES), 0)
    cols = lax.broadcasted_iota(jnp.int32, (LANES, LANES), 1)
    turn = jnp.where(rows + cols == LANES - 1, 1.0, 0.0).astype(BF)
    stride = 4
    full[:16, :] = jnp.zeros((16, LANES), F32)
    full[SUB * NLAT :, :] = jnp.zeros((2 * EDGE, LANES), F32)
    for t in range(SUB):
        table = jnp.concatenate(
            [raw[h, pl.ds(t, NLAT, stride=SUB), :] for h in range(STEPS // LANES)], axis=1
        ).astype(BF)
        count = NLAT // LANES
        turned = jnp.concatenate(
            [
                jnp.dot(
                    turn,
                    table[(count - 1 - n) * LANES : (count - n) * LANES],
                    preferred_element_type=F32,
                ).astype(BF)
                for n in range(count)
            ],
            axis=0,
        )
        coeffs = []
        for p in range(2):
            pieces = []
            for x in range(2):
                for j in range(CHS):
                    start = j * C + t * 4 * OWN + p * 2 + x
                    pieces.append(
                        jnp.concatenate(
                            [
                                specs[h, pl.ds(start, OWN, stride=stride), :]
                                for h in range(STEPS // LANES)
                            ],
                            axis=1,
                        )
                    )
            coeffs.append(jnp.concatenate(pieces, axis=0).astype(BF))

        def dot(a, b):
            return lax.dot_general(a, b, NT, preferred_element_type=F32)

        north = dot(table[:half], coeffs[0]) - dot(turned[:half], coeffs[1])
        south = dot(table[half:], coeffs[1]) + dot(turned[half:], coeffs[0])
        full[pl.ds(EDGE + t, half, stride=SUB), :] = north
        full[pl.ds(EDGE + t + SUB * half, half, stride=SUB), :] = south
    for i in range(LATS):
        start = EDGE - REACH * SUB + i * ROWS * SUB
        out_ref[i] = full[start : start + HALO_ROWS * SUB, :].astype(BF)


def order_stage(leg, pieces):
    return pl.pallas_call(
        order_kernel,
        out_shape=jax.ShapeDtypeStruct((LATS, HALO_ROWS * SUB, LANES), BF),
        in_specs=[pl.BlockSpec(memory_space=VMEM)] * (1 + TURNS),
        out_specs=pl.BlockSpec(memory_space=VMEM),
        scratch_shapes=[
            pltpu.VMEM((STEPS // LANES, LATS * SUB * ROWS + MARGIN, LANES), F32),
            pltpu.VMEM((STEPS // LANES, CHS * C + MARGIN, LANES), F32),
            pltpu.VMEM((SUB * NLAT + 2 * EDGE, LANES), F32),
        ],
        compiler_params=pltpu.CompilerParams(vmem_limit_bytes=24 << 20),
        cost_estimate=pl.CostEstimate(flops=700 << 20, bytes_accessed=2 << 20, transcendentals=0),
        name="order_stage",
    )(leg, *pieces)


def coef_kernel(values_ref, near_ref, mix_ref, waves_ref, coef_ref, mixed_ref, taps):
    first = lax.axis_index("lat") * ROWS
    step = near_ref[...] - lax.broadcasted_iota(jnp.int32, (SLOTS, ROWS), 1) - (first - REACH)
    taps[...] = jnp.zeros_like(taps)
    for d in range(SPREAD):
        hit = jnp.where(step == d, 1.0, 0.0)
        for b in range(KER):
            for s in range(TAPS):
                value = values_ref[b, s].astype(F32)
                taps[b * SPREAD + d, s : s + 1, :] = jnp.sum(hit * value, axis=0, keepdims=True)
    waves = waves_ref[lax.axis_index("ch")]
    for n in range(KER * SPREAD):
        coef_ref[n] = lax.dot_general(
            taps[n], waves, TN, precision=lax.Precision.HIGHEST, preferred_element_type=F32
        )
    turned = jnp.concatenate([mix_ref[b].astype(F32).T for b in range(KER)], axis=0)
    mixed_ref[...] = jnp.concatenate([turned, turned], axis=1).astype(BF)


def coef_stage(kernel_values, near_rows, mix_weights):
    return pl.pallas_call(
        coef_kernel,
        out_shape=(
            jax.ShapeDtypeStruct((KER * SPREAD, ROWS, 2 * LANES), F32),
            jax.ShapeDtypeStruct((KER * C, 2 * C), BF),
        ),
        in_specs=[pl.BlockSpec(memory_space=VMEM)] * 4,
        out_specs=[pl.BlockSpec(memory_space=VMEM)] * 2,
        scratch_shapes=[pltpu.VMEM((KER * SPREAD, WAVE_ROWS, ROWS), F32)],
        compiler_params=pltpu.CompilerParams(vmem_limit_bytes=16 << 20),
        cost_estimate=pl.CostEstimate(flops=16 << 20, bytes_accessed=1 << 20, transcendentals=0),
        name="coef_stage",
    )(
        jnp.transpose(kernel_values, (0, 3, 2, 1)),
        jnp.transpose(near_rows, (1, 0)),
        mix_weights,
        jnp.asarray(wave_table()),
    )


def row_kernel(slots_ref, rows_ref, coef_ref, mix_ref, out_ref, field, mixed):
    for i in range(LATS):
        block = slots_ref[i]
        start = pl.multiple_of(block * (SUB * HALO_ROWS), 8)
        field[pl.ds(start, SUB * HALO_ROWS), :] = rows_ref[i].astype(F32)
    low = lax.broadcasted_iota(jnp.int32, (PICKS, LANES), 1) < C
    weights = mix_ref[...]
    for r in range(HALO_ROWS):
        one = jnp.concatenate(
            [
                field[pl.ds(r * SUB + t, BLOCKS, stride=SUB * HALO_ROWS), :]
                for t in range(SUB)
            ],
            axis=0,
        )
        real = jnp.where(low, one, 0.0)
        imag = jnp.where(low, 0.0, one)
        both = jnp.concatenate([real, imag, imag, real], axis=0).astype(BF)
        mixed[r] = lax.dot_general(weights, both, NT, preferred_element_type=F32)
    for r in range(ROWS):
        total = None
        for b in range(KER):
            for d in range(SPREAD):
                n = b * SPREAD + d
                part = mixed[r + d, b * C : (b + 1) * C, :]
                term = coef_ref[n, r : r + 1, :LANES] * part[:, :LANES]
                term = term + coef_ref[n, r : r + 1, LANES:] * part[:, LANES:]
                total = term if total is None else total + term
        out_ref[:, r * OWN : (r + 1) * OWN, :] = total.astype(BF).reshape(CHS, OWN, LANES)


def row_stage(block_slots, rows, coefs, mix):
    return pl.pallas_call(
        row_kernel,
        out_shape=jax.ShapeDtypeStruct((CHS, OWN * ROWS, LANES), BF),
        in_specs=[
            pl.BlockSpec(memory_space=pltpu.SMEM),
            pl.BlockSpec(memory_space=VMEM),
            pl.BlockSpec(memory_space=VMEM),
            pl.BlockSpec(memory_space=VMEM),
        ],
        out_specs=pl.BlockSpec(memory_space=VMEM),
        scratch_shapes=[
            pltpu.VMEM((BLOCKS * SUB * HALO_ROWS + MARGIN, LANES), F32),
            pltpu.VMEM((HALO_ROWS, KER * C, 2 * LANES), F32),
        ],
        compiler_params=pltpu.CompilerParams(vmem_limit_bytes=16 << 20),
        cost_estimate=pl.CostEstimate(flops=200 << 20, bytes_accessed=2 << 20, transcendentals=0),
        name="row_stage",
    )(block_slots, rows, coefs, mix)


LON_PARTS = 2


def longitude_kernel(rows_ref, table_ref, out_ref, whole, sems):
    rows = ROWS // LON_PARTS
    lines = rows * OWN
    departures = []
    for g in range(LON_PARTS):
        even = jnp.concatenate(
            [rows_ref[j, g * lines : (g + 1) * lines] for j in range(CHS)], axis=1
        )
        lane = lax.broadcasted_iota(jnp.int32, even.shape, 1)
        flipped = jnp.where(lane % PICKS < BLOCKS, even.astype(F32), -even.astype(F32)).astype(BF)
        both = jnp.concatenate([even, flipped], axis=0)
        field = jnp.dot(both, table_ref[...], preferred_element_type=F32)
        part = pl.ds(g * rows, rows)
        halves = jnp.concatenate([field[:lines], field[lines:]], axis=1)
        whole[part] = halves.astype(BF).reshape(rows, OWN, NLON)
        departures.append(pltpu.make_async_copy(whole.at[part], out_ref.at[part], sems.at[g]))
        departures[-1].start()
    for copy in departures:
        copy.wait()


def longitude_stage(rows, table):
    return pl.pallas_call(
        longitude_kernel,
        out_shape=jax.ShapeDtypeStruct((ROWS, OWN, NLON), BF),
        in_specs=[pl.BlockSpec(memory_space=VMEM)] * 2,
        out_specs=pl.BlockSpec(memory_space=pltpu.HBM),
        scratch_shapes=[
            pltpu.VMEM((ROWS, OWN, NLON), BF),
            pltpu.SemaphoreType.DMA((LON_PARTS,)),
        ],
        compiler_params=pltpu.CompilerParams(vmem_limit_bytes=40 << 20),
        cost_estimate=pl.CostEstimate(flops=480 << 20, bytes_accessed=4 << 20, transcendentals=0),
        name="longitude_stage",
    )(rows, table)


def per_device(spectrum, legendre, block_slots, kernel_values, near_rows, mix_weights):
    ch_index = lax.axis_index("ch")
    picked = pick(block_slots, legendre)
    picked, spectrum = lax.optimization_barrier((picked, spectrum))
    leg = lax.all_to_all(picked, "lat", 0, 0, tiled=True)
    blocks = spectrum.reshape(TURNS, PAIR, C, STEPS)
    turn, side = ch_index // PAIR, ch_index % PAIR
    kept = lax.dynamic_index_in_dim(blocks, side, 1, keepdims=False)
    given = lax.dynamic_index_in_dim(blocks, 1 - side, 1, keepdims=False)
    taken = lax.ppermute(given, "ch", [(j, j ^ 1) for j in range(CHS)])
    both = jnp.stack([kept, taken], axis=1)
    pieces = []
    for d in range(TURNS):
        piece = lax.dynamic_index_in_dim(both, (turn + d) % TURNS, 0, keepdims=False)
        shift = [(j, (j + PAIR * d) % CHS) for j in range(CHS)]
        pieces.append(lax.ppermute(piece, "ch", shift) if d else piece)
    by_order = order_stage(leg, pieces)
    by_order, kernel_values, near_rows, mix_weights = lax.optimization_barrier(
        (by_order, kernel_values, near_rows, mix_weights)
    )
    by_row = lax.all_to_all(by_order, "lat", 0, 0, tiled=True)
    coefs, mix = coef_stage(kernel_values, near_rows, mix_weights)
    mixed = row_stage(block_slots, by_row, coefs, mix)
    own = lax.all_to_all(mixed, "ch", 0, 0, tiled=True)
    field = longitude_stage(own, jnp.asarray(longitude_table()))
    return jnp.transpose(field, (1, 0, 2))


def solution(mesh):
    return jax.shard_map(
        per_device,
        mesh=mesh,
        in_specs=(
            P("lat", "ch", None, None, None),
            P("lat", None, None),
            P(),
            P(None, "lat", None, None),
            P("lat", None),
            P(),
        ),
        out_specs=P("ch", "lat", None),
        check_vma=False,
    )
```

```python
import math

import jax
import jax.numpy as jnp
import ml_dtypes
import numpy as np
from jax import lax
from jax.experimental import pallas as pl
from jax.experimental.pallas import tpu as pltpu
from jax.sharding import PartitionSpec as P

NLAT = 640
NLON = 1440
LMAX = 512
C = 64
ORDER_BLOCK = 16
KER = 3
SLOTS = 6
REACH = 2
LON_REACH = 4
TAPS = 9
STEPS = 256
BLOCKS = 32
LATS = 32
CHS = 8
ROWS = NLAT // LATS
OWN = C // CHS
SUB = ORDER_BLOCK // CHS
HALO_ROWS = ROWS + 2 * REACH
SPREAD = 2 * REACH + 1
PICKS = LATS * SUB
LANES = 128
BF = jnp.bfloat16
F32 = jnp.float32
NT = (((1,), (1,)), ((), ()))
TN = (((0,), (0,)), ((), ()))
VMEM = pltpu.VMEM
GRANT = 62 << 20
MARGIN = 48
PAIR = 2
TURNS = CHS // PAIR


HALF_LON = NLON // 2
WAVE_ROWS = 16


def order_table():
    orders = (
        ORDER_BLOCK * np.arange(BLOCKS)[None, None, :]
        + SUB * np.arange(CHS)[:, None, None]
        + np.arange(SUB)[None, :, None]
    )
    return orders.reshape(CHS, 1, PICKS, 1)


def longitude_table():
    orders = order_table()
    phases = (orders * np.arange(HALF_LON)) % NLON
    angles = phases * (2.0 * math.pi / NLON)
    weight = np.where(orders == 0, 1.0, 2.0)
    table = np.concatenate([weight * np.cos(angles), -weight * np.sin(angles)], axis=1)
    return table.reshape(CHS * LANES, HALF_LON).astype(ml_dtypes.bfloat16)


def wave_table():
    shifts = np.arange(TAPS)[:, None] - LON_REACH
    orders = order_table().reshape(CHS, 1, PICKS)
    angles = ((orders * shifts) % NLON) * (2.0 * math.pi / NLON)
    waves = np.zeros((CHS, WAVE_ROWS, 2 * LANES), np.float32)
    cosine, sine = np.cos(angles), np.sin(angles)
    waves[:, :TAPS] = np.concatenate([cosine, cosine, -sine, sine], axis=2)
    return waves


PICK_GROUPS = (4, 4, 8, 4)
EDGE = 12
ORDER_LIMITS = (LMAX, LMAX - 2 * LANES)


def pick_kernel(slots_ref, leg_ref, out_ref, buf, wide, flat, sems):
    arrivals, departures, firsts = [], [], []
    for g, count in enumerate(PICK_GROUPS):
        first = sum(PICK_GROUPS[:g])
        firsts.append(first)
        pair = []
        for h in range(STEPS // LANES):
            part = (pl.ds(first, count), pl.ds(h * LANES, LANES), pl.ds(0, ORDER_LIMITS[h]))
            pair.append(pltpu.make_async_copy(leg_ref.at[part], buf.at[part], sems.at[h, g]))
            pair[-1].start()
        arrivals.append(pair)
        lines = pl.ds(first * SUB, count * SUB)
        departures.append(
            pltpu.make_async_copy(flat.at[:, lines, :], out_ref.at[:, lines, :], sems.at[2, g])
        )
    line = lax.broadcasted_iota(jnp.int32, (PICKS, LANES), 0)
    lane = lax.broadcasted_iota(jnp.int32, (PICKS, LANES), 1)
    blocks = jnp.zeros((PICKS, LANES), jnp.int32)
    for i in range(LATS):
        blocks = jnp.where(line % LATS == i, slots_ref[i], blocks)
    wanted = blocks * ORDER_BLOCK + line // LATS + SUB * lax.axis_index("ch")
    hot = jnp.concatenate(
        [
            jnp.where(lane + n * LANES == wanted, 1.0, 0.0).astype(BF)
            for n in range(LMAX // LANES)
        ],
        axis=1,
    )
    for g, count in enumerate(PICK_GROUPS):
        for copy in arrivals[g]:
            copy.wait()
        first, size = firsts[g], count * SUB
        base = first * SUB * LATS
        limit = ORDER_LIMITS[1]
        for r in range(count):
            lead = lax.dot_general(
                hot[:, :limit], buf[first + r, :, :limit], NT, preferred_element_type=F32
            )
            rest = lax.dot_general(
                hot[:, limit:], buf[first + r, :LANES, limit:], NT, preferred_element_type=F32
            )
            for h, picked in enumerate((lead[:, :LANES] + rest, lead[:, LANES:])):
                for t in range(SUB):
                    wide[h, pl.ds(base + r * SUB + t, LATS, stride=size), :] = picked[
                        t * LATS : (t + 1) * LATS
                    ]
        for h in range(STEPS // LANES):
            lanes = slice(h * LANES, (h + 1) * LANES)
            flat[:, first * SUB : first * SUB + size, lanes] = (
                wide[h, base : base + LATS * size].reshape(LATS, size, LANES).astype(BF)
            )
        departures[g].start()
    for copy in departures:
        copy.wait()


def pick(block_slots, legendre):
    return pl.pallas_call(
        pick_kernel,
        out_shape=jax.ShapeDtypeStruct((LATS, ROWS * SUB, STEPS), BF),
        in_specs=[pl.BlockSpec(memory_space=pltpu.SMEM), pl.BlockSpec(memory_space=pltpu.HBM)],
        out_specs=pl.BlockSpec(memory_space=pltpu.HBM),
        scratch_shapes=[
            pltpu.VMEM((ROWS, STEPS, LMAX), BF),
            pltpu.VMEM((STEPS // LANES, LATS * ROWS * SUB + MARGIN, LANES), F32),
            pltpu.VMEM((LATS, ROWS * SUB, STEPS), BF),
            pltpu.SemaphoreType.DMA((3, len(PICK_GROUPS))),
        ],
        compiler_params=pltpu.CompilerParams(vmem_limit_bytes=GRANT),
        cost_estimate=pl.CostEstimate(flops=2 * 64 * 512 * 5120, bytes_accessed=6 << 20, transcendentals=0),
        name="pick",
    )(block_slots, legendre)


def order_kernel(leg_ref, *refs):
    pieces_in, (out_ref, raw, specs, full) = refs[:PAIR], refs[PAIR:]
    half = NLAT // 2
    ch_index = lax.axis_index("ch")
    side = lax.rem(ch_index, PAIR)
    for d in range(TURNS):
        turn = lax.rem(lax.div(ch_index, PAIR) + (TURNS - d), TURNS)
        for q in range(PAIR):
            source = turn * PAIR + (side if q == 0 else 1 - side)
            for h in range(STEPS // LANES):
                lanes = slice(h * LANES, (h + 1) * LANES)
                start = pl.multiple_of(source * C, C)
                specs[h, pl.ds(start, C), :] = pieces_in[q][d, :, lanes].astype(F32)
    for h in range(STEPS // LANES):
        lanes = slice(h * LANES, (h + 1) * LANES)
        lines = leg_ref[:, :, lanes].astype(F32).reshape(LATS * ROWS * SUB, LANES)
        raw[h, : LATS * ROWS * SUB, :] = lines
    rows = lax.broadcasted_iota(jnp.int32, (LANES, LANES), 0)
    cols = lax.broadcasted_iota(jnp.int32, (LANES, LANES), 1)
    turn = jnp.where(rows + cols == LANES - 1, 1.0, 0.0).astype(BF)
    stride = 4
    full[:16, :] = jnp.zeros((16, LANES), F32)
    full[SUB * NLAT :, :] = jnp.zeros((2 * EDGE, LANES), F32)
    for t in range(SUB):
        table = jnp.concatenate(
            [raw[h, pl.ds(t, NLAT, stride=SUB), :] for h in range(STEPS // LANES)], axis=1
        ).astype(BF)
        count = NLAT // LANES
        turned = jnp.concatenate(
            [
                jnp.dot(
                    turn,
                    table[(count - 1 - n) * LANES : (count - n) * LANES],
                    preferred_element_type=F32,
                ).astype(BF)
                for n in range(count)
            ],
            axis=0,
        )
        coeffs = []
        for p in range(2):
            pieces = []
            for x in range(2):
                for j in range(CHS):
                    start = j * C + t * 4 * OWN + p * 2 + x
                    pieces.append(
                        jnp.concatenate(
                            [
                                specs[h, pl.ds(start, OWN, stride=stride), :]
                                for h in range(STEPS // LANES)
                            ],
                            axis=1,
                        )
                    )
            coeffs.append(jnp.concatenate(pieces, axis=0).astype(BF))

        def dot(a, b):
            return lax.dot_general(a, b, NT, preferred_element_type=F32)

        north = dot(table[:half], coeffs[0]) - dot(turned[:half], coeffs[1])
        south = dot(table[half:], coeffs[1]) + dot(turned[half:], coeffs[0])
        full[pl.ds(EDGE + t, half, stride=SUB), :] = north
        full[pl.ds(EDGE + t + SUB * half, half, stride=SUB), :] = south
    for i in range(LATS):
        start = EDGE - REACH * SUB + i * ROWS * SUB
        out_ref[i] = full[start : start + HALO_ROWS * SUB, :].astype(BF)


def order_stage(leg, pieces):
    return pl.pallas_call(
        order_kernel,
        out_shape=jax.ShapeDtypeStruct((LATS, HALO_ROWS * SUB, LANES), BF),
        in_specs=[pl.BlockSpec(memory_space=VMEM)] * (1 + PAIR),
        out_specs=pl.BlockSpec(memory_space=VMEM),
        scratch_shapes=[
            pltpu.VMEM((STEPS // LANES, LATS * SUB * ROWS + MARGIN, LANES), F32),
            pltpu.VMEM((STEPS // LANES, CHS * C + MARGIN, LANES), F32),
            pltpu.VMEM((SUB * NLAT + 2 * EDGE, LANES), F32),
        ],
        compiler_params=pltpu.CompilerParams(vmem_limit_bytes=24 << 20),
        cost_estimate=pl.CostEstimate(flops=700 << 20, bytes_accessed=2 << 20, transcendentals=0),
        name="order_stage",
    )(leg, *pieces)


def coef_kernel(values_ref, near_ref, mix_ref, waves_ref, coef_ref, mixed_ref, taps):
    first = lax.axis_index("lat") * ROWS
    step = near_ref[...] - lax.broadcasted_iota(jnp.int32, (SLOTS, ROWS), 1) - (first - REACH)
    taps[...] = jnp.zeros_like(taps)
    for d in range(SPREAD):
        hit = jnp.where(step == d, 1.0, 0.0)
        for b in range(KER):
            for s in range(TAPS):
                value = values_ref[b, s].astype(F32)
                taps[b * SPREAD + d, s : s + 1, :] = jnp.sum(hit * value, axis=0, keepdims=True)
    waves = waves_ref[lax.axis_index("ch")]
    for n in range(KER * SPREAD):
        coef_ref[n] = lax.dot_general(
            taps[n], waves, TN, precision=lax.Precision.HIGHEST, preferred_element_type=F32
        )
    turned = jnp.concatenate([mix_ref[b].astype(F32).T for b in range(KER)], axis=0)
    mixed_ref[...] = jnp.concatenate([turned, turned], axis=1).astype(BF)


def coef_stage(kernel_values, near_rows, mix_weights):
    return pl.pallas_call(
        coef_kernel,
        out_shape=(
            jax.ShapeDtypeStruct((KER * SPREAD, ROWS, 2 * LANES), F32),
            jax.ShapeDtypeStruct((KER * C, 2 * C), BF),
        ),
        in_specs=[pl.BlockSpec(memory_space=VMEM)] * 4,
        out_specs=[pl.BlockSpec(memory_space=VMEM)] * 2,
        scratch_shapes=[pltpu.VMEM((KER * SPREAD, WAVE_ROWS, ROWS), F32)],
        compiler_params=pltpu.CompilerParams(vmem_limit_bytes=16 << 20),
        cost_estimate=pl.CostEstimate(flops=16 << 20, bytes_accessed=1 << 20, transcendentals=0),
        name="coef_stage",
    )(
        jnp.transpose(kernel_values, (0, 3, 2, 1)),
        jnp.transpose(near_rows, (1, 0)),
        mix_weights,
        jnp.asarray(wave_table()),
    )


def row_kernel(slots_ref, rows_ref, coef_ref, mix_ref, out_ref, field, mixed):
    for i in range(LATS):
        block = slots_ref[i]
        start = pl.multiple_of(block * (SUB * HALO_ROWS), 8)
        field[pl.ds(start, SUB * HALO_ROWS), :] = rows_ref[i].astype(F32)
    low = lax.broadcasted_iota(jnp.int32, (PICKS, LANES), 1) < C
    weights = mix_ref[...]
    for r in range(HALO_ROWS):
        one = jnp.concatenate(
            [
                field[pl.ds(r * SUB + t, BLOCKS, stride=SUB * HALO_ROWS), :]
                for t in range(SUB)
            ],
            axis=0,
        )
        real = jnp.where(low, one, 0.0)
        imag = jnp.where(low, 0.0, one)
        both = jnp.concatenate([real, imag, imag, real], axis=0).astype(BF)
        mixed[r] = lax.dot_general(weights, both, NT, preferred_element_type=F32)
    for r in range(ROWS):
        total = None
        for b in range(KER):
            for d in range(SPREAD):
                n = b * SPREAD + d
                part = mixed[r + d, b * C : (b + 1) * C, :]
                term = coef_ref[n, r : r + 1, :LANES] * part[:, :LANES]
                term = term + coef_ref[n, r : r + 1, LANES:] * part[:, LANES:]
                total = term if total is None else total + term
        out_ref[:, r * OWN : (r + 1) * OWN, :] = total.astype(BF).reshape(CHS, OWN, LANES)


def row_stage(block_slots, rows, coefs, mix):
    return pl.pallas_call(
        row_kernel,
        out_shape=jax.ShapeDtypeStruct((CHS, OWN * ROWS, LANES), BF),
        in_specs=[
            pl.BlockSpec(memory_space=pltpu.SMEM),
            pl.BlockSpec(memory_space=VMEM),
            pl.BlockSpec(memory_space=VMEM),
            pl.BlockSpec(memory_space=VMEM),
        ],
        out_specs=pl.BlockSpec(memory_space=VMEM),
        scratch_shapes=[
            pltpu.VMEM((BLOCKS * SUB * HALO_ROWS + MARGIN, LANES), F32),
            pltpu.VMEM((HALO_ROWS, KER * C, 2 * LANES), F32),
        ],
        compiler_params=pltpu.CompilerParams(vmem_limit_bytes=16 << 20),
        cost_estimate=pl.CostEstimate(flops=200 << 20, bytes_accessed=2 << 20, transcendentals=0),
        name="row_stage",
    )(block_slots, rows, coefs, mix)


LON_PARTS = 2


def longitude_kernel(rows_ref, table_ref, out_ref, whole, sems):
    rows = ROWS // LON_PARTS
    lines = rows * OWN
    departures = []
    for g in range(LON_PARTS):
        even = jnp.concatenate(
            [rows_ref[j, g * lines : (g + 1) * lines] for j in range(CHS)], axis=1
        )
        lane = lax.broadcasted_iota(jnp.int32, even.shape, 1)
        flipped = jnp.where(lane % PICKS < BLOCKS, even.astype(F32), -even.astype(F32)).astype(BF)
        both = jnp.concatenate([even, flipped], axis=0)
        field = jnp.dot(both, table_ref[...], preferred_element_type=F32)
        part = pl.ds(g * rows, rows)
        halves = jnp.concatenate([field[:lines], field[lines:]], axis=1)
        whole[part] = halves.astype(BF).reshape(rows, OWN, NLON)
        departures.append(pltpu.make_async_copy(whole.at[part], out_ref.at[part], sems.at[g]))
        departures[-1].start()
    for copy in departures:
        copy.wait()


def longitude_stage(rows, table):
    return pl.pallas_call(
        longitude_kernel,
        out_shape=jax.ShapeDtypeStruct((ROWS, OWN, NLON), BF),
        in_specs=[pl.BlockSpec(memory_space=VMEM)] * 2,
        out_specs=pl.BlockSpec(memory_space=pltpu.HBM),
        scratch_shapes=[
            pltpu.VMEM((ROWS, OWN, NLON), BF),
            pltpu.SemaphoreType.DMA((LON_PARTS,)),
        ],
        compiler_params=pltpu.CompilerParams(vmem_limit_bytes=40 << 20),
        cost_estimate=pl.CostEstimate(flops=480 << 20, bytes_accessed=4 << 20, transcendentals=0),
        name="longitude_stage",
    )(rows, table)


def per_device(spectrum, legendre, block_slots, kernel_values, near_rows, mix_weights):
    ch_index = lax.axis_index("ch")
    picked = pick(block_slots, legendre)
    picked, spectrum = lax.optimization_barrier((picked, spectrum))
    leg = lax.all_to_all(picked, "lat", 0, 0, tiled=True)
    blocks = spectrum.reshape(TURNS, PAIR, C, STEPS)
    turn, side = ch_index // PAIR, ch_index % PAIR
    pieces = []
    for d in range(TURNS):
        piece = lax.dynamic_index_in_dim(blocks, (turn + d) % TURNS, 0, keepdims=False)
        shift = [(j, (j + PAIR * d) % CHS) for j in range(CHS)]
        pieces.append(lax.ppermute(piece, "ch", shift) if d else piece)
    both = jnp.stack(pieces, axis=0)
    kept = lax.dynamic_index_in_dim(both, side, 1, keepdims=False)
    given = lax.dynamic_index_in_dim(both, 1 - side, 1, keepdims=False)
    taken = lax.ppermute(given, "ch", [(j, j ^ 1) for j in range(CHS)])
    pieces = [kept, taken]
    by_order = order_stage(leg, pieces)
    by_order, kernel_values, near_rows, mix_weights = lax.optimization_barrier(
        (by_order, kernel_values, near_rows, mix_weights)
    )
    by_row = lax.all_to_all(by_order, "lat", 0, 0, tiled=True)
    coefs, mix = coef_stage(kernel_values, near_rows, mix_weights)
    mixed = row_stage(block_slots, by_row, coefs, mix)
    own = lax.all_to_all(mixed, "ch", 0, 0, tiled=True)
    field = longitude_stage(own, jnp.asarray(longitude_table()))
    return jnp.transpose(field, (1, 0, 2))


def solution(mesh):
    return jax.shard_map(
        per_device,
        mesh=mesh,
        in_specs=(
            P("lat", "ch", None, None, None),
            P("lat", None, None),
            P(),
            P(None, "lat", None, None),
            P("lat", None),
            P(),
        ),
        out_specs=P("ch", "lat", None),
        check_vma=False,
    )
```

```python
import math

import jax
import jax.numpy as jnp
import ml_dtypes
import numpy as np
from jax import lax
from jax.experimental import pallas as pl
from jax.experimental.pallas import tpu as pltpu
from jax.sharding import PartitionSpec as P

NLAT = 640
NLON = 1440
LMAX = 512
C = 64
ORDER_BLOCK = 16
KER = 3
SLOTS = 6
REACH = 2
LON_REACH = 4
TAPS = 9
STEPS = 256
BLOCKS = 32
LATS = 32
CHS = 8
ROWS = NLAT // LATS
OWN = C // CHS
SUB = ORDER_BLOCK // CHS
HALO_ROWS = ROWS + 2 * REACH
SPREAD = 2 * REACH + 1
PICKS = LATS * SUB
LANES = 128
BF = jnp.bfloat16
F32 = jnp.float32
NT = (((1,), (1,)), ((), ()))
TN = (((0,), (0,)), ((), ()))
VMEM = pltpu.VMEM
GRANT = 62 << 20
MARGIN = 48
PAIR = 2
TURNS = CHS // PAIR


HALF_LON = NLON // 2
WAVE_ROWS = 16


def order_table():
    orders = (
        ORDER_BLOCK * np.arange(BLOCKS)[None, None, :]
        + SUB * np.arange(CHS)[:, None, None]
        + np.arange(SUB)[None, :, None]
    )
    return orders.reshape(CHS, 1, PICKS, 1)


def longitude_table():
    orders = order_table()
    phases = (orders * np.arange(HALF_LON)) % NLON
    angles = phases * (2.0 * math.pi / NLON)
    weight = np.where(orders == 0, 1.0, 2.0)
    table = np.concatenate([weight * np.cos(angles), -weight * np.sin(angles)], axis=1)
    return table.reshape(CHS * LANES, HALF_LON).astype(ml_dtypes.bfloat16)


def wave_table():
    shifts = np.arange(TAPS)[:, None] - LON_REACH
    orders = order_table().reshape(CHS, 1, PICKS)
    angles = ((orders * shifts) % NLON) * (2.0 * math.pi / NLON)
    waves = np.zeros((CHS, WAVE_ROWS, 2 * LANES), np.float32)
    cosine, sine = np.cos(angles), np.sin(angles)
    waves[:, :TAPS] = np.concatenate([cosine, cosine, -sine, sine], axis=2)
    return waves


PICK_GROUPS = (4, 4, 8, 4)
EDGE = 12
ORDER_LIMITS = (LMAX, LMAX - 2 * LANES)


def pick_kernel(slots_ref, leg_ref, out_ref, buf, wide, flat, sems):
    arrivals, departures, firsts = [], [], []
    for g, count in enumerate(PICK_GROUPS):
        first = sum(PICK_GROUPS[:g])
        firsts.append(first)
        pair = []
        for h in range(STEPS // LANES):
            part = (pl.ds(first, count), pl.ds(h * LANES, LANES), pl.ds(0, ORDER_LIMITS[h]))
            pair.append(pltpu.make_async_copy(leg_ref.at[part], buf.at[part], sems.at[h, g]))
            pair[-1].start()
        arrivals.append(pair)
        lines = pl.ds(first * SUB, count * SUB)
        departures.append(
            pltpu.make_async_copy(flat.at[:, lines, :], out_ref.at[:, lines, :], sems.at[2, g])
        )
    line = lax.broadcasted_iota(jnp.int32, (PICKS, LANES), 0)
    lane = lax.broadcasted_iota(jnp.int32, (PICKS, LANES), 1)
    blocks = jnp.zeros((PICKS, LANES), jnp.int32)
    for i in range(LATS):
        blocks = jnp.where(line % LATS == i, slots_ref[i], blocks)
    wanted = blocks * ORDER_BLOCK + line // LATS + SUB * lax.axis_index("ch")
    hot = jnp.concatenate(
        [
            jnp.where(lane + n * LANES == wanted, 1.0, 0.0).astype(BF)
            for n in range(LMAX // LANES)
        ],
        axis=1,
    )
    for g, count in enumerate(PICK_GROUPS):
        for copy in arrivals[g]:
            copy.wait()
        first, size = firsts[g], count * SUB
        base = first * SUB * LATS
        limit = ORDER_LIMITS[1]
        for r in range(count):
            lead = lax.dot_general(
                hot[:, :limit], buf[first + r, :, :limit], NT, preferred_element_type=F32
            )
            rest = lax.dot_general(
                hot[:, limit:], buf[first + r, :LANES, limit:], NT, preferred_element_type=F32
            )
            for h, picked in enumerate((lead[:, :LANES] + rest, lead[:, LANES:])):
                for t in range(SUB):
                    wide[h, pl.ds(base + r * SUB + t, LATS, stride=size), :] = picked[
                        t * LATS : (t + 1) * LATS
                    ]
        for h in range(STEPS // LANES):
            lanes = slice(h * LANES, (h + 1) * LANES)
            flat[:, first * SUB : first * SUB + size, lanes] = (
                wide[h, base : base + LATS * size].reshape(LATS, size, LANES).astype(BF)
            )
        departures[g].start()
    for copy in departures:
        copy.wait()


def pick(block_slots, legendre):
    return pl.pallas_call(
        pick_kernel,
        out_shape=jax.ShapeDtypeStruct((LATS, ROWS * SUB, STEPS), BF),
        in_specs=[pl.BlockSpec(memory_space=pltpu.SMEM), pl.BlockSpec(memory_space=pltpu.HBM)],
        out_specs=pl.BlockSpec(memory_space=pltpu.HBM),
        scratch_shapes=[
            pltpu.VMEM((ROWS, STEPS, LMAX), BF),
            pltpu.VMEM((STEPS // LANES, LATS * ROWS * SUB + MARGIN, LANES), F32),
            pltpu.VMEM((LATS, ROWS * SUB, STEPS), BF),
            pltpu.SemaphoreType.DMA((3, len(PICK_GROUPS))),
        ],
        compiler_params=pltpu.CompilerParams(vmem_limit_bytes=GRANT),
        cost_estimate=pl.CostEstimate(flops=2 * 64 * 512 * 5120, bytes_accessed=6 << 20, transcendentals=0),
        name="pick",
    )(block_slots, legendre)


def spec_kernel(*refs):
    pieces_in, (out_ref, specs) = refs[:PAIR], refs[PAIR:]
    ch_index = lax.axis_index("ch")
    side = lax.rem(ch_index, PAIR)
    for d in range(TURNS):
        turn = lax.rem(lax.div(ch_index, PAIR) + (TURNS - d), TURNS)
        for q in range(PAIR):
            source = turn * PAIR + (side if q == 0 else 1 - side)
            for h in range(STEPS // LANES):
                lanes = slice(h * LANES, (h + 1) * LANES)
                start = pl.multiple_of(source * C, C)
                specs[h, pl.ds(start, C), :] = pieces_in[q][d, :, lanes].astype(F32)
    for t in range(SUB):
        for p in range(2):
            pieces = []
            for x in range(2):
                for j in range(CHS):
                    start = j * C + t * 4 * OWN + p * 2 + x
                    pieces.append(
                        jnp.concatenate(
                            [
                                specs[h, pl.ds(start, OWN, stride=4), :]
                                for h in range(STEPS // LANES)
                            ],
                            axis=1,
                        )
                    )
            out_ref[t, p] = jnp.concatenate(pieces, axis=0).astype(BF)


def spec_stage(pieces):
    return pl.pallas_call(
        spec_kernel,
        out_shape=jax.ShapeDtypeStruct((SUB, 2, LANES, STEPS), BF),
        in_specs=[pl.BlockSpec(memory_space=VMEM)] * PAIR,
        out_specs=pl.BlockSpec(memory_space=VMEM),
        scratch_shapes=[pltpu.VMEM((STEPS // LANES, CHS * C + MARGIN, LANES), F32)],
        compiler_params=pltpu.CompilerParams(vmem_limit_bytes=8 << 20),
        cost_estimate=pl.CostEstimate(flops=1 << 20, bytes_accessed=1 << 19, transcendentals=0),
        name="spec_stage",
    )(*pieces)


def order_kernel(leg_ref, spec_ref, out_ref, raw, full):
    half = NLAT // 2
    for h in range(STEPS // LANES):
        lanes = slice(h * LANES, (h + 1) * LANES)
        lines = leg_ref[:, :, lanes].astype(F32).reshape(LATS * ROWS * SUB, LANES)
        raw[h, : LATS * ROWS * SUB, :] = lines
    rows = lax.broadcasted_iota(jnp.int32, (LANES, LANES), 0)
    cols = lax.broadcasted_iota(jnp.int32, (LANES, LANES), 1)
    turn = jnp.where(rows + cols == LANES - 1, 1.0, 0.0).astype(BF)
    full[:16, :] = jnp.zeros((16, LANES), F32)
    full[SUB * NLAT :, :] = jnp.zeros((2 * EDGE, LANES), F32)
    for t in range(SUB):
        table = jnp.concatenate(
            [raw[h, pl.ds(t, NLAT, stride=SUB), :] for h in range(STEPS // LANES)], axis=1
        ).astype(BF)
        count = NLAT // LANES
        turned = jnp.concatenate(
            [
                jnp.dot(
                    turn,
                    table[(count - 1 - n) * LANES : (count - n) * LANES],
                    preferred_element_type=F32,
                ).astype(BF)
                for n in range(count)
            ],
            axis=0,
        )
        coeffs = [spec_ref[t, p] for p in range(2)]

        def dot(a, b):
            return lax.dot_general(a, b, NT, preferred_element_type=F32)

        north = dot(table[:half], coeffs[0]) - dot(turned[:half], coeffs[1])
        south = dot(table[half:], coeffs[1]) + dot(turned[half:], coeffs[0])
        full[pl.ds(EDGE + t, half, stride=SUB), :] = north
        full[pl.ds(EDGE + t + SUB * half, half, stride=SUB), :] = south
    for i in range(LATS):
        start = EDGE - REACH * SUB + i * ROWS * SUB
        out_ref[i] = full[start : start + HALO_ROWS * SUB, :].astype(BF)


def order_stage(leg, spec):
    return pl.pallas_call(
        order_kernel,
        out_shape=jax.ShapeDtypeStruct((LATS, HALO_ROWS * SUB, LANES), BF),
        in_specs=[pl.BlockSpec(memory_space=VMEM)] * 2,
        out_specs=pl.BlockSpec(memory_space=VMEM),
        scratch_shapes=[
            pltpu.VMEM((STEPS // LANES, LATS * SUB * ROWS + MARGIN, LANES), F32),
            pltpu.VMEM((SUB * NLAT + 2 * EDGE, LANES), F32),
        ],
        compiler_params=pltpu.CompilerParams(vmem_limit_bytes=24 << 20),
        cost_estimate=pl.CostEstimate(flops=700 << 20, bytes_accessed=2 << 20, transcendentals=0),
        name="order_stage",
    )(leg, spec)


def coef_kernel(values_ref, near_ref, mix_ref, waves_ref, coef_ref, mixed_ref, taps):
    first = lax.axis_index("lat") * ROWS
    step = near_ref[...] - lax.broadcasted_iota(jnp.int32, (SLOTS, ROWS), 1) - (first - REACH)
    taps[...] = jnp.zeros_like(taps)
    for d in range(SPREAD):
        hit = jnp.where(step == d, 1.0, 0.0)
        for b in range(KER):
            for s in range(TAPS):
                value = values_ref[b, s].astype(F32)
                taps[b * SPREAD + d, s : s + 1, :] = jnp.sum(hit * value, axis=0, keepdims=True)
    waves = waves_ref[lax.axis_index("ch")]
    for n in range(KER * SPREAD):
        coef_ref[n] = lax.dot_general(
            taps[n], waves, TN, precision=lax.Precision.HIGHEST, preferred_element_type=F32
        )
    turned = jnp.concatenate([mix_ref[b].astype(F32).T for b in range(KER)], axis=0)
    mixed_ref[...] = jnp.concatenate([turned, turned], axis=1).astype(BF)


def coef_stage(kernel_values, near_rows, mix_weights):
    return pl.pallas_call(
        coef_kernel,
        out_shape=(
            jax.ShapeDtypeStruct((KER * SPREAD, ROWS, 2 * LANES), F32),
            jax.ShapeDtypeStruct((KER * C, 2 * C), BF),
        ),
        in_specs=[pl.BlockSpec(memory_space=VMEM)] * 4,
        out_specs=[pl.BlockSpec(memory_space=VMEM)] * 2,
        scratch_shapes=[pltpu.VMEM((KER * SPREAD, WAVE_ROWS, ROWS), F32)],
        compiler_params=pltpu.CompilerParams(vmem_limit_bytes=16 << 20),
        cost_estimate=pl.CostEstimate(flops=16 << 20, bytes_accessed=1 << 20, transcendentals=0),
        name="coef_stage",
    )(
        jnp.transpose(kernel_values, (0, 3, 2, 1)),
        jnp.transpose(near_rows, (1, 0)),
        mix_weights,
        jnp.asarray(wave_table()),
    )


def row_kernel(slots_ref, rows_ref, coef_ref, mix_ref, out_ref, field, mixed):
    for i in range(LATS):
        block = slots_ref[i]
        start = pl.multiple_of(block * (SUB * HALO_ROWS), 8)
        field[pl.ds(start, SUB * HALO_ROWS), :] = rows_ref[i].astype(F32)
    low = lax.broadcasted_iota(jnp.int32, (PICKS, LANES), 1) < C
    weights = mix_ref[...]
    for r in range(HALO_ROWS):
        one = jnp.concatenate(
            [
                field[pl.ds(r * SUB + t, BLOCKS, stride=SUB * HALO_ROWS), :]
                for t in range(SUB)
            ],
            axis=0,
        )
        real = jnp.where(low, one, 0.0)
        imag = jnp.where(low, 0.0, one)
        both = jnp.concatenate([real, imag, imag, real], axis=0).astype(BF)
        mixed[r] = lax.dot_general(weights, both, NT, preferred_element_type=F32)
    for r in range(ROWS):
        total = None
        for b in range(KER):
            for d in range(SPREAD):
                n = b * SPREAD + d
                part = mixed[r + d, b * C : (b + 1) * C, :]
                term = coef_ref[n, r : r + 1, :LANES] * part[:, :LANES]
                term = term + coef_ref[n, r : r + 1, LANES:] * part[:, LANES:]
                total = term if total is None else total + term
        out_ref[:, r * OWN : (r + 1) * OWN, :] = total.astype(BF).reshape(CHS, OWN, LANES)


def row_stage(block_slots, rows, coefs, mix):
    return pl.pallas_call(
        row_kernel,
        out_shape=jax.ShapeDtypeStruct((CHS, OWN * ROWS, LANES), BF),
        in_specs=[
            pl.BlockSpec(memory_space=pltpu.SMEM),
            pl.BlockSpec(memory_space=VMEM),
            pl.BlockSpec(memory_space=VMEM),
            pl.BlockSpec(memory_space=VMEM),
        ],
        out_specs=pl.BlockSpec(memory_space=VMEM),
        scratch_shapes=[
            pltpu.VMEM((BLOCKS * SUB * HALO_ROWS + MARGIN, LANES), F32),
            pltpu.VMEM((HALO_ROWS, KER * C, 2 * LANES), F32),
        ],
        compiler_params=pltpu.CompilerParams(vmem_limit_bytes=16 << 20),
        cost_estimate=pl.CostEstimate(flops=200 << 20, bytes_accessed=2 << 20, transcendentals=0),
        name="row_stage",
    )(block_slots, rows, coefs, mix)


LON_PARTS = 2


def longitude_kernel(rows_ref, table_ref, out_ref, whole, sems):
    rows = ROWS // LON_PARTS
    lines = rows * OWN
    departures = []
    for g in range(LON_PARTS):
        even = jnp.concatenate(
            [rows_ref[j, g * lines : (g + 1) * lines] for j in range(CHS)], axis=1
        )
        lane = lax.broadcasted_iota(jnp.int32, even.shape, 1)
        flipped = jnp.where(lane % PICKS < BLOCKS, even.astype(F32), -even.astype(F32)).astype(BF)
        both = jnp.concatenate([even, flipped], axis=0)
        field = jnp.dot(both, table_ref[...], preferred_element_type=F32)
        part = pl.ds(g * rows, rows)
        halves = jnp.concatenate([field[:lines], field[lines:]], axis=1)
        whole[part] = halves.astype(BF).reshape(rows, OWN, NLON)
        departures.append(pltpu.make_async_copy(whole.at[part], out_ref.at[part], sems.at[g]))
        departures[-1].start()
    for copy in departures:
        copy.wait()


def longitude_stage(rows, table):
    return pl.pallas_call(
        longitude_kernel,
        out_shape=jax.ShapeDtypeStruct((ROWS, OWN, NLON), BF),
        in_specs=[pl.BlockSpec(memory_space=VMEM)] * 2,
        out_specs=pl.BlockSpec(memory_space=pltpu.HBM),
        scratch_shapes=[
            pltpu.VMEM((ROWS, OWN, NLON), BF),
            pltpu.SemaphoreType.DMA((LON_PARTS,)),
        ],
        compiler_params=pltpu.CompilerParams(vmem_limit_bytes=40 << 20),
        cost_estimate=pl.CostEstimate(flops=480 << 20, bytes_accessed=4 << 20, transcendentals=0),
        name="longitude_stage",
    )(rows, table)


def per_device(spectrum, legendre, block_slots, kernel_values, near_rows, mix_weights):
    ch_index = lax.axis_index("ch")
    picked = pick(block_slots, legendre)
    picked, spectrum = lax.optimization_barrier((picked, spectrum))
    leg = lax.all_to_all(picked, "lat", 0, 0, tiled=True)
    blocks = spectrum.reshape(TURNS, PAIR, C, STEPS)
    turn, side = ch_index // PAIR, ch_index % PAIR
    pieces = []
    for d in range(TURNS):
        piece = lax.dynamic_index_in_dim(blocks, (turn + d) % TURNS, 0, keepdims=False)
        shift = [(j, (j + PAIR * d) % CHS) for j in range(CHS)]
        pieces.append(lax.ppermute(piece, "ch", shift) if d else piece)
    both = jnp.stack(pieces, axis=0)
    kept = lax.dynamic_index_in_dim(both, side, 1, keepdims=False)
    given = lax.dynamic_index_in_dim(both, 1 - side, 1, keepdims=False)
    taken = lax.ppermute(given, "ch", [(j, j ^ 1) for j in range(CHS)])
    by_order = order_stage(leg, spec_stage([kept, taken]))
    by_order, kernel_values, near_rows, mix_weights = lax.optimization_barrier(
        (by_order, kernel_values, near_rows, mix_weights)
    )
    by_row = lax.all_to_all(by_order, "lat", 0, 0, tiled=True)
    coefs, mix = coef_stage(kernel_values, near_rows, mix_weights)
    mixed = row_stage(block_slots, by_row, coefs, mix)
    own = lax.all_to_all(mixed, "ch", 0, 0, tiled=True)
    field = longitude_stage(own, jnp.asarray(longitude_table()))
    return jnp.transpose(field, (1, 0, 2))


def solution(mesh):
    return jax.shard_map(
        per_device,
        mesh=mesh,
        in_specs=(
            P("lat", "ch", None, None, None),
            P("lat", None, None),
            P(),
            P(None, "lat", None, None),
            P("lat", None),
            P(),
        ),
        out_specs=P("ch", "lat", None),
        check_vma=False,
    )
```

```python
import math

import jax
import jax.numpy as jnp
import ml_dtypes
import numpy as np
from jax import lax
from jax.experimental import pallas as pl
from jax.experimental.pallas import tpu as pltpu
from jax.sharding import PartitionSpec as P

NLAT = 640
NLON = 1440
LMAX = 512
C = 64
ORDER_BLOCK = 16
KER = 3
SLOTS = 6
REACH = 2
LON_REACH = 4
TAPS = 9
STEPS = 256
BLOCKS = 32
LATS = 32
CHS = 8
ROWS = NLAT // LATS
OWN = C // CHS
SUB = ORDER_BLOCK // CHS
HALO_ROWS = ROWS + 2 * REACH
SPREAD = 2 * REACH + 1
PICKS = LATS * SUB
LANES = 128
BF = jnp.bfloat16
F32 = jnp.float32
NT = (((1,), (1,)), ((), ()))
TN = (((0,), (0,)), ((), ()))
VMEM = pltpu.VMEM
GRANT = 62 << 20
MARGIN = 48
PAIR = 2
TURNS = CHS // PAIR


HALF_LON = NLON // 2
WAVE_ROWS = 16


def order_table():
    orders = (
        ORDER_BLOCK * np.arange(BLOCKS)[None, None, :]
        + SUB * np.arange(CHS)[:, None, None]
        + np.arange(SUB)[None, :, None]
    )
    return orders.reshape(CHS, SUB, 1, BLOCKS, 1)


def longitude_table():
    orders = order_table()
    phases = (orders * np.arange(HALF_LON)) % NLON
    angles = phases * (2.0 * math.pi / NLON)
    weight = np.where(orders == 0, 1.0, 2.0)
    table = np.concatenate([weight * np.cos(angles), -weight * np.sin(angles)], axis=2)
    table = np.swapaxes(table, 0, 1)
    return table.reshape(SUB, CHS * PICKS, HALF_LON).astype(ml_dtypes.bfloat16)


def wave_table():
    shifts = np.arange(TAPS)[:, None] - LON_REACH
    orders = order_table().reshape(CHS, 1, SUB, 1, BLOCKS)
    shifts = shifts.reshape(TAPS, 1, 1, 1)
    angles = ((orders * shifts) % NLON) * (2.0 * math.pi / NLON)
    waves = np.zeros((CHS, WAVE_ROWS, 2 * LANES), np.float32)
    cosine, sine = np.cos(angles), np.sin(angles)
    for n, parts in enumerate(([cosine, cosine], [-sine, sine])):
        both = np.concatenate(parts, axis=3).reshape(CHS, TAPS, LANES)
        waves[:, :TAPS, n * LANES : (n + 1) * LANES] = both
    return waves


PICK_GROUPS = (4, 4, 8, 4)
EDGE = 12
ORDER_LIMITS = (LMAX, LMAX - 2 * LANES)


def pick_kernel(slots_ref, leg_ref, out_ref, buf, wide, flat, sems):
    arrivals, departures, firsts = [], [], []
    for g, count in enumerate(PICK_GROUPS):
        first = sum(PICK_GROUPS[:g])
        firsts.append(first)
        pair = []
        for h in range(STEPS // LANES):
            part = (pl.ds(first, count), pl.ds(h * LANES, LANES), pl.ds(0, ORDER_LIMITS[h]))
            pair.append(pltpu.make_async_copy(leg_ref.at[part], buf.at[part], sems.at[h, g]))
            pair[-1].start()
        arrivals.append(pair)
        lines = pl.ds(first * SUB, count * SUB)
        departures.append(
            pltpu.make_async_copy(flat.at[:, lines, :], out_ref.at[:, lines, :], sems.at[2, g])
        )
    line = lax.broadcasted_iota(jnp.int32, (PICKS, LANES), 0)
    lane = lax.broadcasted_iota(jnp.int32, (PICKS, LANES), 1)
    blocks = jnp.zeros((PICKS, LANES), jnp.int32)
    for i in range(LATS):
        blocks = jnp.where(line % LATS == i, slots_ref[i], blocks)
    wanted = blocks * ORDER_BLOCK + line // LATS + SUB * lax.axis_index("ch")
    hot = jnp.concatenate(
        [
            jnp.where(lane + n * LANES == wanted, 1.0, 0.0).astype(BF)
            for n in range(LMAX // LANES)
        ],
        axis=1,
    )
    for g, count in enumerate(PICK_GROUPS):
        for copy in arrivals[g]:
            copy.wait()
        first, size = firsts[g], count * SUB
        base = first * SUB * LATS
        limit = ORDER_LIMITS[1]
        for r in range(count):
            lead = lax.dot_general(
                hot[:, :limit], buf[first + r, :, :limit], NT, preferred_element_type=F32
            )
            rest = lax.dot_general(
                hot[:, limit:], buf[first + r, :LANES, limit:], NT, preferred_element_type=F32
            )
            for h, picked in enumerate((lead[:, :LANES] + rest, lead[:, LANES:])):
                for t in range(SUB):
                    wide[h, pl.ds(base + r * SUB + t, LATS, stride=size), :] = picked[
                        t * LATS : (t + 1) * LATS
                    ]
        for h in range(STEPS // LANES):
            lanes = slice(h * LANES, (h + 1) * LANES)
            flat[:, first * SUB : first * SUB + size, lanes] = (
                wide[h, base : base + LATS * size].reshape(LATS, size, LANES).astype(BF)
            )
        departures[g].start()
    for copy in departures:
        copy.wait()


def pick(block_slots, legendre):
    return pl.pallas_call(
        pick_kernel,
        out_shape=jax.ShapeDtypeStruct((LATS, ROWS * SUB, STEPS), BF),
        in_specs=[pl.BlockSpec(memory_space=pltpu.SMEM), pl.BlockSpec(memory_space=pltpu.HBM)],
        out_specs=pl.BlockSpec(memory_space=pltpu.HBM),
        scratch_shapes=[
            pltpu.VMEM((ROWS, STEPS, LMAX), BF),
            pltpu.VMEM((STEPS // LANES, LATS * ROWS * SUB + MARGIN, LANES), F32),
            pltpu.VMEM((LATS, ROWS * SUB, STEPS), BF),
            pltpu.SemaphoreType.DMA((3, len(PICK_GROUPS))),
        ],
        compiler_params=pltpu.CompilerParams(vmem_limit_bytes=GRANT),
        cost_estimate=pl.CostEstimate(flops=2 * 64 * 512 * 5120, bytes_accessed=6 << 20, transcendentals=0),
        name="pick",
    )(block_slots, legendre)


def order_kernel(leg_ref, *refs):
    pieces_in, (out_ref, raw, specs, full) = refs[:PAIR], refs[PAIR:]
    half = NLAT // 2
    ch_index = lax.axis_index("ch")
    side = lax.rem(ch_index, PAIR)
    for d in range(TURNS):
        turn = lax.rem(lax.div(ch_index, PAIR) + (TURNS - d), TURNS)
        for q in range(PAIR):
            source = turn * PAIR + (side if q == 0 else 1 - side)
            for h in range(STEPS // LANES):
                lanes = slice(h * LANES, (h + 1) * LANES)
                start = pl.multiple_of(source * C, C)
                specs[h, pl.ds(start, C), :] = pieces_in[q][d, :, lanes].astype(F32)
    for h in range(STEPS // LANES):
        lanes = slice(h * LANES, (h + 1) * LANES)
        lines = leg_ref[:, :, lanes].astype(F32).reshape(LATS * ROWS * SUB, LANES)
        raw[h, : LATS * ROWS * SUB, :] = lines
    rows = lax.broadcasted_iota(jnp.int32, (LANES, LANES), 0)
    cols = lax.broadcasted_iota(jnp.int32, (LANES, LANES), 1)
    turn = jnp.where(rows + cols == LANES - 1, 1.0, 0.0).astype(BF)
    stride = 4
    full[:16, :] = jnp.zeros((16, LANES), F32)
    full[SUB * NLAT :, :] = jnp.zeros((2 * EDGE, LANES), F32)
    for t in range(SUB):
        table = jnp.concatenate(
            [raw[h, pl.ds(t, NLAT, stride=SUB), :] for h in range(STEPS // LANES)], axis=1
        ).astype(BF)
        count = NLAT // LANES
        turned = jnp.concatenate(
            [
                jnp.dot(
                    turn,
                    table[(count - 1 - n) * LANES : (count - n) * LANES],
                    preferred_element_type=F32,
                ).astype(BF)
                for n in range(count)
            ],
            axis=0,
        )
        coeffs = []
        for p in range(2):
            pieces = []
            for x in range(2):
                for j in range(CHS):
                    start = j * C + t * 4 * OWN + p * 2 + x
                    pieces.append(
                        jnp.concatenate(
                            [
                                specs[h, pl.ds(start, OWN, stride=stride), :]
                                for h in range(STEPS // LANES)
                            ],
                            axis=1,
                        )
                    )
            coeffs.append(jnp.concatenate(pieces, axis=0).astype(BF))

        def dot(a, b):
            return lax.dot_general(a, b, NT, preferred_element_type=F32)

        north = dot(table[:half], coeffs[0]) - dot(turned[:half], coeffs[1])
        south = dot(table[half:], coeffs[1]) + dot(turned[half:], coeffs[0])
        full[pl.ds(EDGE + t, half, stride=SUB), :] = north
        full[pl.ds(EDGE + t + SUB * half, half, stride=SUB), :] = south
    for i in range(LATS):
        start = EDGE - REACH * SUB + i * ROWS * SUB
        out_ref[i] = full[start : start + HALO_ROWS * SUB, :].astype(BF)


def order_stage(leg, pieces):
    return pl.pallas_call(
        order_kernel,
        out_shape=jax.ShapeDtypeStruct((LATS, HALO_ROWS * SUB, LANES), BF),
        in_specs=[pl.BlockSpec(memory_space=VMEM)] * (1 + PAIR),
        out_specs=pl.BlockSpec(memory_space=VMEM),
        scratch_shapes=[
            pltpu.VMEM((STEPS // LANES, LATS * SUB * ROWS + MARGIN, LANES), F32),
            pltpu.VMEM((STEPS // LANES, CHS * C + MARGIN, LANES), F32),
            pltpu.VMEM((SUB * NLAT + 2 * EDGE, LANES), F32),
        ],
        compiler_params=pltpu.CompilerParams(vmem_limit_bytes=24 << 20),
        cost_estimate=pl.CostEstimate(flops=700 << 20, bytes_accessed=2 << 20, transcendentals=0),
        name="order_stage",
    )(leg, *pieces)


def coef_kernel(values_ref, near_ref, mix_ref, waves_ref, coef_ref, mixed_ref, taps):
    first = lax.axis_index("lat") * ROWS
    step = near_ref[...] - lax.broadcasted_iota(jnp.int32, (SLOTS, ROWS), 1) - (first - REACH)
    taps[...] = jnp.zeros_like(taps)
    for d in range(SPREAD):
        hit = jnp.where(step == d, 1.0, 0.0)
        for b in range(KER):
            for s in range(TAPS):
                value = values_ref[b, s].astype(F32)
                taps[b * SPREAD + d, s : s + 1, :] = jnp.sum(hit * value, axis=0, keepdims=True)
    waves = waves_ref[lax.axis_index("ch")]
    for n in range(KER * SPREAD):
        coef_ref[n] = lax.dot_general(
            taps[n], waves, TN, precision=lax.Precision.HIGHEST, preferred_element_type=F32
        )
    turned = jnp.concatenate([mix_ref[b].astype(F32).T for b in range(KER)], axis=0)
    mixed_ref[...] = jnp.concatenate([turned, turned], axis=1).astype(BF)


def coef_stage(kernel_values, near_rows, mix_weights):
    return pl.pallas_call(
        coef_kernel,
        out_shape=(
            jax.ShapeDtypeStruct((KER * SPREAD, ROWS, 2 * LANES), F32),
            jax.ShapeDtypeStruct((KER * C, 2 * C), BF),
        ),
        in_specs=[pl.BlockSpec(memory_space=VMEM)] * 4,
        out_specs=[pl.BlockSpec(memory_space=VMEM)] * 2,
        scratch_shapes=[pltpu.VMEM((KER * SPREAD, WAVE_ROWS, ROWS), F32)],
        compiler_params=pltpu.CompilerParams(vmem_limit_bytes=16 << 20),
        cost_estimate=pl.CostEstimate(flops=16 << 20, bytes_accessed=1 << 20, transcendentals=0),
        name="coef_stage",
    )(
        jnp.transpose(kernel_values, (0, 3, 2, 1)),
        jnp.transpose(near_rows, (1, 0)),
        mix_weights,
        jnp.asarray(wave_table()),
    )


def row_kernel(slots_ref, rows_ref, coef_ref, mix_ref, out_ref, field, mixed):
    for i in range(LATS):
        block = slots_ref[i]
        start = pl.multiple_of(block * (SUB * HALO_ROWS), 8)
        field[pl.ds(start, SUB * HALO_ROWS), :] = rows_ref[i].astype(F32)
    low = lax.broadcasted_iota(jnp.int32, (PICKS, LANES), 1) < C
    weights = mix_ref[...]
    for r in range(HALO_ROWS):
        one = jnp.concatenate(
            [
                field[pl.ds(r * SUB + t, BLOCKS, stride=SUB * HALO_ROWS), :]
                for t in range(SUB)
            ],
            axis=0,
        )
        real = jnp.where(low, one, 0.0)
        imag = jnp.where(low, 0.0, one)
        turns = [real[:BLOCKS], imag[:BLOCKS], real[BLOCKS:], imag[BLOCKS:]]
        swaps = [imag[:BLOCKS], real[:BLOCKS], imag[BLOCKS:], real[BLOCKS:]]
        both = jnp.concatenate(turns + swaps, axis=0).astype(BF)
        mixed[r] = lax.dot_general(weights, both, NT, preferred_element_type=F32)
    for r in range(ROWS):
        total = None
        for b in range(KER):
            for d in range(SPREAD):
                n = b * SPREAD + d
                part = mixed[r + d, b * C : (b + 1) * C, :]
                term = coef_ref[n, r : r + 1, :LANES] * part[:, :LANES]
                term = term + coef_ref[n, r : r + 1, LANES:] * part[:, LANES:]
                total = term if total is None else total + term
        out_ref[:, r * OWN : (r + 1) * OWN, :] = total.astype(BF).reshape(CHS, OWN, LANES)


def row_stage(block_slots, rows, coefs, mix):
    return pl.pallas_call(
        row_kernel,
        out_shape=jax.ShapeDtypeStruct((CHS, OWN * ROWS, LANES), BF),
        in_specs=[
            pl.BlockSpec(memory_space=pltpu.SMEM),
            pl.BlockSpec(memory_space=VMEM),
            pl.BlockSpec(memory_space=VMEM),
            pl.BlockSpec(memory_space=VMEM),
        ],
        out_specs=pl.BlockSpec(memory_space=VMEM),
        scratch_shapes=[
            pltpu.VMEM((BLOCKS * SUB * HALO_ROWS + MARGIN, LANES), F32),
            pltpu.VMEM((HALO_ROWS, KER * C, 2 * LANES), F32),
        ],
        compiler_params=pltpu.CompilerParams(vmem_limit_bytes=16 << 20),
        cost_estimate=pl.CostEstimate(flops=200 << 20, bytes_accessed=2 << 20, transcendentals=0),
        name="row_stage",
    )(block_slots, rows, coefs, mix)


LON_PARTS = 2


def longitude_kernel(rows_ref, table_ref, out_ref, whole, sems):
    rows = ROWS // LON_PARTS
    lines = rows * OWN
    departures = []
    for g in range(LON_PARTS):
        parts = []
        for t in range(SUB):
            lanes = slice(t * PICKS, (t + 1) * PICKS)
            own = [rows_ref[j, g * lines : (g + 1) * lines, lanes] for j in range(CHS)]
            lhs = jnp.concatenate(own, axis=1)
            parts.append(jnp.dot(lhs, table_ref[t], preferred_element_type=F32))
        part = pl.ds(g * rows, rows)
        halves = jnp.concatenate([parts[0] + parts[1], parts[0] - parts[1]], axis=1)
        whole[part] = halves.astype(BF).reshape(rows, OWN, NLON)
        departures.append(pltpu.make_async_copy(whole.at[part], out_ref.at[part], sems.at[g]))
        departures[-1].start()
    for copy in departures:
        copy.wait()


def longitude_stage(rows, table):
    return pl.pallas_call(
        longitude_kernel,
        out_shape=jax.ShapeDtypeStruct((ROWS, OWN, NLON), BF),
        in_specs=[pl.BlockSpec(memory_space=VMEM)] * 2,
        out_specs=pl.BlockSpec(memory_space=pltpu.HBM),
        scratch_shapes=[
            pltpu.VMEM((ROWS, OWN, NLON), BF),
            pltpu.SemaphoreType.DMA((LON_PARTS,)),
        ],
        compiler_params=pltpu.CompilerParams(vmem_limit_bytes=40 << 20),
        cost_estimate=pl.CostEstimate(flops=480 << 20, bytes_accessed=4 << 20, transcendentals=0),
        name="longitude_stage",
    )(rows, table)


def per_device(spectrum, legendre, block_slots, kernel_values, near_rows, mix_weights):
    ch_index = lax.axis_index("ch")
    picked = pick(block_slots, legendre)
    picked, spectrum = lax.optimization_barrier((picked, spectrum))
    leg = lax.all_to_all(picked, "lat", 0, 0, tiled=True)
    blocks = spectrum.reshape(TURNS, PAIR, C, STEPS)
    turn, side = ch_index // PAIR, ch_index % PAIR
    pieces = []
    for d in range(TURNS):
        piece = lax.dynamic_index_in_dim(blocks, (turn + d) % TURNS, 0, keepdims=False)
        shift = [(j, (j + PAIR * d) % CHS) for j in range(CHS)]
        pieces.append(lax.ppermute(piece, "ch", shift) if d else piece)
    both = jnp.stack(pieces, axis=0)
    kept = lax.dynamic_index_in_dim(both, side, 1, keepdims=False)
    given = lax.dynamic_index_in_dim(both, 1 - side, 1, keepdims=False)
    taken = lax.ppermute(given, "ch", [(j, j ^ 1) for j in range(CHS)])
    pieces = [kept, taken]
    by_order = order_stage(leg, pieces)
    by_order, kernel_values, near_rows, mix_weights = lax.optimization_barrier(
        (by_order, kernel_values, near_rows, mix_weights)
    )
    by_row = lax.all_to_all(by_order, "lat", 0, 0, tiled=True)
    coefs, mix = coef_stage(kernel_values, near_rows, mix_weights)
    mixed = row_stage(block_slots, by_row, coefs, mix)
    own = lax.all_to_all(mixed, "ch", 0, 0, tiled=True)
    field = longitude_stage(own, jnp.asarray(longitude_table()))
    return jnp.transpose(field, (1, 0, 2))


def solution(mesh):
    return jax.shard_map(
        per_device,
        mesh=mesh,
        in_specs=(
            P("lat", "ch", None, None, None),
            P("lat", None, None),
            P(),
            P(None, "lat", None, None),
            P("lat", None),
            P(),
        ),
        out_specs=P("ch", "lat", None),
        check_vma=False,
    )
```

```python
import math

import jax
import jax.numpy as jnp
import ml_dtypes
import numpy as np
from jax import lax
from jax.experimental import pallas as pl
from jax.experimental.pallas import tpu as pltpu
from jax.sharding import PartitionSpec as P

NLAT = 640
NLON = 1440
LMAX = 512
C = 64
ORDER_BLOCK = 16
KER = 3
SLOTS = 6
REACH = 2
LON_REACH = 4
TAPS = 9
STEPS = 256
BLOCKS = 32
LATS = 32
CHS = 8
ROWS = NLAT // LATS
OWN = C // CHS
SUB = ORDER_BLOCK // CHS
HALO_ROWS = ROWS + 2 * REACH
SPREAD = 2 * REACH + 1
PICKS = LATS * SUB
LANES = 128
BF = jnp.bfloat16
F32 = jnp.float32
NT = (((1,), (1,)), ((), ()))
TN = (((0,), (0,)), ((), ()))
VMEM = pltpu.VMEM
GRANT = 62 << 20
MARGIN = 48
PAIR = 2
TURNS = CHS // PAIR


HALF_LON = NLON // 2
WAVE_ROWS = 16


def order_table():
    orders = (
        ORDER_BLOCK * np.arange(BLOCKS)[None, None, :]
        + SUB * np.arange(CHS)[:, None, None]
        + np.arange(SUB)[None, :, None]
    )
    return orders.reshape(CHS, 1, PICKS, 1)


def longitude_table():
    orders = order_table()
    phases = (orders * np.arange(HALF_LON)) % NLON
    angles = phases * (2.0 * math.pi / NLON)
    weight = np.where(orders == 0, 1.0, 2.0)
    table = np.concatenate([weight * np.cos(angles), -weight * np.sin(angles)], axis=1)
    return table.reshape(CHS * LANES, HALF_LON).astype(ml_dtypes.bfloat16)


def wave_table():
    shifts = np.arange(TAPS)[:, None] - LON_REACH
    orders = order_table().reshape(CHS, 1, PICKS)
    angles = ((orders * shifts) % NLON) * (2.0 * math.pi / NLON)
    waves = np.zeros((CHS, WAVE_ROWS, 2 * LANES), np.float32)
    cosine, sine = np.cos(angles), np.sin(angles)
    waves[:, :TAPS] = np.concatenate([cosine, cosine, -sine, sine], axis=2)
    return waves


PICK_GROUPS = (8, 8, 4)
EDGE = 12
ORDER_LIMITS = (LMAX, LMAX - 2 * LANES)


def pick_kernel(slots_ref, leg_ref, out_ref, buf, wide, flat, sems):
    arrivals, departures, firsts = [], [], []
    for g, count in enumerate(PICK_GROUPS):
        first = sum(PICK_GROUPS[:g])
        firsts.append(first)
        pair = []
        for h in range(STEPS // LANES):
            part = (pl.ds(first, count), pl.ds(h * LANES, LANES), pl.ds(0, ORDER_LIMITS[h]))
            pair.append(pltpu.make_async_copy(leg_ref.at[part], buf.at[part], sems.at[h, g]))
            pair[-1].start()
        arrivals.append(pair)
        lines = pl.ds(first * SUB, count * SUB)
        departures.append(
            pltpu.make_async_copy(flat.at[:, lines, :], out_ref.at[:, lines, :], sems.at[2, g])
        )
    line = lax.broadcasted_iota(jnp.int32, (PICKS, LANES), 0)
    lane = lax.broadcasted_iota(jnp.int32, (PICKS, LANES), 1)
    blocks = jnp.zeros((PICKS, LANES), jnp.int32)
    for i in range(LATS):
        blocks = jnp.where(line % LATS == i, slots_ref[i], blocks)
    wanted = blocks * ORDER_BLOCK + line // LATS + SUB * lax.axis_index("ch")
    hot = jnp.concatenate(
        [
            jnp.where(lane + n * LANES == wanted, 1.0, 0.0).astype(BF)
            for n in range(LMAX // LANES)
        ],
        axis=1,
    )
    for g, count in enumerate(PICK_GROUPS):
        for copy in arrivals[g]:
            copy.wait()
        first, size = firsts[g], count * SUB
        base = first * SUB * LATS
        limit = ORDER_LIMITS[1]
        for r in range(count):
            lead = lax.dot_general(
                hot[:, :limit], buf[first + r, :, :limit], NT, preferred_element_type=F32
            )
            rest = lax.dot_general(
                hot[:, limit:], buf[first + r, :LANES, limit:], NT, preferred_element_type=F32
            )
            for h, picked in enumerate((lead[:, :LANES] + rest, lead[:, LANES:])):
                for t in range(SUB):
                    wide[h, pl.ds(base + r * SUB + t, LATS, stride=size), :] = picked[
                        t * LATS : (t + 1) * LATS
                    ]
        for h in range(STEPS // LANES):
            lanes = slice(h * LANES, (h + 1) * LANES)
            flat[:, first * SUB : first * SUB + size, lanes] = (
                wide[h, base : base + LATS * size].reshape(LATS, size, LANES).astype(BF)
            )
        departures[g].start()
    for copy in departures:
        copy.wait()


def pick(block_slots, legendre):
    return pl.pallas_call(
        pick_kernel,
        out_shape=jax.ShapeDtypeStruct((LATS, ROWS * SUB, STEPS), BF),
        in_specs=[pl.BlockSpec(memory_space=pltpu.SMEM), pl.BlockSpec(memory_space=pltpu.HBM)],
        out_specs=pl.BlockSpec(memory_space=pltpu.HBM),
        scratch_shapes=[
            pltpu.VMEM((ROWS, STEPS, LMAX), BF),
            pltpu.VMEM((STEPS // LANES, LATS * ROWS * SUB + MARGIN, LANES), F32),
            pltpu.VMEM((LATS, ROWS * SUB, STEPS), BF),
            pltpu.SemaphoreType.DMA((3, len(PICK_GROUPS))),
        ],
        compiler_params=pltpu.CompilerParams(vmem_limit_bytes=GRANT),
        cost_estimate=pl.CostEstimate(flops=2 * 64 * 512 * 5120, bytes_accessed=6 << 20, transcendentals=0),
        name="pick",
    )(block_slots, legendre)


def order_kernel(leg_ref, *refs):
    pieces_in, (out_ref, raw, specs, full) = refs[:PAIR], refs[PAIR:]
    half = NLAT // 2
    ch_index = lax.axis_index("ch")
    side = lax.rem(ch_index, PAIR)
    for d in range(TURNS):
        turn = lax.rem(lax.div(ch_index, PAIR) + (TURNS - d), TURNS)
        for q in range(PAIR):
            source = turn * PAIR + (side if q == 0 else 1 - side)
            for h in range(STEPS // LANES):
                lanes = slice(h * LANES, (h + 1) * LANES)
                start = pl.multiple_of(source * C, C)
                specs[h, pl.ds(start, C), :] = pieces_in[q][d, :, lanes].astype(F32)
    for h in range(STEPS // LANES):
        lanes = slice(h * LANES, (h + 1) * LANES)
        lines = leg_ref[:, :, lanes].astype(F32).reshape(LATS * ROWS * SUB, LANES)
        raw[h, : LATS * ROWS * SUB, :] = lines
    rows = lax.broadcasted_iota(jnp.int32, (LANES, LANES), 0)
    cols = lax.broadcasted_iota(jnp.int32, (LANES, LANES), 1)
    turn = jnp.where(rows + cols == LANES - 1, 1.0, 0.0).astype(BF)
    stride = 4
    full[:16, :] = jnp.zeros((16, LANES), F32)
    full[SUB * NLAT :, :] = jnp.zeros((2 * EDGE, LANES), F32)
    for t in range(SUB):
        table = jnp.concatenate(
            [raw[h, pl.ds(t, NLAT, stride=SUB), :] for h in range(STEPS // LANES)], axis=1
        ).astype(BF)
        count = NLAT // LANES
        turned = jnp.concatenate(
            [
                jnp.dot(
                    turn,
                    table[(count - 1 - n) * LANES : (count - n) * LANES],
                    preferred_element_type=F32,
                ).astype(BF)
                for n in range(count)
            ],
            axis=0,
        )
        coeffs = []
        for p in range(2):
            pieces = []
            for x in range(2):
                for j in range(CHS):
                    start = j * C + t * 4 * OWN + p * 2 + x
                    pieces.append(
                        jnp.concatenate(
                            [
                                specs[h, pl.ds(start, OWN, stride=stride), :]
                                for h in range(STEPS // LANES)
                            ],
                            axis=1,
                        )
                    )
            coeffs.append(jnp.concatenate(pieces, axis=0).astype(BF))

        def dot(a, b):
            return lax.dot_general(a, b, NT, preferred_element_type=F32)

        north = dot(table[:half], coeffs[0]) - dot(turned[:half], coeffs[1])
        south = dot(table[half:], coeffs[1]) + dot(turned[half:], coeffs[0])
        full[pl.ds(EDGE + t, half, stride=SUB), :] = north
        full[pl.ds(EDGE + t + SUB * half, half, stride=SUB), :] = south
    for i in range(LATS):
        start = EDGE - REACH * SUB + i * ROWS * SUB
        out_ref[i] = full[start : start + HALO_ROWS * SUB, :].astype(BF)


def order_stage(leg, pieces):
    return pl.pallas_call(
        order_kernel,
        out_shape=jax.ShapeDtypeStruct((LATS, HALO_ROWS * SUB, LANES), BF),
        in_specs=[pl.BlockSpec(memory_space=VMEM)] * (1 + PAIR),
        out_specs=pl.BlockSpec(memory_space=VMEM),
        scratch_shapes=[
            pltpu.VMEM((STEPS // LANES, LATS * SUB * ROWS + MARGIN, LANES), F32),
            pltpu.VMEM((STEPS // LANES, CHS * C + MARGIN, LANES), F32),
            pltpu.VMEM((SUB * NLAT + 2 * EDGE, LANES), F32),
        ],
        compiler_params=pltpu.CompilerParams(vmem_limit_bytes=24 << 20),
        cost_estimate=pl.CostEstimate(flops=700 << 20, bytes_accessed=2 << 20, transcendentals=0),
        name="order_stage",
    )(leg, *pieces)


def coef_kernel(values_ref, near_ref, mix_ref, waves_ref, coef_ref, mixed_ref, taps):
    first = lax.axis_index("lat") * ROWS
    step = near_ref[...] - lax.broadcasted_iota(jnp.int32, (SLOTS, ROWS), 1) - (first - REACH)
    taps[...] = jnp.zeros_like(taps)
    for d in range(SPREAD):
        hit = jnp.where(step == d, 1.0, 0.0)
        for b in range(KER):
            for s in range(TAPS):
                value = values_ref[b, s].astype(F32)
                taps[b * SPREAD + d, s : s + 1, :] = jnp.sum(hit * value, axis=0, keepdims=True)
    waves = waves_ref[lax.axis_index("ch")]
    for n in range(KER * SPREAD):
        coef_ref[n] = lax.dot_general(
            taps[n], waves, TN, precision=lax.Precision.HIGHEST, preferred_element_type=F32
        )
    turned = jnp.concatenate([mix_ref[b].astype(F32).T for b in range(KER)], axis=0)
    mixed_ref[...] = jnp.concatenate([turned, turned], axis=1).astype(BF)


def coef_stage(kernel_values, near_rows, mix_weights):
    return pl.pallas_call(
        coef_kernel,
        out_shape=(
            jax.ShapeDtypeStruct((KER * SPREAD, ROWS, 2 * LANES), F32),
            jax.ShapeDtypeStruct((KER * C, 2 * C), BF),
        ),
        in_specs=[pl.BlockSpec(memory_space=VMEM)] * 4,
        out_specs=[pl.BlockSpec(memory_space=VMEM)] * 2,
        scratch_shapes=[pltpu.VMEM((KER * SPREAD, WAVE_ROWS, ROWS), F32)],
        compiler_params=pltpu.CompilerParams(vmem_limit_bytes=16 << 20),
        cost_estimate=pl.CostEstimate(flops=16 << 20, bytes_accessed=1 << 20, transcendentals=0),
        name="coef_stage",
    )(
        jnp.transpose(kernel_values, (0, 3, 2, 1)),
        jnp.transpose(near_rows, (1, 0)),
        mix_weights,
        jnp.asarray(wave_table()),
    )


def row_kernel(slots_ref, rows_ref, coef_ref, mix_ref, out_ref, field, mixed):
    for i in range(LATS):
        block = slots_ref[i]
        start = pl.multiple_of(block * (SUB * HALO_ROWS), 8)
        field[pl.ds(start, SUB * HALO_ROWS), :] = rows_ref[i].astype(F32)
    low = lax.broadcasted_iota(jnp.int32, (PICKS, LANES), 1) < C
    weights = mix_ref[...]
    for r in range(HALO_ROWS):
        one = jnp.concatenate(
            [
                field[pl.ds(r * SUB + t, BLOCKS, stride=SUB * HALO_ROWS), :]
                for t in range(SUB)
            ],
            axis=0,
        )
        real = jnp.where(low, one, 0.0)
        imag = jnp.where(low, 0.0, one)
        both = jnp.concatenate([real, imag, imag, real], axis=0).astype(BF)
        mixed[r] = lax.dot_general(weights, both, NT, preferred_element_type=F32)
    for r in range(ROWS):
        total = None
        for b in range(KER):
            for d in range(SPREAD):
                n = b * SPREAD + d
                part = mixed[r + d, b * C : (b + 1) * C, :]
                term = coef_ref[n, r : r + 1, :LANES] * part[:, :LANES]
                term = term + coef_ref[n, r : r + 1, LANES:] * part[:, LANES:]
                total = term if total is None else total + term
        out_ref[:, r * OWN : (r + 1) * OWN, :] = total.astype(BF).reshape(CHS, OWN, LANES)


def row_stage(block_slots, rows, coefs, mix):
    return pl.pallas_call(
        row_kernel,
        out_shape=jax.ShapeDtypeStruct((CHS, OWN * ROWS, LANES), BF),
        in_specs=[
            pl.BlockSpec(memory_space=pltpu.SMEM),
            pl.BlockSpec(memory_space=VMEM),
            pl.BlockSpec(memory_space=VMEM),
            pl.BlockSpec(memory_space=VMEM),
        ],
        out_specs=pl.BlockSpec(memory_space=VMEM),
        scratch_shapes=[
            pltpu.VMEM((BLOCKS * SUB * HALO_ROWS + MARGIN, LANES), F32),
            pltpu.VMEM((HALO_ROWS, KER * C, 2 * LANES), F32),
        ],
        compiler_params=pltpu.CompilerParams(vmem_limit_bytes=16 << 20),
        cost_estimate=pl.CostEstimate(flops=200 << 20, bytes_accessed=2 << 20, transcendentals=0),
        name="row_stage",
    )(block_slots, rows, coefs, mix)


LON_PARTS = 2


def longitude_kernel(rows_ref, table_ref, out_ref, whole, sems):
    rows = ROWS // LON_PARTS
    lines = rows * OWN
    departures = []
    for g in range(LON_PARTS):
        even = jnp.concatenate(
            [rows_ref[j, g * lines : (g + 1) * lines] for j in range(CHS)], axis=1
        )
        lane = lax.broadcasted_iota(jnp.int32, even.shape, 1)
        flipped = jnp.where(lane % PICKS < BLOCKS, even.astype(F32), -even.astype(F32)).astype(BF)
        both = jnp.concatenate([even, flipped], axis=0)
        field = jnp.dot(both, table_ref[...], preferred_element_type=F32)
        part = pl.ds(g * rows, rows)
        halves = jnp.concatenate([field[:lines], field[lines:]], axis=1)
        whole[part] = halves.astype(BF).reshape(rows, OWN, NLON)
        departures.append(pltpu.make_async_copy(whole.at[part], out_ref.at[part], sems.at[g]))
        departures[-1].start()
    for copy in departures:
        copy.wait()


def longitude_stage(rows, table):
    return pl.pallas_call(
        longitude_kernel,
        out_shape=jax.ShapeDtypeStruct((ROWS, OWN, NLON), BF),
        in_specs=[pl.BlockSpec(memory_space=VMEM)] * 2,
        out_specs=pl.BlockSpec(memory_space=pltpu.HBM),
        scratch_shapes=[
            pltpu.VMEM((ROWS, OWN, NLON), BF),
            pltpu.SemaphoreType.DMA((LON_PARTS,)),
        ],
        compiler_params=pltpu.CompilerParams(vmem_limit_bytes=40 << 20),
        cost_estimate=pl.CostEstimate(flops=480 << 20, bytes_accessed=4 << 20, transcendentals=0),
        name="longitude_stage",
    )(rows, table)


def per_device(spectrum, legendre, block_slots, kernel_values, near_rows, mix_weights):
    ch_index = lax.axis_index("ch")
    picked = pick(block_slots, legendre)
    picked, spectrum = lax.optimization_barrier((picked, spectrum))
    leg = lax.all_to_all(picked, "lat", 0, 0, tiled=True)
    blocks = spectrum.reshape(TURNS, PAIR, C, STEPS)
    turn, side = ch_index // PAIR, ch_index % PAIR
    pieces = []
    for d in range(TURNS):
        piece = lax.dynamic_index_in_dim(blocks, (turn + d) % TURNS, 0, keepdims=False)
        shift = [(j, (j + PAIR * d) % CHS) for j in range(CHS)]
        pieces.append(lax.ppermute(piece, "ch", shift) if d else piece)
    both = jnp.stack(pieces, axis=0)
    kept = lax.dynamic_index_in_dim(both, side, 1, keepdims=False)
    given = lax.dynamic_index_in_dim(both, 1 - side, 1, keepdims=False)
    taken = lax.ppermute(given, "ch", [(j, j ^ 1) for j in range(CHS)])
    pieces = [kept, taken]
    by_order = order_stage(leg, pieces)
    by_order, kernel_values, near_rows, mix_weights = lax.optimization_barrier(
        (by_order, kernel_values, near_rows, mix_weights)
    )
    by_row = lax.all_to_all(by_order, "lat", 0, 0, tiled=True)
    coefs, mix = coef_stage(kernel_values, near_rows, mix_weights)
    mixed = row_stage(block_slots, by_row, coefs, mix)
    own = lax.all_to_all(mixed, "ch", 0, 0, tiled=True)
    field = longitude_stage(own, jnp.asarray(longitude_table()))
    return jnp.transpose(field, (1, 0, 2))


def solution(mesh):
    return jax.shard_map(
        per_device,
        mesh=mesh,
        in_specs=(
            P("lat", "ch", None, None, None),
            P("lat", None, None),
            P(),
            P(None, "lat", None, None),
            P("lat", None),
            P(),
        ),
        out_specs=P("ch", "lat", None),
        check_vma=False,
    )
```
